32 devices in a mesh: gx: 4 (over z), gy: 8 (over y, x, core).
Axes of the slice: x: 2, y: 2, z: 4, core: 2. Of those that a mesh axis runs over, the one named last changes fastest.
Arguments:
- initial_field: float32 [8, 32, 2048], P(None, 'gx', 'gy'), may hold values from -6 to 6
- target_field: float32 [8, 32, 2048], P(None, 'gx', 'gy'), may hold values from -8 to 8
- land_mask: int32 [32, 2048], P('gx', 'gy'), may hold values 0 or 1
- conv_one: float32 [64, 73], replicated, may hold values from -0.75 to 0.75
- conv_two: float32 [64, 577], replicated, may hold values from -0.25 to 0.25
- head_weights: float32 [32, 65], replicated, may hold values from -0.75 to 0.75
- dir_one: float32 [64, 73], replicated, may hold values from -6 to 6
- dir_two: float32 [64, 577], replicated, may hold values from -6 to 6
- dir_three: float32 [32, 65], replicated, may hold values from -6 to 6
- group_ids: int32 [160], replicated, may hold values from 0 to 5, as said below
Outputs:
- final_field: float32 [8, 32, 2048], P(None, 'gx', 'gy')
- update_one: float32 [64, 73], replicated
- update_two: float32 [64, 577], replicated
- update_three: float32 [32, 65], replicated
The draws below stay inside these ranges and needn't reach their ends.
Inputs may be any that keep to these rules, and one draw needn't show every extreme that they name: `group_ids`: each of the 6 group numbers names 26 or 27 rows.
All inputs are finite; a program needn't handle non-finite values. No bound on the sum of `land_mask` on one device may be relied on, other than what follows from the above.
Results may differ from the reference program's by a relative error of at most 0.0024.
The reference program's roundings to bfloat16 on the way count: a program that leaves them out, or rounds other values in their place, can miss the bound.
Values may be sent and summed in bfloat16 or wider, within the bound.
A program may use at most 64 MiB of HBM per device.

```python
import math
import jax
import jax.numpy as jnp
from jax import lax

LEV = 8
C = 64
K = 32
STEPS = 2
GROUPS = 6
NX = 32
NY = 2048
ROWS = 160
PARAMS = 43680


def draw_target_field(key, part):
    sample = jax.random.normal(key, (LEV, NX, NY), jnp.float32)
    position = jnp.arange(NX, dtype=jnp.float32)[None, :, None] / NX
    values = sample * 3.0 ** position
    return jnp.clip(values, -8.0, 8.0)


def draw_group_ids(key, part):
    return (jax.random.permutation(key, ROWS) % GROUPS).astype(jnp.int32)


def touch_ends(result, rng, low, largest):
    longest = result.shape.index(max(result.shape))
    spots = []
    for shift in (0, 1):
        where = [jax.random.randint(jax.random.fold_in(rng, axis), (), 0, length) for axis, length in enumerate(result.shape)]
        where[longest] = (where[longest] + shift) % result.shape[longest]
        spots.append(tuple(where))
    return result.at[spots[0]].set(low).at[spots[1]].set(largest)


def steps_of(key, shape, cuts, least, largest):
    gain, own = 1.0, jax.random.fold_in(key, 6)
    for dim, shards_of in cuts:
        steps = jnp.exp(jax.random.uniform(jax.random.fold_in(own, dim), (shards_of,), jnp.float32, least / len(cuts), largest / len(cuts)))
        gain = gain * jnp.repeat(steps, shape[dim] // shards_of).reshape([-1 if axis == dim else 1 for axis in range(len(shape))])
    return gain


def gaussian(key, extent, scale, limit, split=(), kind=jnp.bfloat16):
    entries = scale * jax.random.normal(key, extent, jnp.float32)
    if split:
        entries = entries * steps_of(key, extent, split, -0.22, 0.18)
    return jnp.clip(entries, -limit, limit).astype(kind)


def setup_inputs(seed: int = 0) -> dict:
    arg_keys = jax.random.split(jax.random.key(seed), 11)
    return {
        "initial_field": gaussian(arg_keys[0], (LEV, NX, NY), 1.0, 6.0, ((1, 4), (2, 8)), jnp.float32),
        "target_field": draw_target_field(jax.random.fold_in(arg_keys[10], 71), 0),
        "land_mask": touch_ends((jax.random.randint(arg_keys[2], (NX, NY), 0, 4) < 3).astype(jnp.int32), jax.random.fold_in(arg_keys[2], 1), 0, 1),
        "conv_one": gaussian(arg_keys[3], (C, 9 * LEV + 1), (9 * LEV) ** -0.5, 0.75, (), jnp.float32),
        "conv_two": gaussian(arg_keys[4], (C, 9 * C + 1), (9 * C) ** -0.5, 0.25, (), jnp.float32),
        "head_weights": gaussian(arg_keys[5], (K, C + 1), C ** -0.5, 0.75, (), jnp.float32),
        "dir_one": gaussian(arg_keys[6], (C, 9 * LEV + 1), 1.0, 6.0, (), jnp.float32),
        "dir_two": gaussian(arg_keys[7], (C, 9 * C + 1), 1.0, 6.0, (), jnp.float32),
        "dir_three": gaussian(arg_keys[8], (K, C + 1), 1.0, 6.0, (), jnp.float32),
        "group_ids": draw_group_ids(jax.random.fold_in(arg_keys[10], 71), 0),
    }


OFFSETS = ((0, 0), (0, 1), (0, 2), (1, 0), (1, 1), (1, 2), (2, 0), (2, 1), (2, 2))
CONTRACT_ROWS = (((1,), (1,)), ((), ()))
CONTRACT_COLS = (((0,), (0,)), ((), ()))

def silu_parts(activation):
    logistic = jax.nn.sigmoid(activation)
    return (activation * logistic, logistic * (1.0 + activation * (1.0 - logistic)))

def convolve(padded, kernel, bias_column):
    inputs = padded.shape[0]
    height = padded.shape[1] - 2
    breadth = padded.shape[2] - 2
    summed = jnp.zeros((kernel.shape[0], height * breadth), jnp.float32)
    for offset_index, offset_pair in enumerate(OFFSETS):
        row_start, col_start = offset_pair
        window = padded[:, row_start:row_start + height, col_start:col_start + breadth].reshape(inputs, height * breadth)
        weight_block = kernel[:, offset_index * inputs:(offset_index + 1) * inputs]
        summed = summed + jnp.dot(weight_block, window, preferred_element_type=jnp.float32)
    return summed.reshape(-1, height, breadth) + bias_column[:, None, None]

def convolve_back(padded, kernel, errors, precision):
    inputs = padded.shape[0]
    height = padded.shape[1] - 2
    breadth = padded.shape[2] - 2
    flat_error = errors.reshape(errors.shape[0], height * breadth)
    pieces = []
    input_grad = jnp.zeros(padded.shape, jnp.float32)
    for offset_index, offset_pair in enumerate(OFFSETS):
        row_start, col_start = offset_pair
        window = padded[:, row_start:row_start + height, col_start:col_start + breadth].reshape(inputs, height * breadth)
        pieces.append(lax.dot_general(flat_error, window, CONTRACT_ROWS, precision=precision, preferred_element_type=jnp.float32))
        weight_block = kernel[:, offset_index * inputs:(offset_index + 1) * inputs]
        carried = lax.dot_general(weight_block, flat_error, CONTRACT_COLS, precision=precision, preferred_element_type=jnp.float32)
        input_grad = input_grad.at[:, row_start:row_start + height, col_start:col_start + breadth].add(carried.reshape(inputs, height, breadth))
    return (jnp.concatenate(pieces, axis=1), input_grad)

def neighbours(padded):
    return (padded[:, 2:, 1:-1], padded[:, :-2, 1:-1], padded[:, 1:-1, 2:], padded[:, 1:-1, :-2])

def advance(padded, coeffs, wet_cells):
    center = padded[:, 1:-1, 1:-1]
    change = jnp.zeros(center.shape, jnp.float32)
    for direction, beside in enumerate(neighbours(padded)):
        change = change + coeffs[direction] * (beside - center)
    return center + wet_cells * change

def advance_back(padded, coeffs, wet_cells, adjoint):
    center = padded[:, 1:-1, 1:-1]
    weighted = wet_cells * adjoint
    grad_coeffs = []
    remains = adjoint
    for direction, beside in enumerate(neighbours(padded)):
        grad_coeffs.append(weighted * (beside - center))
        remains = remains - weighted * coeffs[direction]
    carried = weighted * coeffs
    grad_pad = jnp.zeros(padded.shape, jnp.float32)
    grad_pad = grad_pad.at[:, 2:, 1:-1].add(carried[0])
    grad_pad = grad_pad.at[:, :-2, 1:-1].add(carried[1])
    grad_pad = grad_pad.at[:, 1:-1, 2:].add(carried[2])
    grad_pad = grad_pad.at[:, 1:-1, :-2].add(carried[3])
    grad_pad = grad_pad.at[:, 1:-1, 1:-1].add(remains)
    return (jnp.stack(grad_coeffs), grad_pad)

def split_kernels(conv_one, conv_two, head_weights):
    return [(weights[:, :-1].astype(jnp.bfloat16), weights[:, -1]) for weights in (conv_one, conv_two, head_weights)]

def tail_forward(hidden_pad, kernels):
    second_pre = convolve(hidden_pad, kernels[1][0], kernels[1][1])
    second_out = silu_parts(second_pre)[0].astype(jnp.bfloat16)
    channels = second_out.shape[0]
    height = second_out.shape[1]
    breadth = second_out.shape[2]
    head_pre = jnp.dot(kernels[2][0], second_out.reshape(channels, height * breadth), preferred_element_type=jnp.float32) + kernels[2][1][:, None]
    logistic = jax.nn.sigmoid(head_pre)
    coeffs = (0.25 * logistic).reshape(4, -1, height, breadth)
    return (second_pre, second_out, logistic, coeffs)

def tail_back(hidden_pad, kernels, stored_tail, grad_coeffs):
    second_pre, second_out, logistic, coeffs = stored_tail
    head_error = grad_coeffs.reshape(logistic.shape) * (0.25 * logistic * (1.0 - logistic))
    head_round = head_error.astype(jnp.bfloat16)
    flat_out = second_out.reshape(second_out.shape[0], -1)
    head_grad = jnp.concatenate([lax.dot_general(head_round, flat_out, CONTRACT_ROWS, preferred_element_type=jnp.float32), lax.optimization_barrier(jnp.sum(head_error, axis=1))[:, None]], axis=1)
    hidden_back = lax.dot_general(kernels[2][0], head_round, CONTRACT_COLS, preferred_element_type=jnp.float32)
    second_error = hidden_back.reshape(second_pre.shape) * silu_parts(second_pre)[1]
    weight_grad, hidden_grad = convolve_back(hidden_pad, kernels[1][0], second_error.astype(jnp.bfloat16), None)
    second_grad = jnp.concatenate([weight_grad, lax.optimization_barrier(jnp.sum(second_error, axis=(1, 2)))[:, None]], axis=1)
    return (head_grad, second_grad, hidden_grad)

def first_back(tracer_round, kernel, first_error):
    first_round = first_error.astype(jnp.bfloat16)
    weight_grad, tracer_grad = convolve_back(tracer_round, kernel, first_round, None)
    return (jnp.concatenate([weight_grad, lax.optimization_barrier(jnp.sum(first_error, axis=(1, 2)))[:, None]], axis=1), tracer_grad)

def finish(gradients, directions, group_ids):
    norm_total = jnp.zeros((), jnp.float32)
    for member in gradients:
        norm_total = norm_total + jnp.sum(member * member)
    factor = 1.0 / jnp.maximum(jnp.sqrt(norm_total), 1.0)
    clipped = [member * factor for member in gradients]
    clip_rows = jnp.concatenate([lax.optimization_barrier(jnp.sum(member * member, axis=1)) for member in clipped])
    dir_rows = jnp.concatenate([lax.optimization_barrier(jnp.sum(member * member, axis=1)) for member in directions])
    choose = (group_ids[:, None] == jnp.arange(GROUPS, dtype=jnp.int32)[None, :]).astype(jnp.float32)
    ratios = jnp.sqrt(lax.optimization_barrier(jnp.sum(choose * clip_rows[:, None], axis=0))) / jnp.sqrt(lax.optimization_barrier(jnp.sum(choose * dir_rows[:, None], axis=0)) + 1e-06)
    row_ratio = lax.optimization_barrier(jnp.sum(choose * ratios[None, :], axis=1))
    scaling = math.sqrt(PARAMS)
    outputs = []
    row_start = 0
    for member, heading in zip(clipped, directions):
        row_count = member.shape[0]
        outputs.append(scaling * (member + row_ratio[row_start:row_start + row_count, None] * heading))
        row_start = row_start + row_count
    return outputs

def step_forward(tracer, kernels, wet_cells):
    tracer_pad = jnp.pad(tracer, ((0, 0), (1, 1), (1, 1)))
    tracer_round = tracer_pad.astype(jnp.bfloat16)
    first_pre = convolve(tracer_round, kernels[0][0], kernels[0][1])
    hidden = silu_parts(first_pre)[0].astype(jnp.bfloat16)
    hidden_pad = jnp.pad(hidden, ((0, 0), (1, 1), (1, 1)))
    stored_tail = tail_forward(hidden_pad, kernels)
    return (advance(tracer_pad, stored_tail[3], wet_cells), (tracer_pad, tracer_round, first_pre, hidden_pad, stored_tail))

def reference(initial_field, target_field, land_mask, conv_one, conv_two, head_weights, dir_one, dir_two, dir_three, group_ids):
    wet_cells = land_mask.astype(jnp.float32)
    kernels = split_kernels(conv_one, conv_two, head_weights)
    tracer = wet_cells * initial_field
    history = [tracer]
    for step_index in range(STEPS):
        tracer = step_forward(tracer, kernels, wet_cells)[0]
        history.append(tracer)
    final_field = tracer
    adjoint = wet_cells * (tracer - target_field)
    totals = [jnp.zeros(conv_one.shape, jnp.float32), jnp.zeros(conv_two.shape, jnp.float32), jnp.zeros(head_weights.shape, jnp.float32)]
    for step_index in reversed(range(STEPS)):
        stored = step_forward(history[step_index], kernels, wet_cells)[1]
        tracer_pad, tracer_round, first_pre, hidden_pad, stored_tail = stored
        grad_coeffs, near_grad = advance_back(tracer_pad, stored_tail[3], wet_cells, adjoint)
        head_grad, second_grad, hidden_grad = tail_back(hidden_pad, kernels, stored_tail, grad_coeffs)
        first_error = hidden_grad[:, 1:-1, 1:-1] * silu_parts(first_pre)[1]
        first_grad, conv_grad = first_back(tracer_round, kernels[0][0], first_error)
        adjoint = (conv_grad + near_grad)[:, 1:-1, 1:-1]
        totals = [totals[0] + first_grad, totals[1] + second_grad, totals[2] + head_grad]
    updates = finish(totals, [dir_one, dir_two, dir_three], group_ids)
    return (final_field, updates[0], updates[1], updates[2])
```

```python
import functools
import math

import jax
import jax.numpy as jnp
from jax import lax
from jax.experimental import pallas as pl
from jax.experimental.pallas import tpu as pltpu
from jax.sharding import PartitionSpec as P

GROUPS = 6
PARAMS = 43680
RIM = 6
NEAR = 2
LEV = 8
C = 64
K = 32
TILE = 128
MESH = pl.DeviceIdType.MESH
F32 = jnp.float32
BF16 = jnp.bfloat16
VM = pl.BlockSpec(memory_space=pltpu.VMEM)
ANY = pl.BlockSpec(memory_space=pl.ANY)
LIMIT = 56 * 1024 * 1024
NT = (((1,), (1,)), ((), ()))


def dot(a, b):
    return jnp.dot(a, b, preferred_element_type=F32)


def dot_nt(a, b):
    return lax.dot_general(a, b, NT, preferred_element_type=F32)


def sigmoid(v):
    return 0.5 * jnp.tanh(0.5 * v) + 0.5


def roll(v, shift):
    return pltpu.roll(v, shift % v.shape[1], 1)


def fused_kernel(
    sizes, field_in, target_in, mask_in, w1_in, w2_in, w3_in,
    final_ref, out_ref,
    fld, wet_s, tgt, adj, x9, z1, h1, z2, h2, prob, e2m, up, e1m, vv, e3m,
    field, target, mask, w1_ref, w2_ref, w3_ref, wet, left, right, packed,
    grads_ref, got, part, parts, mine,
    load_sem, send_sem, recv_sem, send_one, recv_one, send_two, recv_two, send_three, recv_three,
):
    n_gx, n_gy = sizes
    gx = lax.axis_index("gx")
    gy = lax.axis_index("gy")
    h, width = mask.shape
    rows = h + 2 * RIM
    wide = width + TILE
    ys = [lax.rem(gy + k, n_gy) for k in range(1, n_gy)]
    xs = [lax.rem(gx + k, n_gx) for k in range(1, n_gx)]
    moves = [(dx, dy) for dx in (-1, 0, 1) for dy in (-1, 0, 1) if (dx, dy) != (0, 0)]

    def exists(dx, dy):
        x = gx + dx
        y = gy + dy
        return (x >= 0) & (x < n_gx) & (y >= 0) & (y < n_gy)

    barrier = pltpu.get_barrier_semaphore()
    count = jnp.int32(n_gy + n_gx - 2)
    for dx, dy in moves:
        if dx and dy:
            @pl.when(exists(dx, dy))
            def _():
                pl.semaphore_signal(barrier, inc=1, device_id=(gx + dx, gy + dy), device_id_type=MESH)
            count = count + jnp.where(exists(dx, dy), 1, 0)
    for x in xs:
        pl.semaphore_signal(barrier, inc=1, device_id=(x, gy), device_id_type=MESH)
    for y in ys:
        pl.semaphore_signal(barrier, inc=1, device_id=(gx, y), device_id_type=MESH)

    loads = [
        pltpu.make_async_copy(src, dst, load_sem.at[i])
        for i, (src, dst) in enumerate(
            [(field_in, field), (target_in, target), (mask_in, mask),
             (w1_in, w1_ref), (w2_in, w2_ref), (w3_in, w3_ref)]
        )
    ]
    for copy in loads:
        copy.start()

    def pairs(dx, dy):
        if dy:
            side = left if dy > 0 else right
            return [(packed.at[0 if dy > 0 else 1], side.at[1 - dx])]
        near = pl.ds(0, width)
        if dx > 0:
            return [
                (fld.at[0, pl.ds(h, RIM), :, near], fld.at[0, pl.ds(0, RIM), :, near]),
                (tgt.at[pl.ds(RIM + h - NEAR, NEAR), :, near], tgt.at[pl.ds(RIM - NEAR, NEAR), :, near]),
                (wet.at[1], wet.at[0]),
            ]
        return [
            (fld.at[0, pl.ds(RIM, RIM), :, near], fld.at[0, pl.ds(RIM + h, RIM), :, near]),
            (tgt.at[pl.ds(RIM, NEAR), :, near], tgt.at[pl.ds(RIM + h, NEAR), :, near]),
            (wet.at[1], wet.at[2]),
        ]

    for dx, dy in moves:
        @pl.when(jnp.logical_not(exists(-dx, -dy)))
        def _():
            for _, dst in pairs(dx, dy):
                dst[...] = jnp.zeros(dst.shape, F32)

    for copy in loads[:3]:
        copy.wait()
    lane = lax.broadcasted_iota(jnp.int32, (3 * LEV, TILE), 1)
    strips = [jnp.zeros((3 * LEV, TILE), F32) for _ in range(2)]
    for r in range(h):
        wide_wet = jnp.broadcast_to(mask[r : r + 1, :].astype(F32), (LEV, width))
        values = wide_wet * field[:, r, :]
        goal = target[:, r, :]
        fld[0, RIM + r, :, :width] = values
        tgt[RIM + r, :, :width] = goal
        mixed = jnp.concatenate([values, wide_wet, goal], axis=0)
        here = (lane >= LEV * r) & (lane < LEV * r + LEV)
        low = mixed[:, :TILE]
        high = mixed[:, width - TILE :]
        strips[0] = jnp.where(here, roll(high, LEV * r + LEV), strips[0])
        strips[1] = jnp.where(here, roll(low, LEV * r), strips[1])
    wet[1] = mask[...].astype(F32)
    packed[0] = strips[0]
    packed[1] = strips[1]

    pl.semaphore_wait(barrier, count)

    copies = []
    index = 0
    for dx, dy in moves:
        group = []
        for src, dst in pairs(dx, dy):
            group.append(
                pltpu.make_async_remote_copy(
                    src_ref=src,
                    dst_ref=dst,
                    send_sem=send_sem.at[index],
                    recv_sem=recv_sem.at[index],
                    device_id=(gx + dx, gy + dy),
                    device_id_type=MESH,
                )
            )
            index += 1
        copies.append((dx, dy, group))
    for dx, dy, group in copies:
        @pl.when(exists(dx, dy))
        def _():
            for copy in group:
                copy.start()

    for copy in loads[3:]:
        copy.wait()
    wa = w1_ref[...]
    w1 = wa[:, : 9 * LEV].astype(BF16)
    b1 = wa[:, 9 * LEV :]
    wb = w2_ref[...]
    tap = lambda a, b: wb[:, (3 * a + b) * C : (3 * a + b + 1) * C]
    w2f = jnp.concatenate(
        [jnp.concatenate([tap(a, b) for a in range(3)], axis=1) for b in range(3)], axis=0
    )
    w2 = w2f.astype(BF16)
    w2t = w2f.T.astype(BF16)
    b2 = wb[:, 9 * C :]
    wc = w3_ref[...]
    w3 = wc[:, :C].astype(BF16)
    w3t = wc[:, :C].T.astype(BF16)
    b3 = wc[:, C:]
    w1t = wa[:, : 9 * LEV].T.astype(BF16)

    is_right = lax.broadcasted_iota(jnp.int32, (3 * LEV, TILE), 1) < TILE // 2
    for dx, dy, group in copies:
        @pl.when(exists(-dx, -dy))
        def _():
            for copy in group:
                copy.wait_recv()

    for r in range(rows):
        where = 0 if r < RIM else 1 if r < RIM + h else 2
        k = (r + h - RIM) % h
        side_tile = jnp.where(
            is_right, roll(right[where], -LEV * k), roll(left[where], -LEV * k - LEV)
        )
        fld[0, r, :, width:] = side_tile[:LEV]
        wet_row = jnp.broadcast_to(wet[where, k : k + 1, :], (LEV, width))
        wet_s[r] = jnp.concatenate([wet_row, side_tile[LEV : 2 * LEV]], axis=1)
        if RIM - NEAR <= r < RIM + h + NEAR:
            tgt[r, :, width:] = side_tile[2 * LEV :]

    col_left = jnp.where(gy > 0, 1.0, 0.0).astype(F32)
    col_right = jnp.where(gy < n_gy - 1, 1.0, 0.0).astype(F32)
    side = jnp.where(is_right[0:1], col_right, col_left)
    col_ok = jnp.concatenate([jnp.ones((1, width), F32), side], axis=1)

    def inside(r):
        i = gx * h + r - RIM
        ok = (i >= 0) & (i < n_gx * h)
        return col_ok * jnp.where(ok, 1.0, 0.0).astype(F32)

    def loop(start, stop, body):
        lax.fori_loop(start, stop, lambda r, c: (body(r), c)[1], 0, unroll=True)

    def forward(s, rad):
        def first(r):
            parts = []
            for a in range(3):
                row = fld[s, r + a - 1]
                parts += [roll(row, 1), row, roll(row, -1)]
            cols = jnp.concatenate(parts, axis=0).astype(BF16)
            x9[s, r] = cols
            z = dot(w1, cols) + b1
            z1[s, r] = z
            h1[s, r] = (z * sigmoid(z) * inside(r)).astype(BF16)

        loop(RIM - rad - 1, RIM + h + rad + 1, first)

        def second(r):
            h3 = jnp.concatenate([h1[s, r - 1], h1[s, r], h1[s, r + 1]], axis=0)
            y = dot(w2, h3)
            z = roll(y[0:C], 1) + y[C : 2 * C] + roll(y[2 * C :], -1) + b2
            z2[s, r] = z
            hb = (z * sigmoid(z)).astype(BF16)
            h2[s, r] = hb
            p = sigmoid(dot(w3, hb) + b3)
            prob[s, r] = p
            center = fld[s, r]
            c = 0.25 * p
            change = (
                c[0:8] * (fld[s, r + 1] - center)
                + c[8:16] * (fld[s, r - 1] - center)
                + c[16:24] * (roll(center, -1) - center)
                + c[24:32] * (roll(center, 1) - center)
            )
            fld[s + 1, r] = center + wet_s[r] * change

        loop(RIM - rad, RIM + h + rad, second)

    forward(0, 4)
    forward(1, 2)
    for r in range(h):
        final_ref[:, r, :] = fld[2, RIM + r][:, :width]

    def adjoint_start(r):
        adj[1, r] = wet_s[r] * (fld[2, r] - tgt[r])

    loop(RIM - 2, RIM + h + 2, adjoint_start)

    lane_w = lax.broadcasted_iota(jnp.int32, (1, wide), 1)
    own_lane = jnp.where(lane_w < width, 1.0, 0.0).astype(F32)
    fold = lambda v: sum(v[:, k * TILE : (k + 1) * TILE] for k in range(v.shape[1] // TILE))

    def errors(s, r):
        center = fld[s, r]
        wg = wet_s[r] * adj[s, r]
        p = prob[s, r]
        diff = jnp.concatenate(
            [
                wg * (fld[s, r + 1] - center),
                wg * (fld[s, r - 1] - center),
                wg * (roll(center, -1) - center),
                wg * (roll(center, 1) - center),
            ],
            axis=0,
        )
        e3 = diff * (0.25 * p * (1.0 - p))
        e3b = e3.astype(BF16)
        z = z2[s, r]
        g = sigmoid(z)
        e2 = dot(w3t, e3b) * (g * (1.0 + z * (1.0 - g)))
        return e3, e3b, e2

    def spread(e2):
        return jnp.concatenate([roll(e2, -1), e2, roll(e2, 1)], axis=0).astype(BF16)

    zero_b = (jnp.zeros((K, TILE), F32), jnp.zeros((C, TILE), F32))

    def own_rows(s, carry):
        def body(r, c):
            e3, e3b, e2 = errors(s, r)
            e3m[s, r - RIM] = e3b[:, :width]
            em = e2 * own_lane
            m = spread(em)
            e2m[s, r - RIM] = m
            if s == 0:
                up[r] = dot(w2t, m)
            else:
                up[r] = dot(w2t, spread(e2))
            return (c[0] + fold(e3[:, :width]), c[1] + fold(e2[:, :width]))

        return lax.fori_loop(RIM, RIM + h, body, carry, unroll=True)

    def rim_row(r):
        _, _, e2 = errors(1, r)
        up[r] = dot(w2t, spread(e2))

    def first_error(s, r):
        hid = up[r + 1][0:C] + up[r][C : 2 * C] + up[r - 1][2 * C :]
        z = z1[s, r]
        g = sigmoid(z)
        return hid * (g * (1.0 + z * (1.0 - g))) * inside(r)

    sums = own_rows(1, zero_b)
    for r in (RIM - 2, RIM - 1, RIM + h, RIM + h + 1):
        rim_row(r)

    def back_one(r, c):
        e1 = first_error(1, r)
        eb = e1.astype(BF16)
        e1m[1, r - RIM + 1] = (e1 * own_lane).astype(BF16)
        t = dot(w1t, eb)
        piece = lambda a, b: t[(3 * a + b) * LEV : (3 * a + b + 1) * LEV]
        for a in range(3):
            vv[r, a] = roll(piece(a, 0), -1) + piece(a, 1) + roll(piece(a, 2), 1)
        keep = jnp.where((r >= RIM) & (r < RIM + h), 1.0, 0.0).astype(F32)
        return c + fold(e1[:, :width]) * keep

    sum_one = lax.fori_loop(
        RIM - 1, RIM + h + 1, back_one, jnp.zeros((C, TILE), F32), unroll=True
    )

    def adjoint_next(r):
        wg = wet_s[r] * adj[1, r]
        p = prob[1, r]
        c = [0.25 * p[n * 8 : n * 8 + 8] for n in range(4)]
        above = wet_s[r - 1] * adj[1, r - 1] * (0.25 * prob[1, r - 1][0:8])
        below = wet_s[r + 1] * adj[1, r + 1] * (0.25 * prob[1, r + 1][8:16])
        adj[0, r] = (
            adj[1, r]
            - wg * (c[0] + c[1] + c[2] + c[3])
            + above
            + below
            + roll(wg * c[2], 1)
            + roll(wg * c[3], -1)
            + vv[r + 1, 0]
            + vv[r, 1]
            + vv[r - 1, 2]
        )

    loop(RIM, RIM + h, adjoint_next)

    sums = own_rows(0, sums)
    for r in (RIM - 2, RIM - 1, RIM + h, RIM + h + 1):
        up[r] = jnp.zeros((3 * C, wide), F32)

    def back_zero(r, c):
        e1 = first_error(0, r)
        e1m[0, r - RIM + 1] = e1.astype(BF16)
        return c + fold(e1)

    sum_one = lax.fori_loop(RIM - 1, RIM + h + 1, back_zero, sum_one, unroll=True)

    g1 = jnp.zeros((C, 9 * LEV), F32)
    g2 = jnp.zeros((3 * C, 3 * C), F32)
    g3 = jnp.zeros((K, C), F32)
    for s in range(2):
        for r in range(h):
            h3 = jnp.concatenate([h1[s, RIM + r + a - 1] for a in range(3)], axis=0)
            g2 = g2 + dot_nt(e2m[s, r], h3)
            g3 = g3 + dot_nt(e3m[s, r], h2[s, RIM + r][:, :width])
        for r in range(h + 2) if s == 0 else range(1, h + 1):
            g1 = g1 + dot_nt(e1m[s, r], x9[s, RIM + r - 1])
    total = lambda v: jnp.sum(v, axis=1, keepdims=True)
    pad = lambda v: jnp.concatenate([v, jnp.zeros((v.shape[0], C - v.shape[1]), F32)], axis=1)
    extra = jnp.concatenate(
        [
            g1[:, :C],
            pad(jnp.concatenate([g1[:, C:], total(sum_one), total(sums[1])], axis=1)),
            g3,
            pad(total(sums[0])),
        ],
        axis=0,
    )
    packed_grads = jnp.concatenate([g2, extra], axis=1)
    chunk = grads_ref.shape[1]
    for y in range(n_gy):
        lo = y * chunk
        if lo + chunk <= 3 * C:
            grads_ref[y] = packed_grads[lo : lo + chunk]
        else:
            grads_ref[y] = jnp.zeros((chunk, 4 * C), F32)

    one = [
        pltpu.make_async_remote_copy(
            src_ref=grads_ref.at[y], dst_ref=got.at[k],
            send_sem=send_one.at[k], recv_sem=recv_one.at[k],
            device_id=(gx, y), device_id_type=MESH,
        )
        for k, y in enumerate(ys)
    ]
    for copy in one:
        copy.start()
    acc = grads_ref[gy]
    for k, copy in enumerate(one):
        copy.wait_recv()
        acc = acc + got[k]
    part[...] = acc
    two = [
        pltpu.make_async_remote_copy(
            src_ref=part, dst_ref=parts.at[gx],
            send_sem=send_two.at[k], recv_sem=recv_two.at[k],
            device_id=(x, gy), device_id_type=MESH,
        )
        for k, x in enumerate(xs)
    ]
    for copy in two:
        copy.start()
    parts[gx] = acc
    for copy in two:
        copy.wait_recv()
    acc = parts[0]
    for x in range(1, n_gx):
        acc = acc + parts[x]
    acc = acc.astype(out_ref.dtype)
    mine[...] = acc
    three = [
        pltpu.make_async_remote_copy(
            src_ref=mine, dst_ref=out_ref.at[gy],
            send_sem=send_three.at[k], recv_sem=recv_three.at[k],
            device_id=(gx, y), device_id_type=MESH,
        )
        for k, y in enumerate(ys)
    ]
    for copy in three:
        copy.start()
    out_ref[gy] = acc
    for copy in three:
        copy.wait_recv()
    for dx, dy, group in copies:
        @pl.when(exists(dx, dy))
        def _():
            for copy in group:
                copy.wait_send()
    for copy in one + two + three:
        copy.wait_send()


def finish_kernel(grads, final, d1, d2, d3, ids, final_out, u1, u2, u3):
    final_out[...] = final[...]
    n_parts = 3 * C // grads.shape[1]
    g = jnp.concatenate([grads[y].astype(F32) for y in range(n_parts)], axis=0)
    block = lambda a, b: g[b * C : (b + 1) * C, a * C : (a + 1) * C]
    side = g[:, 3 * C :]
    one = jnp.concatenate([side[:C], side[C : 2 * C, : 9 * LEV - C + 1]], axis=1)
    bias_two = side[C : 2 * C, 9 * LEV - C + 1 : 9 * LEV - C + 2]
    two = jnp.concatenate([block(a, b) for a in range(3) for b in range(3)] + [bias_two], axis=1)
    three = jnp.concatenate([side[2 * C : 2 * C + K], side[2 * C + K :, 0:1]], axis=1)
    members = [one, two, three]
    heads = [d1[...], d2[...], d3[...]]
    row_sq = lambda v: jnp.sum(v * v, axis=1, keepdims=True)
    grad_rows = jnp.concatenate([row_sq(m) for m in members], axis=0)
    dir_rows = jnp.concatenate([row_sq(m) for m in heads], axis=0)
    total = jnp.sum(grad_rows, axis=0, keepdims=True)
    factor = 1.0 / jnp.maximum(jnp.sqrt(total), 1.0)
    clip_rows = grad_rows * (factor * factor)
    count = grad_rows.shape[0]
    i0 = lax.broadcasted_iota(jnp.int32, (count, count), 0)
    i1 = lax.broadcasted_iota(jnp.int32, (count, count), 1)
    spread = jnp.broadcast_to(ids[...].astype(F32), (count, count))
    column = jnp.sum(jnp.where(i0 == i1, spread, 0.0), axis=1, keepdims=True)
    row_ratio = jnp.zeros((count, 1), F32)
    for k in range(GROUPS):
        hit = column == float(k)
        pick = lambda v: jnp.sum(jnp.where(hit, v, 0.0), axis=0, keepdims=True)
        ratio = jnp.sqrt(pick(clip_rows)) / jnp.sqrt(pick(dir_rows) + 1e-06)
        row_ratio = row_ratio + jnp.where(hit, ratio, 0.0)
    scaling = math.sqrt(PARAMS)
    start = 0
    for ref, member, head in zip((u1, u2, u3), members, heads):
        n = member.shape[0]
        ref[...] = scaling * (member * factor + row_ratio[start : start + n] * head)
        start += n


def per_device(sizes, field, target, mask, conv_one, conv_two, head, d1, d2, d3, ids):
    n_gx, n_gy = sizes
    _, h, width = field.shape
    rows = h + 2 * RIM
    wide = width + TILE
    shape = jax.ShapeDtypeStruct
    chunk = 8 * -(-3 * C // (8 * n_gy))
    dma = pltpu.SemaphoreType.DMA
    final, summed = pl.pallas_call(
        functools.partial(fused_kernel, sizes),
        name="fused",
        out_shape=[shape(field.shape, F32), shape((n_gy, chunk, 4 * C), BF16)],
        in_specs=[ANY] * 6,
        out_specs=[VM] * 2,
        scratch_shapes=[
            pltpu.VMEM((3, rows, LEV, wide), F32),
            pltpu.VMEM((rows, LEV, wide), F32),
            pltpu.VMEM((rows, LEV, wide), F32),
            pltpu.VMEM((2, rows, LEV, wide), F32),
            pltpu.VMEM((2, rows, 9 * LEV, wide), BF16),
            pltpu.VMEM((2, rows, C, wide), F32),
            pltpu.VMEM((2, rows, C, wide), BF16),
            pltpu.VMEM((2, rows, C, wide), F32),
            pltpu.VMEM((2, rows, C, wide), BF16),
            pltpu.VMEM((2, rows, K, wide), F32),
            pltpu.VMEM((2, h, 3 * C, wide), BF16),
            pltpu.VMEM((rows, 3 * C, wide), F32),
            pltpu.VMEM((2, h + 2, C, wide), BF16),
            pltpu.VMEM((rows, 3, LEV, wide), F32),
            pltpu.VMEM((2, h, K, width), BF16),
            pltpu.VMEM(field.shape, F32),
            pltpu.VMEM(target.shape, F32),
            pltpu.VMEM(mask.shape, jnp.int32),
            pltpu.VMEM(conv_one.shape, F32),
            pltpu.VMEM(conv_two.shape, F32),
            pltpu.VMEM(head.shape, F32),
            pltpu.VMEM((3, h, width), F32),
            pltpu.VMEM((3, 3 * LEV, TILE), F32),
            pltpu.VMEM((3, 3 * LEV, TILE), F32),
            pltpu.VMEM((2, 3 * LEV, TILE), F32),
            pltpu.VMEM((n_gy, chunk, 4 * C), F32),
            pltpu.VMEM((n_gy - 1, chunk, 4 * C), F32),
            pltpu.VMEM((chunk, 4 * C), F32),
            pltpu.VMEM((n_gx, chunk, 4 * C), F32),
            pltpu.VMEM((chunk, 4 * C), BF16),
            dma((6,)), dma((12,)), dma((12,)),
            dma((n_gy - 1,)), dma((n_gy - 1,)),
            dma((n_gx - 1,)), dma((n_gx - 1,)),
            dma((n_gy - 1,)), dma((n_gy - 1,)),
        ],
        compiler_params=pltpu.CompilerParams(
            collective_id=0, has_side_effects=True, vmem_limit_bytes=LIMIT
        ),
    )(field, target, mask, conv_one, conv_two, head)
    final, u1, u2, u3 = pl.pallas_call(
        finish_kernel,
        name="update",
        out_shape=[
            shape(field.shape, F32),
            shape(conv_one.shape, F32), shape(conv_two.shape, F32), shape(head.shape, F32),
        ],
        in_specs=[VM] * 6,
        out_specs=[VM] * 4,
    )(summed, final, d1, d2, d3, ids.reshape(1, -1))
    return final, u1, u2, u3


def solution(mesh):
    grid = P(None, "gx", "gy")
    placed = (grid, grid, P("gx", "gy")) + (P(),) * 7
    return jax.shard_map(
        functools.partial(per_device, (mesh.shape["gx"], mesh.shape["gy"])),
        mesh=mesh,
        in_specs=placed,
        out_specs=(grid, P(), P(), P()),
        check_vma=False,
    )
```

```python
import functools
import math

import jax
import jax.numpy as jnp
from jax import lax
from jax.experimental import pallas as pl
from jax.experimental.pallas import tpu as pltpu
from jax.sharding import PartitionSpec as P

GROUPS = 6
PARAMS = 43680
RIM = 6
NEAR = 2
LEV = 8
C = 64
K = 32
TILE = 128
SLOTS = 4
SLOT = TILE // SLOTS
MESH = pl.DeviceIdType.MESH
F32 = jnp.float32
BF16 = jnp.bfloat16
VM = pl.BlockSpec(memory_space=pltpu.VMEM)
ANY = pl.BlockSpec(memory_space=pl.ANY)
LIMIT = 56 * 1024 * 1024
NT = (((1,), (1,)), ((), ()))


def dot(a, b):
    return jnp.dot(a, b, preferred_element_type=F32)


def dot_nt(a, b):
    return lax.dot_general(a, b, NT, preferred_element_type=F32)


def sigmoid(v):
    return 0.5 * jnp.tanh(0.5 * v) + 0.5


def roll(v, shift):
    return pltpu.roll(v, shift % v.shape[1], 1)


def fused_kernel(
    sizes, field_in, target_in, mask_in, w1_in, w2_in, w3_in,
    final_ref, out_ref, rest_ref,
    fo, fh, fl, fr, flh, frh, wo, wh, to, th, ao, ah, ad,
    xo, xh, ho, hh, p1o, p1h, p2o, p2h, t3o, t3h, h2o, eo, eh, e3o, e1o, e1h, vo,
    field, target, mask, w1_ref, w2_ref, w3_ref, wet, left, right, packed,
    grads_ref, got, part, parts, mine, extra_ref, extra_got, extra_part, extra_parts, extra_mine,
    load_sem, send_sem, recv_sem, send_one, recv_one, send_two, recv_two, send_three, recv_three,
    send_four, recv_four, send_five, recv_five, send_six, recv_six,
):
    n_gx, n_gy = sizes
    gx = lax.axis_index("gx")
    gy = lax.axis_index("gy")
    h, width = mask.shape
    rows = h + 2 * RIM
    tiles = rows // SLOTS
    ys = [lax.rem(gy + k, n_gy) for k in range(1, n_gy)]
    xs = [lax.rem(gx + k, n_gx) for k in range(1, n_gx)]
    moves = [(dx, dy) for dx in (-1, 0, 1) for dy in (-1, 0, 1) if (dx, dy) != (0, 0)]

    def exists(dx, dy):
        x = gx + dx
        y = gy + dy
        return (x >= 0) & (x < n_gx) & (y >= 0) & (y < n_gy)

    barrier = pltpu.get_barrier_semaphore()
    count = jnp.int32(n_gy + n_gx - 2)
    for dx, dy in moves:
        if dx and dy:
            @pl.when(exists(dx, dy))
            def _():
                pl.semaphore_signal(barrier, inc=1, device_id=(gx + dx, gy + dy), device_id_type=MESH)
            count = count + jnp.where(exists(dx, dy), 1, 0)
    for x in xs:
        pl.semaphore_signal(barrier, inc=1, device_id=(x, gy), device_id_type=MESH)
    for y in ys:
        pl.semaphore_signal(barrier, inc=1, device_id=(gx, y), device_id_type=MESH)

    loads = [
        pltpu.make_async_copy(src, dst, load_sem.at[i])
        for i, (src, dst) in enumerate(
            [(field_in, field), (target_in, target), (mask_in, mask),
             (w1_in, w1_ref), (w2_in, w2_ref), (w3_in, w3_ref)]
        )
    ]
    for copy in loads:
        copy.start()

    def pairs(dx, dy):
        if dy:
            side = left if dy > 0 else right
            return [(packed.at[0 if dy > 0 else 1], side.at[1 - dx])]
        if dx > 0:
            return [
                (fo.at[0, pl.ds(h, RIM)], fo.at[0, pl.ds(0, RIM)]),
                (to.at[pl.ds(RIM + h - NEAR, NEAR)], to.at[pl.ds(RIM - NEAR, NEAR)]),
                (wet.at[1], wet.at[0]),
            ]
        return [
            (fo.at[0, pl.ds(RIM, RIM)], fo.at[0, pl.ds(RIM + h, RIM)]),
            (to.at[pl.ds(RIM, NEAR)], to.at[pl.ds(RIM + h, NEAR)]),
            (wet.at[1], wet.at[2]),
        ]

    for dx, dy in moves:
        @pl.when(jnp.logical_not(exists(-dx, -dy)))
        def _():
            for _, dst in pairs(dx, dy):
                dst[...] = jnp.zeros(dst.shape, F32)

    for copy in loads[:3]:
        copy.wait()
    lane = lax.broadcasted_iota(jnp.int32, (3 * LEV, TILE), 1)
    strips = [jnp.zeros((3 * LEV, TILE), F32) for _ in range(2)]
    for r in range(h):
        wide_wet = jnp.broadcast_to(mask[r : r + 1, :].astype(F32), (LEV, width))
        values = wide_wet * field[:, r, :]
        goal = target[:, r, :]
        fo[0, RIM + r] = values
        to[RIM + r] = goal
        mixed = jnp.concatenate([values, wide_wet, goal], axis=0)
        here = (lane >= LEV * r) & (lane < LEV * r + LEV)
        low = mixed[:, :TILE]
        high = mixed[:, width - TILE :]
        strips[0] = jnp.where(here, roll(high, LEV * r + LEV), strips[0])
        strips[1] = jnp.where(here, roll(low, LEV * r), strips[1])
    wet[1] = mask[...].astype(F32)
    packed[0] = strips[0]
    packed[1] = strips[1]

    pl.semaphore_wait(barrier, count)

    copies = []
    index = 0
    for dx, dy in moves:
        group = []
        for src, dst in pairs(dx, dy):
            group.append(
                pltpu.make_async_remote_copy(
                    src_ref=src,
                    dst_ref=dst,
                    send_sem=send_sem.at[index],
                    recv_sem=recv_sem.at[index],
                    device_id=(gx + dx, gy + dy),
                    device_id_type=MESH,
                )
            )
            index += 1
        copies.append((dx, dy, group))
    for dx, dy, group in copies:
        @pl.when(exists(dx, dy))
        def _():
            for copy in group:
                copy.start()

    for copy in loads[3:]:
        copy.wait()
    slot_lane = lax.broadcasted_iota(jnp.int32, (1, TILE), 1) % SLOT
    slot_row = lax.broadcasted_iota(jnp.int32, (1, TILE), 1) // SLOT * tiles
    lane1 = lax.broadcasted_iota(jnp.int32, (1, TILE), 1)

    def pad16(v, n):
        return jnp.concatenate([v, jnp.zeros((v.shape[0], n - v.shape[1]), F32)], axis=1)

    def thirds(b):
        high = b.astype(BF16).astype(F32)
        low = b - high
        middle = low.astype(BF16).astype(F32)
        return jnp.concatenate([high, middle, low - middle], axis=1)

    wa = 0.5 * w1_ref[...]
    wb = 0.5 * w2_ref[...]
    wc = 0.5 * w3_ref[...]
    none = jnp.zeros((C, LEV), F32)
    w1 = jnp.concatenate(
        [
            wa[:, : 3 * LEV], none,
            wa[:, 3 * LEV : 6 * LEV], pad16(thirds(wa[:, 9 * LEV :]), LEV),
            wa[:, 6 * LEV : 9 * LEV], none,
        ],
        axis=1,
    ).astype(BF16)
    w2 = jnp.concatenate([wb[:, : 9 * C], pad16(thirds(wb[:, 9 * C :]), 16)], axis=1).astype(BF16)
    w3 = jnp.concatenate([wc[:, :C], pad16(thirds(wc[:, C:]), 16)], axis=1).astype(BF16)
    w3t = wc[:, :C].T.astype(BF16)
    flip = wb[:, : 9 * C].T
    w2t = jnp.concatenate([flip[k * C : (k + 1) * C] for k in range(8, -1, -1)], axis=1).astype(BF16)
    turn = (2.0 * wa[:, : 9 * LEV]).T
    w1t = jnp.concatenate(
        [
            jnp.concatenate(
                [turn[(3 * a + b) * LEV : (3 * a + b + 1) * LEV] for b in (2, 1, 0)], axis=1
            )
            for a in range(3)
        ],
        axis=0,
    ).astype(BF16)
    ones = jnp.ones((16, width), BF16)
    unit = jnp.ones((LEV, width), F32)

    first_lane = lane1 == 0
    last_lane = lane1 == TILE - 1

    def own_left(own, halo, q):
        r0 = roll(own[:, :TILE], 1)
        r1 = roll(own[:, TILE:], 1)
        rh = roll(halo, 1 - SLOT * (q + 1))
        return jnp.concatenate([jnp.where(first_lane, rh, r0), jnp.where(first_lane, r0, r1)], axis=1)

    def own_right(own, halo, q):
        r0 = roll(own[:, :TILE], -1)
        r1 = roll(own[:, TILE:], -1)
        rh = roll(halo, TILE - 1 - SLOT * q)
        return jnp.concatenate([jnp.where(last_lane, r1, r0), jnp.where(last_lane, rh, r1)], axis=1)

    def halo_left(halo, owns):
        out = roll(halo, 1)
        for q, own in enumerate(owns):
            if own is not None:
                out = jnp.where(lane1 == SLOT * q, roll(own[:, TILE:], 1 + SLOT * q), out)
        return out

    def halo_right(halo, owns):
        out = roll(halo, -1)
        for q, own in enumerate(owns):
            if own is not None:
                out = jnp.where(lane1 == SLOT * q + SLOT - 1, roll(own[:, :TILE], SLOT * q + SLOT - 1), out)
        return out

    def at(r):
        return slice(r * width, (r + 1) * width)

    def tile(t, n=1):
        return slice((t + 1) * TILE, (t + 1 + n) * TILE)

    def twist(ref, s):
        ref[s, :, tile(-1)] = roll(ref[s, :, tile(tiles - 1)], SLOT)
        ref[s, :, tile(tiles)] = roll(ref[s, :, tile(0)], -SLOT)

    def stack_own(ref, s, r, *more):
        return jnp.concatenate([ref[s, :, at(r + a)] for a in (-1, 0, 1)] + list(more), axis=0)

    def stack_halo(ref, s, t, n, *more):
        return jnp.concatenate([ref[s, :, tile(t + a, n)] for a in (-1, 0, 1)] + list(more), axis=0)

    pieces = [(t, min(2, tiles - t)) for t in range(0, tiles, 2)]
    up_ok = jnp.where(gx > 0, 1.0, 0.0).astype(F32)
    down_ok = jnp.where(gx < n_gx - 1, 1.0, 0.0).astype(F32)
    left_ok = jnp.where(gy > 0, 1.0, 0.0).astype(F32)
    right_ok = jnp.where(gy < n_gy - 1, 1.0, 0.0).astype(F32)

    def inside_halo(t):
        r = slot_row + t
        side = jnp.where(slot_lane < SLOT // 2, right_ok, left_ok)
        return side * jnp.where(r < RIM, up_ok, jnp.where(r >= RIM + h, down_ok, 1.0))

    def inside_own(v, r):
        return v * up_ok if r < RIM else v * down_ok if r >= RIM + h else v

    in_halo = [inside_halo(t) for t in range(tiles)]

    def halo_mask(t, n):
        return jnp.concatenate(in_halo[t : t + n], axis=1)

    for dx, dy, group in copies:
        @pl.when(exists(-dx, -dy))
        def _():
            for copy in group:
                copy.wait_recv()

    for t in range(tiles):
        side_tile = jnp.zeros((3 * LEV, TILE), F32)
        for q in range(SLOTS):
            r = t + tiles * q
            where = 0 if r < RIM else 1 if r < RIM + h else 2
            k = (r + h - RIM) % h
            is_right = (lane1 >= SLOT * q) & (lane1 < SLOT * q + LEV)
            is_left = (lane1 >= SLOT * q + SLOT - LEV) & (lane1 < SLOT * q + SLOT)
            side_tile = jnp.where(is_right, roll(right[where], SLOT * q - LEV * k), side_tile)
            side_tile = jnp.where(
                is_left, roll(left[where], SLOT * q + SLOT - LEV - LEV * k), side_tile
            )
        fh[0, :, tile(t)] = side_tile[:LEV]
        wh[t] = side_tile[LEV : 2 * LEV]
        th[t] = side_tile[2 * LEV :]
    twist(fh, 0)
    for r in range(rows):
        where = 0 if r < RIM else 1 if r < RIM + h else 2
        k = (r + h - RIM) % h
        wo[r] = jnp.broadcast_to(wet[where, k : k + 1, :], (LEV, width))

    def activate(u):
        t = jnp.tanh(u)
        ut = u * t
        return u + ut, (1.0 + t) * (1.0 + u - ut)

    def forward(s, rad):
        low, high = (0, rows - 1) if s == 0 else (RIM - 4, RIM + h + 3)
        near = lambda r: min(max(r, low), high)
        for t in range(tiles):
            halo = fh[s, :, tile(t)]
            owns = [fo[s, near(t + tiles * q)] for q in range(SLOTS)]
            before = halo_left(halo, owns)
            after = halo_right(halo, owns)
            flh[s, t] = before
            frh[s, t] = after
            xh[s, :, tile(t)] = jnp.concatenate(
                [before, halo, after, unit[:, :TILE]], axis=0
            ).astype(BF16)
        twist(xh, s)
        for r in range(RIM - rad - 2, RIM + h + rad + 2):
            own = fo[s, r]
            halo = fh[s, :, tile(r % tiles)]
            before = own_left(own, halo, r // tiles)
            after = own_right(own, halo, r // tiles)
            fl[s, r] = before
            fr[s, r] = after
            xo[s, :, at(r)] = jnp.concatenate([before, own, after, unit], axis=0).astype(BF16)
        for t, n in pieces:
            hid, slope = activate(dot(w1, stack_halo(xh, s, t, n)))
            ok = halo_mask(t, n)
            p1h[s, :, t * TILE : (t + n) * TILE] = slope * ok
            hh[s, C : 2 * C, tile(t, n)] = (hid * ok).astype(BF16)
        for r in range(RIM - rad - 1, RIM + h + rad + 1):
            hid, slope = activate(dot(w1, stack_own(xo, s, r)))
            if RIM - 1 <= r < RIM + h + 1:
                p1o[s, :, at(r)] = inside_own(slope, r)
            hid = inside_own(hid, r).astype(BF16)
            halo = hh[s, C : 2 * C, tile(r % tiles)]
            ho[s, :, at(r)] = jnp.concatenate(
                [own_left(hid, halo, r // tiles), hid, own_right(hid, halo, r // tiles)], axis=0
            )
        low, high = RIM - rad - 1, RIM + h + rad
        for t in range(tiles):
            halo = hh[s, C : 2 * C, tile(t)]
            owns = [
                ho[s, C : 2 * C, at(t + tiles * q)] if low <= t + tiles * q <= high else None
                for q in range(SLOTS)
            ]
            hh[s, :C, tile(t)] = halo_left(halo, owns)
            hh[s, 2 * C :, tile(t)] = halo_right(halo, owns)
        twist(hh, s)

        def finish(hid, n):
            return jnp.tanh(dot(w3, jnp.concatenate([hid, ones[:, :n]], axis=0)))

        def change(t3, center, others):
            total = 0.0
            for k, other in enumerate(others):
                total = total + (1.0 + t3[k * LEV : (k + 1) * LEV]) * (other - center)
            return total

        for t, n in pieces:
            hid, slope = activate(dot(w2, stack_halo(hh, s, t, n, ones[:, : n * TILE])))
            t3 = finish(hid.astype(BF16), n * TILE)
            if s == 1:
                p2h[:, t * TILE : (t + n) * TILE] = slope
                t3h[:, t * TILE : (t + n) * TILE] = t3
            for i in range(n):
                center = fh[s, :, tile(t + i)]
                fh[s + 1, :, tile(t + i)] = center + 0.125 * wh[t + i] * change(
                    t3[:, i * TILE : (i + 1) * TILE], center,
                    [fh[s, :, tile(t + i + 1)], fh[s, :, tile(t + i - 1)], frh[s, t + i], flh[s, t + i]],
                )
        twist(fh, s + 1)
        for r in range(RIM - rad, RIM + h + rad):
            hid, slope = activate(dot(w2, stack_own(ho, s, r, ones)))
            hid = hid.astype(BF16)
            mine_row = RIM <= r < RIM + h
            if s == 1 or mine_row:
                p2o[s, :, at(r)] = slope
            if mine_row:
                h2o[s, :, at(r - RIM)] = hid
            t3 = finish(hid, width)
            if s == 1 or mine_row:
                t3o[s, :, at(r)] = t3
            center = fo[s, r]
            fo[s + 1, r] = center + 0.125 * wo[r] * change(
                t3, center, [fo[s, r + 1], fo[s, r - 1], fr[s, r], fl[s, r]]
            )

    forward(0, 4)
    forward(1, 2)
    for r in range(h):
        final_ref[:, r, :] = fo[2, RIM + r]

    fold = lambda v: sum(v[:, k * TILE : (k + 1) * TILE] for k in range(v.shape[1] // TILE))

    for r in range(RIM - 2, RIM + h + 2):
        ao[r] = wo[r] * wo[r] * (fo[2, r] - to[r])
    for t in range(tiles):
        ah[t] = wh[t] * wh[t] * (fh[2, :, tile(t)] - th[t])

    def errors(scaled, t3, slope, center, others):
        e3 = jnp.concatenate([scaled * (other - center) for other in others], axis=0) * (1.0 - t3 * t3)
        e3b = e3.astype(BF16)
        return e3, e3b, dot(w3t, e3b) * slope

    sum3 = jnp.zeros((K, TILE), F32)
    sum2 = jnp.zeros((C, TILE), F32)
    sum1 = jnp.zeros((C, TILE), F32)

    def own_errors(s, r, wg, halo):
        e3, e3b, e2 = errors(
            wg * 0.0625, t3o[s, :, at(r)], p2o[s, :, at(r)], fo[s, r],
            [fo[s, r + 1], fo[s, r - 1], fr[s, r], fl[s, r]],
        )
        e2b = e2.astype(BF16)
        eo[s, :, at(r)] = jnp.concatenate(
            [own_left(e2b, halo, r // tiles), e2b, own_right(e2b, halo, r // tiles)], axis=0
        )
        if RIM <= r < RIM + h:
            e3o[s, :, at(r - RIM)] = e3b
        return e3, e2

    for t in range(tiles):
        lanes = slice(t * TILE, (t + 1) * TILE)
        _, _, e2 = errors(
            ah[t] * 0.0625, t3h[:, lanes], p2h[:, lanes], fh[1, :, tile(t)],
            [fh[1, :, tile(t + 1)], fh[1, :, tile(t - 1)], frh[1, t], flh[1, t]],
        )
        eh[1, C : 2 * C, tile(t)] = e2.astype(BF16)
    for r in range(RIM - 2, RIM + h + 2):
        e3, e2 = own_errors(1, r, ao[r], eh[1, C : 2 * C, tile(r % tiles)])
        if RIM <= r < RIM + h:
            sum3 = sum3 + fold(e3)
            sum2 = sum2 + fold(e2)
    for t in range(tiles):
        halo = eh[1, C : 2 * C, tile(t)]
        owns = [
            eo[1, C : 2 * C, at(t + tiles * q)] if RIM - 2 <= t + tiles * q < RIM + h + 2 else None
            for q in range(SLOTS)
        ]
        eh[1, :C, tile(t)] = halo_left(halo, owns)
        eh[1, 2 * C :, tile(t)] = halo_right(halo, owns)
    twist(eh, 1)
    for t, n in pieces:
        e1 = dot(w2t, stack_halo(eh, 1, t, n)) * p1h[1, :, t * TILE : (t + n) * TILE]
        e1h[:, t * TILE : (t + n) * TILE] = e1.astype(BF16)
    for r in range(RIM - 1, RIM + h + 1):
        e1 = dot(w2t, stack_own(eo, 1, r)) * p1o[1, :, at(r)]
        e1b = e1.astype(BF16)
        if RIM <= r < RIM + h:
            e1o[1, :, at(r)] = e1b
            sum1 = sum1 + fold(e1)
        t = r % tiles
        halo = e1h[:, t * TILE : (t + 1) * TILE]
        vo[r] = dot(
            w1t,
            jnp.concatenate(
                [own_left(e1b, halo, r // tiles), e1b, own_right(e1b, halo, r // tiles)], axis=0
            ),
        )

    def carried(k, r):
        return 0.125 * ao[r] * (1.0 + t3o[1, k * LEV : (k + 1) * LEV, at(r)])

    for r in range(RIM, RIM + h):
        t, q = r % tiles, r // tiles
        lanes = slice(t * TILE, (t + 1) * TILE)
        halo = lambda k: 0.125 * ah[t] * (1.0 + t3h[k * LEV : (k + 1) * LEV, lanes])
        parts_here = [carried(k, r) for k in range(4)]
        raw = wo[r] * (fo[2, r] - to[r])
        ad[r - RIM] = (
            raw
            - (parts_here[0] + parts_here[1] + parts_here[2] + parts_here[3])
            + carried(0, r - 1)
            + carried(1, r + 1)
            + own_left(parts_here[2], halo(2), q)
            + own_right(parts_here[3], halo(3), q)
            + vo[r + 1, :LEV]
            + vo[r, LEV : 2 * LEV]
            + vo[r - 1, 2 * LEV :]
        )

    nothing = jnp.zeros((C, TILE), BF16)
    for r in range(RIM, RIM + h):
        e3, e2 = own_errors(0, r, wo[r] * ad[r - RIM], nothing)
        sum3 = sum3 + fold(e3)
        sum2 = sum2 + fold(e2)

    inner = slice(RIM * width, (RIM + h) * width)

    def shifted(ref, s):
        return jnp.concatenate(
            [ref[s, :, (RIM + a) * width : (RIM + a + h) * width] for a in (-1, 0, 1)], axis=0
        )

    g2 = [
        dot_nt(eo[1, C : 2 * C, inner], ho[1, :, (RIM + a) * width : (RIM + a + h) * width])
        + dot_nt(eo[0, C : 2 * C, inner], ho[0, :, (RIM + a) * width : (RIM + a + h) * width])
        for a in (-1, 0, 1)
    ]
    g3 = dot_nt(e3o[1], h2o[1]) + dot_nt(e3o[0], h2o[0])
    big = jnp.concatenate(g2 + [jnp.concatenate([g3, jnp.zeros((C - K, C), F32)], axis=0)], axis=1)
    chunk = grads_ref.shape[1]

    def spread_rows(ref, v):
        for y in range(n_gy):
            lo = y * chunk
            ref[y] = v[lo : lo + chunk] if lo + chunk <= C else jnp.zeros((chunk, v.shape[1]), F32)

    def to_peers(src, dst, send, recv, peers, key):
        return [
            pltpu.make_async_remote_copy(
                src_ref=src(k, p), dst_ref=dst(k, p), send_sem=send.at[k], recv_sem=recv.at[k],
                device_id=key(p), device_id_type=MESH,
            )
            for k, p in enumerate(peers)
        ]

    def begin(group):
        for copy in group:
            copy.start()
        return group

    along_y = lambda y: (gx, y)
    along_x = lambda x: (x, gy)
    spread_rows(grads_ref, big)
    one = begin(to_peers(
        lambda k, y: grads_ref.at[y], lambda k, y: got.at[k], send_one, recv_one, ys, along_y
    ))

    for t in range(tiles):
        owns = [
            eo[0, C : 2 * C, at(t + tiles * q)] if RIM <= t + tiles * q < RIM + h else None
            for q in range(SLOTS)
        ]
        eh[0, C : 2 * C, tile(t)] = nothing
        eh[0, :C, tile(t)] = halo_left(nothing, owns)
        eh[0, 2 * C :, tile(t)] = halo_right(nothing, owns)
    twist(eh, 0)
    for r in (RIM - 2, RIM - 1, RIM + h, RIM + h + 1):
        eo[0, :, at(r)] = jnp.zeros((3 * C, width), BF16)
    g1 = dot_nt(e1o[1, :, inner], shifted(xo, 1))
    for t, n in pieces:
        e1 = dot(w2t, stack_halo(eh, 0, t, n)) * p1h[0, :, t * TILE : (t + n) * TILE]
        sum1 = sum1 + fold(e1)
        g1 = g1 + dot_nt(e1.astype(BF16), stack_halo(xh, 0, t, n))
    for r in range(RIM - 1, RIM + h + 1):
        e1 = dot(w2t, stack_own(eo, 0, r)) * p1o[0, :, at(r)]
        sum1 = sum1 + fold(e1)
        e1o[0, :, at(r)] = e1.astype(BF16)
    ring = h + 2
    g1 = g1 + dot_nt(
        e1o[0, :, (RIM - 1) * width : (RIM + h + 1) * width],
        jnp.concatenate(
            [xo[0, :, (RIM - 1 + a) * width : (RIM - 1 + a + ring) * width] for a in (-1, 0, 1)], axis=0
        ),
    )
    total = lambda v: jnp.sum(v, axis=1, keepdims=True)
    tall = lambda v: jnp.concatenate([v, jnp.zeros((C - v.shape[0], 1), F32)], axis=0)
    extra = pad16(
        jnp.concatenate([g1, total(sum1), total(sum2), tall(total(sum3))], axis=1), TILE
    )
    spread_rows(extra_ref, extra)
    four = begin(to_peers(
        lambda k, y: extra_ref.at[y], lambda k, y: extra_got.at[k], send_four, recv_four, ys, along_y
    ))

    def gather_one(group, ref, arrived, here):
        acc = ref[gy]
        for k, copy in enumerate(group):
            copy.wait_recv()
            acc = acc + arrived[k]
        here[...] = acc
        return acc

    def gather_two(group, ref, acc, to_send, out):
        ref[gx] = acc
        for copy in group:
            copy.wait_recv()
        acc = ref[0]
        for x in range(1, n_gx):
            acc = acc + ref[x]
        acc = acc.astype(BF16)
        to_send[...] = acc
        out[gy] = acc

    acc_big = gather_one(one, grads_ref, got, part)
    two = begin(to_peers(
        lambda k, x: part, lambda k, x: parts.at[gx], send_two, recv_two, xs, along_x
    ))
    acc_extra = gather_one(four, extra_ref, extra_got, extra_part)
    five = begin(to_peers(
        lambda k, x: extra_part, lambda k, x: extra_parts.at[gx], send_five, recv_five, xs, along_x
    ))
    gather_two(two, parts, acc_big, mine, out_ref)
    three = begin(to_peers(
        lambda k, y: mine, lambda k, y: out_ref.at[gy], send_three, recv_three, ys, along_y
    ))
    gather_two(five, extra_parts, acc_extra, extra_mine, rest_ref)
    six = begin(to_peers(
        lambda k, y: extra_mine, lambda k, y: rest_ref.at[gy], send_six, recv_six, ys, along_y
    ))
    for copy in three + six:
        copy.wait_recv()
    for dx, dy, group in copies:
        @pl.when(exists(dx, dy))
        def _():
            for copy in group:
                copy.wait_send()
    for copy in one + two + three + four + five + six:
        copy.wait_send()


def finish_kernel(grads, rest, final, d1, d2, d3, ids, final_out, u1, u2, u3):
    final_out[...] = final[...]
    n_parts = C // grads.shape[1]
    big = jnp.concatenate([grads[y].astype(F32) for y in range(n_parts)], axis=0)
    side = jnp.concatenate([rest[y].astype(F32) for y in range(n_parts)], axis=0)
    one = jnp.concatenate(
        [side[:, 4 * LEV * a : 4 * LEV * a + 3 * LEV] for a in range(3)]
        + [side[:, 12 * LEV : 12 * LEV + 1]],
        axis=1,
    )
    two = jnp.concatenate([big[:, : 9 * C], side[:, 12 * LEV + 1 : 12 * LEV + 2]], axis=1)
    three = jnp.concatenate(
        [big[:K, 9 * C : 10 * C], side[:K, 12 * LEV + 2 : 12 * LEV + 3]], axis=1
    )
    members = [one, two, three]
    heads = [d1[...], d2[...], d3[...]]
    row_sq = lambda v: jnp.sum(v * v, axis=1, keepdims=True)
    grad_rows = jnp.concatenate([row_sq(m) for m in members], axis=0)
    dir_rows = jnp.concatenate([row_sq(m) for m in heads], axis=0)
    total = jnp.sum(grad_rows, axis=0, keepdims=True)
    factor = 1.0 / jnp.maximum(jnp.sqrt(total), 1.0)
    clip_rows = grad_rows * (factor * factor)
    count = grad_rows.shape[0]
    i0 = lax.broadcasted_iota(jnp.int32, (count, count), 0)
    i1 = lax.broadcasted_iota(jnp.int32, (count, count), 1)
    spread = jnp.broadcast_to(ids[...].astype(F32), (count, count))
    column = jnp.sum(jnp.where(i0 == i1, spread, 0.0), axis=1, keepdims=True)
    row_ratio = jnp.zeros((count, 1), F32)
    for k in range(GROUPS):
        hit = column == float(k)
        pick = lambda v: jnp.sum(jnp.where(hit, v, 0.0), axis=0, keepdims=True)
        ratio = jnp.sqrt(pick(clip_rows)) / jnp.sqrt(pick(dir_rows) + 1e-06)
        row_ratio = row_ratio + jnp.where(hit, ratio, 0.0)
    scaling = math.sqrt(PARAMS)
    start = 0
    for ref, member, head in zip((u1, u2, u3), members, heads):
        n = member.shape[0]
        ref[...] = scaling * (member * factor + row_ratio[start : start + n] * head)
        start += n


def per_device(sizes, field, target, mask, conv_one, conv_two, head, d1, d2, d3, ids):
    n_gx, n_gy = sizes
    _, h, width = field.shape
    rows = h + 2 * RIM
    tiles = rows // SLOTS
    flat = rows * width
    edge = (tiles + 2) * TILE
    shape = jax.ShapeDtypeStruct
    chunk = 8 * -(-C // (8 * n_gy))
    wide = 10 * C
    dma = pltpu.SemaphoreType.DMA
    vmem = pltpu.VMEM
    over_y = [dma((n_gy - 1,)), dma((n_gy - 1,))]
    over_x = [dma((n_gx - 1,)), dma((n_gx - 1,))]

    def sums(columns):
        return [
            vmem((n_gy, chunk, columns), F32),
            vmem((n_gy - 1, chunk, columns), F32),
            vmem((chunk, columns), F32),
            vmem((n_gx, chunk, columns), F32),
            vmem((chunk, columns), BF16),
        ]

    final, summed, rest = pl.pallas_call(
        functools.partial(fused_kernel, sizes),
        name="fused",
        out_shape=[
            shape(field.shape, F32),
            shape((n_gy, chunk, wide), BF16),
            shape((n_gy, chunk, TILE), BF16),
        ],
        in_specs=[ANY] * 6,
        out_specs=[VM] * 3,
        scratch_shapes=[
            vmem((3, rows, LEV, width), F32),
            vmem((3, LEV, edge), F32),
            vmem((2, rows, LEV, width), F32),
            vmem((2, rows, LEV, width), F32),
            vmem((2, tiles, LEV, TILE), F32),
            vmem((2, tiles, LEV, TILE), F32),
            vmem((rows, LEV, width), F32),
            vmem((tiles, LEV, TILE), F32),
            vmem((rows, LEV, width), F32),
            vmem((tiles, LEV, TILE), F32),
            vmem((rows, LEV, width), F32),
            vmem((tiles, LEV, TILE), F32),
            vmem((h, LEV, width), F32),
            vmem((2, 4 * LEV, flat), BF16),
            vmem((2, 4 * LEV, edge), BF16),
            vmem((2, 3 * C, flat), BF16),
            vmem((2, 3 * C, edge), BF16),
            vmem((2, C, flat), F32),
            vmem((2, C, tiles * TILE), F32),
            vmem((2, C, flat), F32),
            vmem((C, tiles * TILE), F32),
            vmem((2, K, flat), F32),
            vmem((K, tiles * TILE), F32),
            vmem((2, C, h * width), BF16),
            vmem((2, 3 * C, flat), BF16),
            vmem((2, 3 * C, edge), BF16),
            vmem((2, K, h * width), BF16),
            vmem((2, C, flat), BF16),
            vmem((C, tiles * TILE), BF16),
            vmem((rows, 3 * LEV, width), F32),
            vmem(field.shape, F32),
            vmem(target.shape, F32),
            vmem(mask.shape, jnp.int32),
            vmem(conv_one.shape, F32),
            vmem(conv_two.shape, F32),
            vmem(head.shape, F32),
            vmem((3, h, width), F32),
            vmem((3, 3 * LEV, TILE), F32),
            vmem((3, 3 * LEV, TILE), F32),
            vmem((2, 3 * LEV, TILE), F32),
        ]
        + sums(wide)
        + sums(TILE)
        + [dma((6,)), dma((12,)), dma((12,))]
        + over_y + over_x + over_y
        + over_y + over_x + over_y,
        compiler_params=pltpu.CompilerParams(
            collective_id=0, has_side_effects=True, vmem_limit_bytes=LIMIT
        ),
    )(field, target, mask, conv_one, conv_two, head)
    final, u1, u2, u3 = pl.pallas_call(
        finish_kernel,
        name="update",
        out_shape=[
            shape(field.shape, F32),
            shape(conv_one.shape, F32), shape(conv_two.shape, F32), shape(head.shape, F32),
        ],
        in_specs=[VM] * 7,
        out_specs=[VM] * 4,
    )(summed, rest, final, d1, d2, d3, ids.reshape(1, -1))
    return final, u1, u2, u3


def solution(mesh):
    grid = P(None, "gx", "gy")
    placed = (grid, grid, P("gx", "gy")) + (P(),) * 7
    return jax.shard_map(
        functools.partial(per_device, (mesh.shape["gx"], mesh.shape["gy"])),
        mesh=mesh,
        in_specs=placed,
        out_specs=(grid, P(), P(), P()),
        check_vma=False,
    )
```

```python
import functools
import math

import jax
import jax.numpy as jnp
from jax import lax
from jax.experimental import pallas as pl
from jax.experimental.pallas import tpu as pltpu
from jax.sharding import PartitionSpec as P

GROUPS = 6
PARAMS = 43680
RIM = 6
NEAR = 2
LEV = 8
C = 64
K = 32
TILE = 128
SLOTS = 4
SLOT = TILE // SLOTS
MESH = pl.DeviceIdType.MESH
F32 = jnp.float32
BF16 = jnp.bfloat16
VM = pl.BlockSpec(memory_space=pltpu.VMEM)
ANY = pl.BlockSpec(memory_space=pl.ANY)
LIMIT = 56 * 1024 * 1024
NT = (((1,), (1,)), ((), ()))


def dot(a, b):
    return jnp.dot(a, b, preferred_element_type=F32)


def dot_nt(a, b):
    return lax.dot_general(a, b, NT, preferred_element_type=F32)


def sigmoid(v):
    return 0.5 * jnp.tanh(0.5 * v) + 0.5


def roll(v, shift):
    return pltpu.roll(v, shift % v.shape[1], 1)


def fused_kernel(
    sizes, field_in, target_in, mask_in, w1_in, w2_in, w3_in,
    final_ref, out_ref, rest_ref,
    fo, fh, fl, fr, flh, frh, wo, wh, to, th, ao, ah, ad,
    xo, xh, ho, hh, p1o, p1h, p2o, p2h, t3o, t3h, h2o, eo, eh, e3o, e1o, e1h, vo, acc2, acc1, acc3,
    field, target, mask, w1_ref, w2_ref, w3_ref, wet, left, right, packed,
    grads_ref, got, part, parts, mine, extra_ref, extra_got, extra_part, extra_parts, extra_mine,
    load_sem, send_sem, recv_sem, send_one, recv_one, send_two, recv_two, send_three, recv_three,
    send_four, recv_four, send_five, recv_five, send_six, recv_six,
):
    n_gx, n_gy = sizes
    gx = lax.axis_index("gx")
    gy = lax.axis_index("gy")
    h, width = mask.shape
    rows = h + 2 * RIM
    tiles = rows // SLOTS
    ys = [lax.rem(gy + k, n_gy) for k in range(1, n_gy)]
    xs = [lax.rem(gx + k, n_gx) for k in range(1, n_gx)]
    moves = [(dx, dy) for dx in (-1, 0, 1) for dy in (-1, 0, 1) if (dx, dy) != (0, 0)]

    def exists(dx, dy):
        x = gx + dx
        y = gy + dy
        return (x >= 0) & (x < n_gx) & (y >= 0) & (y < n_gy)

    barrier = pltpu.get_barrier_semaphore()
    count = jnp.int32(n_gy + n_gx - 2)
    for dx, dy in moves:
        if dx and dy:
            @pl.when(exists(dx, dy))
            def _():
                pl.semaphore_signal(barrier, inc=1, device_id=(gx + dx, gy + dy), device_id_type=MESH)
            count = count + jnp.where(exists(dx, dy), 1, 0)
    for x in xs:
        pl.semaphore_signal(barrier, inc=1, device_id=(x, gy), device_id_type=MESH)
    for y in ys:
        pl.semaphore_signal(barrier, inc=1, device_id=(gx, y), device_id_type=MESH)

    loads = [
        pltpu.make_async_copy(src, dst, load_sem.at[i])
        for i, (src, dst) in enumerate(
            [(field_in, field), (target_in, target), (mask_in, mask),
             (w1_in, w1_ref), (w2_in, w2_ref), (w3_in, w3_ref)]
        )
    ]
    for copy in loads:
        copy.start()

    def pairs(dx, dy):
        if dy:
            side = left if dy > 0 else right
            return [(packed.at[0 if dy > 0 else 1], side.at[1 - dx])]
        if dx > 0:
            return [
                (fo.at[0, pl.ds(h, RIM)], fo.at[0, pl.ds(0, RIM)]),
                (to.at[pl.ds(RIM + h - NEAR, NEAR)], to.at[pl.ds(RIM - NEAR, NEAR)]),
                (wet.at[1], wet.at[0]),
            ]
        return [
            (fo.at[0, pl.ds(RIM, RIM)], fo.at[0, pl.ds(RIM + h, RIM)]),
            (to.at[pl.ds(RIM, NEAR)], to.at[pl.ds(RIM + h, NEAR)]),
            (wet.at[1], wet.at[2]),
        ]

    for dx, dy in moves:
        @pl.when(jnp.logical_not(exists(-dx, -dy)))
        def _():
            for _, dst in pairs(dx, dy):
                dst[...] = jnp.zeros(dst.shape, F32)

    for copy in loads[:3]:
        copy.wait()
    lane = lax.broadcasted_iota(jnp.int32, (3 * LEV, TILE), 1)
    strips = [jnp.zeros((3 * LEV, TILE), F32) for _ in range(2)]
    for r in range(h):
        wide_wet = jnp.broadcast_to(mask[r : r + 1, :].astype(F32), (LEV, width))
        values = wide_wet * field[:, r, :]
        goal = target[:, r, :]
        fo[0, RIM + r] = values
        to[RIM + r] = goal
        mixed = jnp.concatenate([values, wide_wet, goal], axis=0)
        here = (lane >= LEV * r) & (lane < LEV * r + LEV)
        low = mixed[:, :TILE]
        high = mixed[:, width - TILE :]
        strips[0] = jnp.where(here, roll(high, LEV * r + LEV), strips[0])
        strips[1] = jnp.where(here, roll(low, LEV * r), strips[1])
    wet[1] = mask[...].astype(F32)
    packed[0] = strips[0]
    packed[1] = strips[1]

    pl.semaphore_wait(barrier, count)

    copies = []
    index = 0
    for dx, dy in moves:
        group = []
        for src, dst in pairs(dx, dy):
            group.append(
                pltpu.make_async_remote_copy(
                    src_ref=src,
                    dst_ref=dst,
                    send_sem=send_sem.at[index],
                    recv_sem=recv_sem.at[index],
                    device_id=(gx + dx, gy + dy),
                    device_id_type=MESH,
                )
            )
            index += 1
        copies.append((dx, dy, group))
    for dx, dy, group in copies:
        @pl.when(exists(dx, dy))
        def _():
            for copy in group:
                copy.start()

    for copy in loads[3:]:
        copy.wait()
    def pipeline(stages, start, stop):
        last = max(lag for lag, _, _, _ in stages)
        for i in range(start, stop + last):
            for lag, low, high, stage in stages:
                if low <= i - lag < high:
                    stage(i - lag)

    slot_lane = lax.broadcasted_iota(jnp.int32, (1, TILE), 1) % SLOT
    slot_row = lax.broadcasted_iota(jnp.int32, (1, TILE), 1) // SLOT * tiles
    lane1 = lax.broadcasted_iota(jnp.int32, (1, TILE), 1)

    def pad16(v, n):
        return jnp.concatenate([v, jnp.zeros((v.shape[0], n - v.shape[1]), F32)], axis=1)

    def thirds(b):
        high = b.astype(BF16).astype(F32)
        low = b - high
        middle = low.astype(BF16).astype(F32)
        return jnp.concatenate([high, middle, low - middle], axis=1)

    wa = 0.5 * w1_ref[...]
    wb = 0.5 * w2_ref[...]
    wc = 0.5 * w3_ref[...]
    none = jnp.zeros((C, LEV), F32)
    w1 = jnp.concatenate(
        [
            wa[:, : 3 * LEV], none,
            wa[:, 3 * LEV : 6 * LEV], pad16(thirds(wa[:, 9 * LEV :]), LEV),
            wa[:, 6 * LEV : 9 * LEV], none,
        ],
        axis=1,
    ).astype(BF16)
    w2 = jnp.concatenate([wb[:, : 9 * C], pad16(thirds(wb[:, 9 * C :]), 16)], axis=1).astype(BF16)
    w3 = jnp.concatenate([wc[:, :C], pad16(thirds(wc[:, C:]), 16)], axis=1).astype(BF16)
    w3t = wc[:, :C].T.astype(BF16)
    flip = wb[:, : 9 * C].T
    w2t = jnp.concatenate([flip[k * C : (k + 1) * C] for k in range(8, -1, -1)], axis=1).astype(BF16)
    turn = (2.0 * wa[:, : 9 * LEV]).T
    w1t = jnp.concatenate(
        [
            jnp.concatenate(
                [turn[(3 * a + b) * LEV : (3 * a + b + 1) * LEV] for b in (2, 1, 0)], axis=1
            )
            for a in range(3)
        ],
        axis=0,
    ).astype(BF16)
    ones = jnp.ones((16, width), BF16)
    unit = jnp.ones((LEV, width), F32)

    first_lane = lane1 == 0
    last_lane = lane1 == TILE - 1

    def own_left(own, halo, q):
        r0 = roll(own[:, :TILE], 1)
        r1 = roll(own[:, TILE:], 1)
        rh = roll(halo, 1 - SLOT * (q + 1))
        return jnp.concatenate([jnp.where(first_lane, rh, r0), jnp.where(first_lane, r0, r1)], axis=1)

    def own_right(own, halo, q):
        r0 = roll(own[:, :TILE], -1)
        r1 = roll(own[:, TILE:], -1)
        rh = roll(halo, TILE - 1 - SLOT * q)
        return jnp.concatenate([jnp.where(last_lane, r1, r0), jnp.where(last_lane, rh, r1)], axis=1)

    def halo_left(halo, owns):
        out = roll(halo, 1)
        for q, own in enumerate(owns):
            if own is not None:
                out = jnp.where(lane1 == SLOT * q, roll(own[:, TILE:], 1 + SLOT * q), out)
        return out

    def halo_right(halo, owns):
        out = roll(halo, -1)
        for q, own in enumerate(owns):
            if own is not None:
                out = jnp.where(lane1 == SLOT * q + SLOT - 1, roll(own[:, :TILE], SLOT * q + SLOT - 1), out)
        return out

    def at(r):
        return slice(r * width, (r + 1) * width)

    def tile(t, n=1):
        return slice((t + 1) * TILE, (t + 1 + n) * TILE)

    def twist(ref, s):
        ref[s, :, tile(-1)] = roll(ref[s, :, tile(tiles - 1)], SLOT)
        ref[s, :, tile(tiles)] = roll(ref[s, :, tile(0)], -SLOT)

    def stack_own(ref, s, r, *more):
        return jnp.concatenate([ref[s, :, at(r + a)] for a in (-1, 0, 1)] + list(more), axis=0)

    def stack_halo(ref, s, t, n, *more):
        return jnp.concatenate([ref[s, :, tile(t + a, n)] for a in (-1, 0, 1)] + list(more), axis=0)

    pieces = [(t, min(2, tiles - t)) for t in range(0, tiles, 2)]
    up_ok = jnp.where(gx > 0, 1.0, 0.0).astype(F32)
    down_ok = jnp.where(gx < n_gx - 1, 1.0, 0.0).astype(F32)
    left_ok = jnp.where(gy > 0, 1.0, 0.0).astype(F32)
    right_ok = jnp.where(gy < n_gy - 1, 1.0, 0.0).astype(F32)

    def inside_halo(t):
        r = slot_row + t
        side = jnp.where(slot_lane < SLOT // 2, right_ok, left_ok)
        return side * jnp.where(r < RIM, up_ok, jnp.where(r >= RIM + h, down_ok, 1.0))

    def inside_own(v, r):
        return v * up_ok if r < RIM else v * down_ok if r >= RIM + h else v

    in_halo = [inside_halo(t) for t in range(tiles)]

    def halo_mask(t, n):
        return jnp.concatenate(in_halo[t : t + n], axis=1)

    for dx, dy, group in copies:
        @pl.when(exists(-dx, -dy))
        def _():
            for copy in group:
                copy.wait_recv()

    for t in range(tiles):
        side_tile = jnp.zeros((3 * LEV, TILE), F32)
        for q in range(SLOTS):
            r = t + tiles * q
            where = 0 if r < RIM else 1 if r < RIM + h else 2
            k = (r + h - RIM) % h
            is_right = (lane1 >= SLOT * q) & (lane1 < SLOT * q + LEV)
            is_left = (lane1 >= SLOT * q + SLOT - LEV) & (lane1 < SLOT * q + SLOT)
            side_tile = jnp.where(is_right, roll(right[where], SLOT * q - LEV * k), side_tile)
            side_tile = jnp.where(
                is_left, roll(left[where], SLOT * q + SLOT - LEV - LEV * k), side_tile
            )
        fh[0, :, tile(t)] = side_tile[:LEV]
        wh[t] = side_tile[LEV : 2 * LEV]
        th[t] = side_tile[2 * LEV :]
    twist(fh, 0)
    for r in range(rows):
        where = 0 if r < RIM else 1 if r < RIM + h else 2
        k = (r + h - RIM) % h
        wo[r] = jnp.broadcast_to(wet[where, k : k + 1, :], (LEV, width))

    def activate(u):
        t = jnp.tanh(u)
        ut = u * t
        return u + ut, (1.0 + t) * (1.0 + u - ut)

    def forward(s, rad):
        low, high = (0, rows - 1) if s == 0 else (RIM - 4, RIM + h + 3)
        near = lambda r: min(max(r, low), high)
        for t in range(tiles):
            halo = fh[s, :, tile(t)]
            owns = [fo[s, near(t + tiles * q)] for q in range(SLOTS)]
            before = halo_left(halo, owns)
            after = halo_right(halo, owns)
            flh[s, t] = before
            frh[s, t] = after
            xh[s, :, tile(t)] = jnp.concatenate(
                [before, halo, after, unit[:, :TILE]], axis=0
            ).astype(BF16)
        twist(xh, s)
        for t, n in pieces:
            hid, slope = activate(dot(w1, stack_halo(xh, s, t, n)))
            ok = halo_mask(t, n)
            p1h[s, :, t * TILE : (t + n) * TILE] = slope * ok
            hh[s, C : 2 * C, tile(t, n)] = (hid * ok).astype(BF16)
        def logits(hid, n):
            return dot(w3, jnp.concatenate([hid, ones[:, :n]], axis=0))

        def change(t3, center, others):
            total = 0.0
            for k, other in enumerate(others):
                total = total + (1.0 + t3[k * LEV : (k + 1) * LEV]) * (other - center)
            return total

        first_u, second_u, third_u = {}, {}, {}
        top, bottom = RIM - rad, RIM + h + rad

        def stack_x(r):
            own = fo[s, r]
            halo = fh[s, :, tile(r % tiles)]
            before = own_left(own, halo, r // tiles)
            after = own_right(own, halo, r // tiles)
            fl[s, r] = before
            fr[s, r] = after
            xo[s, :, at(r)] = jnp.concatenate([before, own, after, unit], axis=0).astype(BF16)

        def dot_first(r):
            first_u[r] = dot(w1, stack_own(xo, s, r))

        def stack_h(r):
            hid, slope = activate(first_u.pop(r))
            if RIM - 1 <= r < RIM + h + 1:
                p1o[s, :, at(r)] = inside_own(slope, r)
            hid = inside_own(hid, r).astype(BF16)
            halo = hh[s, C : 2 * C, tile(r % tiles)]
            ho[s, :, at(r)] = jnp.concatenate(
                [own_left(hid, halo, r // tiles), hid, own_right(hid, halo, r // tiles)], axis=0
            )

        def dot_second(r):
            second_u[r] = dot(w2, stack_own(ho, s, r, ones))

        def dot_third(r):
            hid, slope = activate(second_u.pop(r))
            hid = hid.astype(BF16)
            mine_row = RIM <= r < RIM + h
            if s == 1 or mine_row:
                p2o[s, :, at(r)] = slope
            if mine_row:
                h2o[s, :, at(r - RIM)] = hid
            third_u[r] = logits(hid, width)

        def advance(r):
            t3 = jnp.tanh(third_u.pop(r))
            if s == 1 or RIM <= r < RIM + h:
                t3o[s, :, at(r)] = t3
            center = fo[s, r]
            fo[s + 1, r] = center + 0.125 * wo[r] * change(
                t3, center, [fo[s, r + 1], fo[s, r - 1], fr[s, r], fl[s, r]]
            )

        def halo_h(t):
            halo = hh[s, C : 2 * C, tile(t)]
            owns = [
                ho[s, C : 2 * C, at(t + tiles * q)] if top - 1 <= t + tiles * q <= bottom else None
                for q in range(SLOTS)
            ]
            hh[s, :C, tile(t)] = halo_left(halo, owns)
            hh[s, 2 * C :, tile(t)] = halo_right(halo, owns)

        pipeline(
            [
                (0, top - 2, bottom + 2, stack_x),
                (2, top - 1, bottom + 1, dot_first),
                (3, top - 1, bottom + 1, stack_h),
                (5, top, bottom, dot_second),
                (6, top, bottom, dot_third),
                (7, top, bottom, advance),
            ],
            top - 2, bottom + 2,
        )
        for t in range(tiles):
            halo_h(t)
        twist(hh, s)

        def halo_second(i):
            t, n = pieces[i]
            second_u[i] = dot(w2, stack_halo(hh, s, t, n, ones[:, : n * TILE]))

        def halo_third(i):
            t, n = pieces[i]
            hid, slope = activate(second_u.pop(i))
            if s == 1:
                p2h[:, t * TILE : (t + n) * TILE] = slope
            third_u[i] = logits(hid.astype(BF16), n * TILE)

        def halo_advance(i):
            t, n = pieces[i]
            t3 = jnp.tanh(third_u.pop(i))
            if s == 1:
                t3h[:, t * TILE : (t + n) * TILE] = t3
            for i in range(n):
                center = fh[s, :, tile(t + i)]
                fh[s + 1, :, tile(t + i)] = center + 0.125 * wh[t + i] * change(
                    t3[:, i * TILE : (i + 1) * TILE], center,
                    [fh[s, :, tile(t + i + 1)], fh[s, :, tile(t + i - 1)], frh[s, t + i], flh[s, t + i]],
                )

        count = len(pieces)
        pipeline(
            [(0, 0, count, halo_second), (1, 0, count, halo_third), (2, 0, count, halo_advance)],
            0, count,
        )
        twist(fh, s + 1)

    forward(0, 4)
    forward(1, 2)
    for r in range(h):
        final_ref[:, r, :] = fo[2, RIM + r]

    fold = lambda v: sum(v[:, k * TILE : (k + 1) * TILE] for k in range(v.shape[1] // TILE))

    for r in range(RIM - 2, RIM + h + 2):
        ao[r] = wo[r] * (fo[2, r] - to[r])
    for t in range(tiles):
        ah[t] = wh[t] * (fh[2, :, tile(t)] - th[t])

    def errors(scaled, t3, center, others):
        e3 = jnp.concatenate([scaled * (other - center) for other in others], axis=0) * (1.0 - t3 * t3)
        return e3, e3.astype(BF16)

    sums = {
        3: jnp.zeros((K, TILE), F32), 2: jnp.zeros((C, TILE), F32), 1: jnp.zeros((C, TILE), F32)
    }
    own_rows = range(RIM, RIM + h)
    back, raw_one = {}, {}

    def dot_errors(s, r):
        wg = ao[r] if s else wo[r] * ad[r - RIM]
        e3, e3b = errors(
            wg * 0.0625, t3o[s, :, at(r)], fo[s, r], [fo[s, r + 1], fo[s, r - 1], fr[s, r], fl[s, r]]
        )
        back[r] = dot(w3t, e3b)
        if r in own_rows:
            e3o[s, :, at(r - RIM)] = e3b
            sums[3] = sums[3] + fold(e3)

    def stack_errors(s, r, halo):
        e2 = back.pop(r) * p2o[s, :, at(r)]
        e2b = e2.astype(BF16)
        eo[s, :, at(r)] = jnp.concatenate(
            [own_left(e2b, halo, r // tiles), e2b, own_right(e2b, halo, r // tiles)], axis=0
        )
        if r in own_rows:
            sums[2] = sums[2] + fold(e2)

    def dot_back(s, r):
        raw_one[r] = dot(w2t, stack_own(eo, s, r))

    def keep_one(s, r):
        e1 = raw_one.pop(r) * p1o[s, :, at(r)]
        e1o[s, :, at(r)] = e1.astype(BF16)
        if s == 0 or r in own_rows:
            sums[1] = sums[1] + fold(e1)

    for t in range(tiles):
        lanes = slice(t * TILE, (t + 1) * TILE)
        _, e3b = errors(
            ah[t] * 0.0625, t3h[:, lanes], fh[1, :, tile(t)],
            [fh[1, :, tile(t + 1)], fh[1, :, tile(t - 1)], frh[1, t], flh[1, t]],
        )
        eh[1, C : 2 * C, tile(t)] = (dot(w3t, e3b) * p2h[:, lanes]).astype(BF16)
    top, bottom = RIM - 2, RIM + h + 2
    pipeline(
        [
            (0, top, bottom, lambda r: dot_errors(1, r)),
            (1, top, bottom, lambda r: stack_errors(1, r, eh[1, C : 2 * C, tile(r % tiles)])),
            (3, top + 1, bottom - 1, lambda r: dot_back(1, r)),
            (4, top + 1, bottom - 1, lambda r: keep_one(1, r)),
        ],
        top, bottom,
    )
    for t in range(tiles):
        halo = eh[1, C : 2 * C, tile(t)]
        owns = [
            eo[1, C : 2 * C, at(t + tiles * q)] if top <= t + tiles * q < bottom else None
            for q in range(SLOTS)
        ]
        eh[1, :C, tile(t)] = halo_left(halo, owns)
        eh[1, 2 * C :, tile(t)] = halo_right(halo, owns)
    twist(eh, 1)
    for t, n in pieces:
        e1 = dot(w2t, stack_halo(eh, 1, t, n)) * p1h[1, :, t * TILE : (t + n) * TILE]
        e1h[:, t * TILE : (t + n) * TILE] = e1.astype(BF16)

    inner = slice(RIM * width, (RIM + h) * width)

    def shifted(ref, s):
        return jnp.concatenate(
            [ref[s, :, (RIM + a) * width : (RIM + a + h) * width] for a in (-1, 0, 1)], axis=0
        )

    def grad_two(s, a):
        return dot_nt(eo[s, C : 2 * C, inner], ho[s, :, (RIM + a) * width : (RIM + a + h) * width])

    def carry_field(r):
        t = r % tiles
        e1b = e1o[1, :, at(r)]
        halo = e1h[:, t * TILE : (t + 1) * TILE]
        vo[r] = dot(
            w1t,
            jnp.concatenate(
                [own_left(e1b, halo, r // tiles), e1b, own_right(e1b, halo, r // tiles)], axis=0
            ),
        )

    def carried(k, r):
        return 0.125 * ao[r] * (1.0 + t3o[1, k * LEV : (k + 1) * LEV, at(r)])

    def adjoint(r):
        t, q = r % tiles, r // tiles
        lanes = slice(t * TILE, (t + 1) * TILE)
        halo = lambda k: 0.125 * ah[t] * (1.0 + t3h[k * LEV : (k + 1) * LEV, lanes])
        parts_here = [carried(k, r) for k in range(4)]
        ad[r - RIM] = (
            ao[r]
            - (parts_here[0] + parts_here[1] + parts_here[2] + parts_here[3])
            + carried(0, r - 1)
            + carried(1, r + 1)
            + own_left(parts_here[2], halo(2), q)
            + own_right(parts_here[3], halo(3), q)
            + vo[r + 1, :LEV]
            + vo[r, LEV : 2 * LEV]
            + vo[r - 1, 2 * LEV :]
        )

    def early(i):
        if i < 3:
            acc2[i] = grad_two(1, i - 1)
        elif i == 3:
            acc1[...] = dot_nt(e1o[1, :, inner], shifted(xo, 1))
        else:
            acc3[...] = dot_nt(e3o[1], h2o[1])

    nothing = jnp.zeros((C, TILE), BF16)
    low, high = RIM, RIM + h
    pipeline(
        [
            (0, low - 1, high + 1, carry_field),
            (2, low, high, adjoint),
            (3, low, high, lambda r: dot_errors(0, r)),
            (4, low, high, lambda r: stack_errors(0, r, nothing)),
            (low, 0, 5, early),
        ],
        low - 1, high + 1,
    )

    g2 = [acc2[a] + grad_two(0, a - 1) for a in range(3)]
    g3 = acc3[...] + dot_nt(e3o[0], h2o[0])
    big = jnp.concatenate(g2 + [jnp.concatenate([g3, jnp.zeros((C - K, C), F32)], axis=0)], axis=1)
    chunk = grads_ref.shape[1]

    def spread_rows(ref, v):
        for y in range(n_gy):
            lo = y * chunk
            ref[y] = v[lo : lo + chunk] if lo + chunk <= C else jnp.zeros((chunk, v.shape[1]), F32)

    def to_peers(src, dst, send, recv, peers, key):
        return [
            pltpu.make_async_remote_copy(
                src_ref=src(k, p), dst_ref=dst(k, p), send_sem=send.at[k], recv_sem=recv.at[k],
                device_id=key(p), device_id_type=MESH,
            )
            for k, p in enumerate(peers)
        ]

    def begin(group):
        for copy in group:
            copy.start()
        return group

    along_y = lambda y: (gx, y)
    along_x = lambda x: (x, gy)
    spread_rows(grads_ref, big)
    one = begin(to_peers(
        lambda k, y: grads_ref.at[y], lambda k, y: got.at[k], send_one, recv_one, ys, along_y
    ))

    for t in range(tiles):
        owns = [
            eo[0, C : 2 * C, at(t + tiles * q)] if RIM <= t + tiles * q < RIM + h else None
            for q in range(SLOTS)
        ]
        eh[0, C : 2 * C, tile(t)] = nothing
        eh[0, :C, tile(t)] = halo_left(nothing, owns)
        eh[0, 2 * C :, tile(t)] = halo_right(nothing, owns)
    twist(eh, 0)
    for r in (RIM - 2, RIM - 1, RIM + h, RIM + h + 1):
        eo[0, :, at(r)] = jnp.zeros((3 * C, width), BF16)
    g1 = acc1[...]
    for t, n in pieces:
        e1 = dot(w2t, stack_halo(eh, 0, t, n)) * p1h[0, :, t * TILE : (t + n) * TILE]
        sums[1] = sums[1] + fold(e1)
        g1 = g1 + dot_nt(e1.astype(BF16), stack_halo(xh, 0, t, n))
    pipeline(
        [
            (0, low - 1, high + 1, lambda r: dot_back(0, r)),
            (1, low - 1, high + 1, lambda r: keep_one(0, r)),
        ],
        low - 1, high + 1,
    )
    ring = h + 2
    g1 = g1 + dot_nt(
        e1o[0, :, (RIM - 1) * width : (RIM + h + 1) * width],
        jnp.concatenate(
            [xo[0, :, (RIM - 1 + a) * width : (RIM - 1 + a + ring) * width] for a in (-1, 0, 1)], axis=0
        ),
    )
    total = lambda v: jnp.sum(v, axis=1, keepdims=True)
    tall = lambda v: jnp.concatenate([v, jnp.zeros((C - v.shape[0], 1), F32)], axis=0)
    extra = pad16(
        jnp.concatenate([g1, total(sums[1]), total(sums[2]), tall(total(sums[3]))], axis=1), TILE
    )
    spread_rows(extra_ref, extra)
    four = begin(to_peers(
        lambda k, y: extra_ref.at[y], lambda k, y: extra_got.at[k], send_four, recv_four, ys, along_y
    ))

    def gather_one(group, ref, arrived, here):
        acc = ref[gy]
        for k, copy in enumerate(group):
            copy.wait_recv()
            acc = acc + arrived[k]
        here[...] = acc
        return acc

    def gather_two(group, ref, acc, to_send, out):
        ref[gx] = acc
        for copy in group:
            copy.wait_recv()
        acc = ref[0]
        for x in range(1, n_gx):
            acc = acc + ref[x]
        acc = acc.astype(BF16)
        to_send[...] = acc
        out[gy] = acc

    acc_big = gather_one(one, grads_ref, got, part)
    two = begin(to_peers(
        lambda k, x: part, lambda k, x: parts.at[gx], send_two, recv_two, xs, along_x
    ))
    acc_extra = gather_one(four, extra_ref, extra_got, extra_part)
    five = begin(to_peers(
        lambda k, x: extra_part, lambda k, x: extra_parts.at[gx], send_five, recv_five, xs, along_x
    ))
    gather_two(two, parts, acc_big, mine, out_ref)
    three = begin(to_peers(
        lambda k, y: mine, lambda k, y: out_ref.at[gy], send_three, recv_three, ys, along_y
    ))
    gather_two(five, extra_parts, acc_extra, extra_mine, rest_ref)
    six = begin(to_peers(
        lambda k, y: extra_mine, lambda k, y: rest_ref.at[gy], send_six, recv_six, ys, along_y
    ))
    for copy in three + six:
        copy.wait_recv()
    for dx, dy, group in copies:
        @pl.when(exists(dx, dy))
        def _():
            for copy in group:
                copy.wait_send()
    for copy in one + two + three + four + five + six:
        copy.wait_send()


def finish_kernel(grads, rest, final, d1, d2, d3, ids, final_out, u1, u2, u3):
    final_out[...] = final[...]
    n_parts = C // grads.shape[1]
    big = jnp.concatenate([grads[y].astype(F32) for y in range(n_parts)], axis=0)
    side = jnp.concatenate([rest[y].astype(F32) for y in range(n_parts)], axis=0)
    one = jnp.concatenate(
        [side[:, 4 * LEV * a : 4 * LEV * a + 3 * LEV] for a in range(3)]
        + [side[:, 12 * LEV : 12 * LEV + 1]],
        axis=1,
    )
    two = jnp.concatenate([big[:, : 9 * C], side[:, 12 * LEV + 1 : 12 * LEV + 2]], axis=1)
    three = jnp.concatenate(
        [big[:K, 9 * C : 10 * C], side[:K, 12 * LEV + 2 : 12 * LEV + 3]], axis=1
    )
    members = [one, two, three]
    heads = [d1[...], d2[...], d3[...]]
    row_sq = lambda v: jnp.sum(v * v, axis=1, keepdims=True)
    grad_rows = jnp.concatenate([row_sq(m) for m in members], axis=0)
    dir_rows = jnp.concatenate([row_sq(m) for m in heads], axis=0)
    total = jnp.sum(grad_rows, axis=0, keepdims=True)
    factor = 1.0 / jnp.maximum(jnp.sqrt(total), 1.0)
    clip_rows = grad_rows * (factor * factor)
    count = grad_rows.shape[0]
    i0 = lax.broadcasted_iota(jnp.int32, (count, count), 0)
    i1 = lax.broadcasted_iota(jnp.int32, (count, count), 1)
    spread = jnp.broadcast_to(ids[...].astype(F32), (count, count))
    column = jnp.sum(jnp.where(i0 == i1, spread, 0.0), axis=1, keepdims=True)
    row_ratio = jnp.zeros((count, 1), F32)
    for k in range(GROUPS):
        hit = column == float(k)
        pick = lambda v: jnp.sum(jnp.where(hit, v, 0.0), axis=0, keepdims=True)
        ratio = jnp.sqrt(pick(clip_rows)) / jnp.sqrt(pick(dir_rows) + 1e-06)
        row_ratio = row_ratio + jnp.where(hit, ratio, 0.0)
    scaling = math.sqrt(PARAMS)
    start = 0
    for ref, member, head in zip((u1, u2, u3), members, heads):
        n = member.shape[0]
        ref[...] = scaling * (member * factor + row_ratio[start : start + n] * head)
        start += n


def per_device(sizes, field, target, mask, conv_one, conv_two, head, d1, d2, d3, ids):
    n_gx, n_gy = sizes
    _, h, width = field.shape
    rows = h + 2 * RIM
    tiles = rows // SLOTS
    flat = rows * width
    edge = (tiles + 2) * TILE
    shape = jax.ShapeDtypeStruct
    chunk = 8 * -(-C // (8 * n_gy))
    wide = 10 * C
    dma = pltpu.SemaphoreType.DMA
    vmem = pltpu.VMEM
    over_y = [dma((n_gy - 1,)), dma((n_gy - 1,))]
    over_x = [dma((n_gx - 1,)), dma((n_gx - 1,))]

    def sums(columns):
        return [
            vmem((n_gy, chunk, columns), F32),
            vmem((n_gy - 1, chunk, columns), F32),
            vmem((chunk, columns), F32),
            vmem((n_gx, chunk, columns), F32),
            vmem((chunk, columns), BF16),
        ]

    final, summed, rest = pl.pallas_call(
        functools.partial(fused_kernel, sizes),
        name="fused",
        out_shape=[
            shape(field.shape, F32),
            shape((n_gy, chunk, wide), BF16),
            shape((n_gy, chunk, TILE), BF16),
        ],
        in_specs=[ANY] * 6,
        out_specs=[VM] * 3,
        scratch_shapes=[
            vmem((3, rows, LEV, width), F32),
            vmem((3, LEV, edge), F32),
            vmem((2, rows, LEV, width), F32),
            vmem((2, rows, LEV, width), F32),
            vmem((2, tiles, LEV, TILE), F32),
            vmem((2, tiles, LEV, TILE), F32),
            vmem((rows, LEV, width), F32),
            vmem((tiles, LEV, TILE), F32),
            vmem((rows, LEV, width), F32),
            vmem((tiles, LEV, TILE), F32),
            vmem((rows, LEV, width), F32),
            vmem((tiles, LEV, TILE), F32),
            vmem((h, LEV, width), F32),
            vmem((2, 4 * LEV, flat), BF16),
            vmem((2, 4 * LEV, edge), BF16),
            vmem((2, 3 * C, flat), BF16),
            vmem((2, 3 * C, edge), BF16),
            vmem((2, C, flat), F32),
            vmem((2, C, tiles * TILE), F32),
            vmem((2, C, flat), F32),
            vmem((C, tiles * TILE), F32),
            vmem((2, K, flat), F32),
            vmem((K, tiles * TILE), F32),
            vmem((2, C, h * width), BF16),
            vmem((2, 3 * C, flat), BF16),
            vmem((2, 3 * C, edge), BF16),
            vmem((2, K, h * width), BF16),
            vmem((2, C, flat), BF16),
            vmem((C, tiles * TILE), BF16),
            vmem((rows, 3 * LEV, width), F32),
            vmem((3, C, 3 * C), F32),
            vmem((C, 12 * LEV), F32),
            vmem((K, C), F32),
            vmem(field.shape, F32),
            vmem(target.shape, F32),
            vmem(mask.shape, jnp.int32),
            vmem(conv_one.shape, F32),
            vmem(conv_two.shape, F32),
            vmem(head.shape, F32),
            vmem((3, h, width), F32),
            vmem((3, 3 * LEV, TILE), F32),
            vmem((3, 3 * LEV, TILE), F32),
            vmem((2, 3 * LEV, TILE), F32),
        ]
        + sums(wide)
        + sums(TILE)
        + [dma((6,)), dma((12,)), dma((12,))]
        + over_y + over_x + over_y
        + over_y + over_x + over_y,
        compiler_params=pltpu.CompilerParams(
            collective_id=0, has_side_effects=True, vmem_limit_bytes=LIMIT
        ),
    )(field, target, mask, conv_one, conv_two, head)
    final, u1, u2, u3 = pl.pallas_call(
        finish_kernel,
        name="update",
        out_shape=[
            shape(field.shape, F32),
            shape(conv_one.shape, F32), shape(conv_two.shape, F32), shape(head.shape, F32),
        ],
        in_specs=[VM] * 7,
        out_specs=[VM] * 4,
    )(summed, rest, final, d1, d2, d3, ids.reshape(1, -1))
    return final, u1, u2, u3


def solution(mesh):
    grid = P(None, "gx", "gy")
    placed = (grid, grid, P("gx", "gy")) + (P(),) * 7
    return jax.shard_map(
        functools.partial(per_device, (mesh.shape["gx"], mesh.shape["gy"])),
        mesh=mesh,
        in_specs=placed,
        out_specs=(grid, P(), P(), P()),
        check_vma=False,
    )
```

```python
import functools
import math

import jax
import jax.numpy as jnp
from jax import lax
from jax.experimental import pallas as pl
from jax.experimental.pallas import tpu as pltpu
from jax.sharding import PartitionSpec as P

GROUPS = 6
PARAMS = 43680
RIM = 6
NEAR = 2
LEV = 8
C = 64
K = 32
TILE = 128
SLOTS = 4
SLOT = TILE // SLOTS
MESH = pl.DeviceIdType.MESH
F32 = jnp.float32
BF16 = jnp.bfloat16
VM = pl.BlockSpec(memory_space=pltpu.VMEM)
ANY = pl.BlockSpec(memory_space=pl.ANY)
LIMIT = 56 * 1024 * 1024
NT = (((1,), (1,)), ((), ()))


def dot(a, b):
    return jnp.dot(a, b, preferred_element_type=F32)


def dot_nt(a, b):
    return lax.dot_general(a, b, NT, preferred_element_type=F32)


def sigmoid(v):
    return 0.5 * jnp.tanh(0.5 * v) + 0.5


def roll(v, shift):
    return pltpu.roll(v, shift % v.shape[1], 1)


def fused_kernel(
    sizes, field_in, target_in, mask_in, w1_in, w2_in, w3_in,
    final_ref, out_ref,
    fo, fh, fl, fr, flh, frh, wo, wh, to, th, ao, ah, ad,
    xo, xh, ho, hh, p1o, p1h, p2o, p2h, t3o, t3h, h2o, eo, eh, e3o, e1o, e1h, vo, acc2, acc1, acc3,
    field, target, mask, w1_ref, w2_ref, w3_ref, wet, left, right, left_rest, right_rest, packed, packed_rest,
    grads_ref, got, part, parts, mine,
    load_sem, send_sem, recv_sem, send_one, recv_one, send_two, recv_two, send_three, recv_three,
):
    n_gx, n_gy = sizes
    gx = lax.axis_index("gx")
    gy = lax.axis_index("gy")
    h, width = mask.shape
    rows = h + 2 * RIM
    tiles = rows // SLOTS
    ys = [lax.rem(gy + k, n_gy) for k in range(1, n_gy)]
    xs = [lax.rem(gx + k, n_gx) for k in range(1, n_gx)]
    moves = [(dx, dy) for dx in (-1, 0, 1) for dy in (-1, 0, 1) if (dx, dy) != (0, 0)]

    def exists(dx, dy):
        x = gx + dx
        y = gy + dy
        return (x >= 0) & (x < n_gx) & (y >= 0) & (y < n_gy)

    barrier = pltpu.get_barrier_semaphore()
    count = jnp.int32(n_gy + n_gx - 2)
    for dx, dy in moves:
        if dx and dy:
            @pl.when(exists(dx, dy))
            def _():
                pl.semaphore_signal(barrier, inc=1, device_id=(gx + dx, gy + dy), device_id_type=MESH)
            count = count + jnp.where(exists(dx, dy), 1, 0)
    for x in xs:
        pl.semaphore_signal(barrier, inc=1, device_id=(x, gy), device_id_type=MESH)
    for y in ys:
        pl.semaphore_signal(barrier, inc=1, device_id=(gx, y), device_id_type=MESH)

    loads = [
        pltpu.make_async_copy(src, dst, load_sem.at[i])
        for i, (src, dst) in enumerate(
            [(field_in, field), (target_in, target), (mask_in, mask),
             (w1_in, w1_ref), (w2_in, w2_ref), (w3_in, w3_ref)]
        )
    ]
    for copy in loads:
        copy.start()

    def pairs(dx, dy):
        if dy:
            k = 0 if dy > 0 else 1
            side = left if dy > 0 else right
            rest = left_rest if dy > 0 else right_rest
            return [
                (packed.at[k], side.at[1 - dx]),
                (packed_rest.at[k], rest.at[1 - dx]),
            ]
        if dx > 0:
            return [
                (fo.at[0, pl.ds(h, RIM)], fo.at[0, pl.ds(0, RIM)]),
                (wet.at[1], wet.at[0]),
                (to.at[pl.ds(RIM + h - NEAR, NEAR)], to.at[pl.ds(RIM - NEAR, NEAR)]),
            ]
        return [
            (fo.at[0, pl.ds(RIM, RIM)], fo.at[0, pl.ds(RIM + h, RIM)]),
            (wet.at[1], wet.at[2]),
            (to.at[pl.ds(RIM, NEAR)], to.at[pl.ds(RIM + h, NEAR)]),
        ]

    for dx, dy in moves:
        @pl.when(jnp.logical_not(exists(-dx, -dy)))
        def _():
            for _, dst in pairs(dx, dy):
                dst[...] = jnp.zeros(dst.shape, F32)

    for copy in loads[:3]:
        copy.wait()
    lane = lax.broadcasted_iota(jnp.int32, (3 * LEV, TILE), 1)
    strips = [jnp.zeros((3 * LEV, TILE), F32) for _ in range(2)]
    for r in range(h):
        wide_wet = jnp.broadcast_to(mask[r : r + 1, :].astype(F32), (LEV, width))
        values = wide_wet * field[:, r, :]
        goal = target[:, r, :]
        fo[0, RIM + r] = values
        to[RIM + r] = goal
        mixed = jnp.concatenate([values, wide_wet, goal], axis=0)
        here = (lane >= LEV * r) & (lane < LEV * r + LEV)
        low = mixed[:, :TILE]
        high = mixed[:, width - TILE :]
        strips[0] = jnp.where(here, roll(high, LEV * r + LEV), strips[0])
        strips[1] = jnp.where(here, roll(low, LEV * r), strips[1])
    wet[1] = mask[...].astype(F32)
    for k in range(2):
        packed[k] = strips[k][:LEV]
        packed_rest[k] = strips[k][LEV:]

    pl.semaphore_wait(barrier, count)

    copies = []
    index = 0
    for dx, dy in moves:
        group = []
        for src, dst in pairs(dx, dy):
            group.append(
                pltpu.make_async_remote_copy(
                    src_ref=src,
                    dst_ref=dst,
                    send_sem=send_sem.at[index],
                    recv_sem=recv_sem.at[index],
                    device_id=(gx + dx, gy + dy),
                    device_id_type=MESH,
                )
            )
            index += 1
        copies.append((dx, dy, group))
    for part_of in (slice(0, 1), slice(1, None)):
        for dx, dy, group in copies:
            @pl.when(exists(dx, dy))
            def _():
                for copy in group[part_of]:
                    copy.start()

    for copy in loads[3:]:
        copy.wait()
    def pipeline(stages, start, stop):
        last = max(lag for lag, _, _, _ in stages)
        for i in range(start, stop + last):
            for lag, low, high, stage in stages:
                if low <= i - lag < high:
                    stage(i - lag)

    slot_lane = lax.broadcasted_iota(jnp.int32, (1, TILE), 1) % SLOT
    slot_row = lax.broadcasted_iota(jnp.int32, (1, TILE), 1) // SLOT * tiles
    lane1 = lax.broadcasted_iota(jnp.int32, (1, TILE), 1)

    def pad16(v, n):
        return jnp.concatenate([v, jnp.zeros((v.shape[0], n - v.shape[1]), F32)], axis=1)

    def thirds(b):
        high = b.astype(BF16).astype(F32)
        low = b - high
        middle = low.astype(BF16).astype(F32)
        return jnp.concatenate([high, middle, low - middle], axis=1)

    wa = 0.5 * w1_ref[...]
    wb = 0.5 * w2_ref[...]
    wc = 0.5 * w3_ref[...]
    none = jnp.zeros((C, LEV), F32)
    w1 = jnp.concatenate(
        [
            wa[:, : 3 * LEV], none,
            wa[:, 3 * LEV : 6 * LEV], pad16(thirds(wa[:, 9 * LEV :]), LEV),
            wa[:, 6 * LEV : 9 * LEV], none,
        ],
        axis=1,
    ).astype(BF16)
    w2 = jnp.concatenate([wb[:, : 9 * C], pad16(thirds(wb[:, 9 * C :]), 16)], axis=1).astype(BF16)
    w3 = jnp.concatenate([wc[:, :C], pad16(thirds(wc[:, C:]), 16)], axis=1).astype(BF16)
    w3t = wc[:, :C].T.astype(BF16)
    flip = wb[:, : 9 * C].T
    w2t = jnp.concatenate([flip[k * C : (k + 1) * C] for k in range(8, -1, -1)], axis=1).astype(BF16)
    turn = (2.0 * wa[:, : 9 * LEV]).T
    w1t = jnp.concatenate(
        [
            jnp.concatenate(
                [turn[(3 * a + b) * LEV : (3 * a + b + 1) * LEV] for b in (2, 1, 0)], axis=1
            )
            for a in range(3)
        ],
        axis=0,
    ).astype(BF16)
    ones = jnp.ones((16, width), BF16)
    unit = jnp.ones((LEV, width), F32)

    first_lane = lane1 == 0
    last_lane = lane1 == TILE - 1

    def own_left(own, halo, q):
        r0 = roll(own[:, :TILE], 1)
        r1 = roll(own[:, TILE:], 1)
        rh = roll(halo, 1 + LEV - SLOT * (q + 1))
        return jnp.concatenate([jnp.where(first_lane, rh, r0), jnp.where(first_lane, r0, r1)], axis=1)

    def own_right(own, halo, q):
        r0 = roll(own[:, :TILE], -1)
        r1 = roll(own[:, TILE:], -1)
        rh = roll(halo, TILE - 1 - LEV - SLOT * q)
        return jnp.concatenate([jnp.where(last_lane, r1, r0), jnp.where(last_lane, rh, r1)], axis=1)

    def edge_left(owns):
        out = jnp.zeros((C, TILE), BF16)
        for q, own in enumerate(owns):
            if own is not None:
                lane = SLOT * q + LEV
                out = jnp.where(lane1 == lane, roll(own[:, TILE:], lane + 1), out)
        return out

    def edge_right(owns):
        out = jnp.zeros((C, TILE), BF16)
        for q, own in enumerate(owns):
            if own is not None:
                lane = SLOT * (q + 1) - LEV - 1
                out = jnp.where(lane1 == lane, roll(own[:, :TILE], lane), out)
        return out

    def around(v):
        return roll(v, 1), v, roll(v, -1)

    def at(r):
        return slice(r * width, (r + 1) * width)

    def tile(t, n=1):
        return slice((t + 1) * TILE, (t + 1 + n) * TILE)

    def twist(ref, s):
        ref[s, :, tile(-1)] = roll(ref[s, :, tile(tiles - 1)], SLOT)
        ref[s, :, tile(tiles)] = roll(ref[s, :, tile(0)], -SLOT)

    def stack_own(ref, s, r, *more):
        return jnp.concatenate([ref[s, :, at(r + a)] for a in (-1, 0, 1)] + list(more), axis=0)

    def stack_halo(ref, s, t, n, *more):
        return jnp.concatenate([ref[s, :, tile(t + a, n)] for a in (-1, 0, 1)] + list(more), axis=0)

    pieces = [(t, min(2, tiles - t)) for t in range(0, tiles, 2)]
    up_ok = jnp.where(gx > 0, 1.0, 0.0).astype(F32)
    down_ok = jnp.where(gx < n_gx - 1, 1.0, 0.0).astype(F32)
    left_ok = jnp.where(gy > 0, 1.0, 0.0).astype(F32)
    right_ok = jnp.where(gy < n_gy - 1, 1.0, 0.0).astype(F32)

    def inside_halo(t):
        r = slot_row + t
        side = jnp.where(slot_lane < SLOT // 2, right_ok, left_ok)
        side = jnp.where((slot_lane < LEV) | (slot_lane >= SLOT - LEV), 1.0, side)
        return side * jnp.where(r < RIM, up_ok, jnp.where(r >= RIM + h, down_ok, 1.0))

    def inside_own(v, r):
        return v * up_ok if r < RIM else v * down_ok if r >= RIM + h else v

    in_halo = [inside_halo(t) for t in range(tiles)]

    def halo_mask(t, n):
        return jnp.concatenate(in_halo[t : t + n], axis=1)

    def arrive(part_of):
        for dx, dy, group in copies:
            @pl.when(exists(-dx, -dy))
            def _():
                for copy in group[part_of]:
                    copy.wait_recv()

    def place(r):
        return (0 if r < RIM else 1 if r < RIM + h else 2), (r + h - RIM) % h

    def side_tile(t, from_right, from_left, own):
        out = None
        for q in range(SLOTS):
            where, k = place(t + tiles * q)
            row = own(t + tiles * q)
            base = SLOT * q
            for lane, piece, shift in (
                (base, row[:, TILE:], base + LEV),
                (base + LEV, from_right[where], base + LEV - LEV * k),
                (base + 2 * LEV, from_left[where], base + 2 * LEV - LEV * k),
                (base + 3 * LEV, row[:, :TILE], base + 3 * LEV),
            ):
                moved = roll(piece, shift)
                out = moved if out is None else jnp.where(lane1 >= lane, moved, out)
        return out

    def widen(r):
        where, k = place(r)
        return jnp.broadcast_to(wet[where, k : k + 1, :], (LEV, width))

    def aim(r):
        inner_row = RIM - NEAR <= r < RIM + h + NEAR
        return to[r] if inner_row else jnp.zeros((LEV, width), F32)

    def activate(u):
        t = jnp.tanh(u)
        ut = u * t
        return u + ut, (1.0 + t) * (1.0 + u - ut)

    def logits(hid, n):
        return dot(w3, jnp.concatenate([hid, ones[:, :n]], axis=0))

    def change(t3, center, others):
        total = 0.0
        for k, other in enumerate(others):
            total = total + (1.0 + t3[k * LEV : (k + 1) * LEV]) * (other - center)
        return total

    count = len(pieces)

    def halo_input(s):
        def stack_x(t):
            before, halo, after = around(fh[s, :, tile(t)])
            flh[s, t] = before
            frh[s, t] = after
            xh[s, :, tile(t)] = jnp.concatenate(
                [before, halo, after, unit[:, :TILE]], axis=0
            ).astype(BF16)

        def all_x():
            for t in range(tiles):
                stack_x(t)
            twist(xh, s)

        def first(i):
            t, n = pieces[i]
            hid, slope = activate(dot(w1, stack_halo(xh, s, t, n)))
            ok = halo_mask(t, n)
            p1h[s, :, t * TILE : (t + n) * TILE] = slope * ok
            hid = (hid * ok).astype(BF16)
            for j in range(n):
                hh[s, :, tile(t + j)] = jnp.concatenate(
                    around(hid[:, j * TILE : (j + 1) * TILE]), axis=0
                )

        return (
            [all_x]
            + [functools.partial(first, i) for i in range(count)]
            + [lambda: twist(hh, s)]
        )

    def halo_step(s):
        second_u, third_u = {}, {}

        def second(i):
            t, n = pieces[i]
            second_u[i] = dot(w2, stack_halo(hh, s, t, n, ones[:, : n * TILE]))

        def third(i):
            t, n = pieces[i]
            hid, slope = activate(second_u.pop(i))
            if s == 1:
                p2h[:, t * TILE : (t + n) * TILE] = slope
            third_u[i] = logits(hid.astype(BF16), n * TILE)

        def advance(i):
            t, n = pieces[i]
            t3 = jnp.tanh(third_u.pop(i))
            if s == 1:
                t3h[:, t * TILE : (t + n) * TILE] = t3
            for j in range(n):
                center = fh[s, :, tile(t + j)]
                fh[s + 1, :, tile(t + j)] = center + 0.125 * wh[t + j] * change(
                    t3[:, j * TILE : (j + 1) * TILE], center,
                    [fh[s, :, tile(t + j + 1)], fh[s, :, tile(t + j - 1)], frh[s, t + j], flh[s, t + j]],
                )

        order = []
        for i in range(count + 2):
            order += [
                functools.partial(stage, i - lag)
                for lag, stage in ((0, second), (1, third), (2, advance))
                if 0 <= i - lag < count
            ]
        return order + [lambda: twist(fh, s + 1)]

    def forward(s, rad, beside):
        first_u, second_u, third_u = {}, {}, {}
        top, bottom = RIM - rad, RIM + h + rad

        def stack_x(r):
            own = fo[s, r]
            halo = fh[s, :, tile(r % tiles)]
            before = own_left(own, halo, r // tiles)
            after = own_right(own, halo, r // tiles)
            fl[s, r] = before
            fr[s, r] = after
            xo[s, :, at(r)] = jnp.concatenate([before, own, after, unit], axis=0).astype(BF16)

        def dot_first(r):
            first_u[r] = dot(w1, stack_own(xo, s, r))

        def stack_h(r):
            hid, slope = activate(first_u.pop(r))
            if RIM - 1 <= r < RIM + h + 1:
                p1o[s, :, at(r)] = inside_own(slope, r)
            hid = inside_own(hid, r).astype(BF16)
            halo = hh[s, C : 2 * C, tile(r % tiles)]
            ho[s, :, at(r)] = jnp.concatenate(
                [own_left(hid, halo, r // tiles), hid, own_right(hid, halo, r // tiles)], axis=0
            )

        def dot_second(r):
            second_u[r] = dot(w2, stack_own(ho, s, r, ones))

        def dot_third(r):
            hid, slope = activate(second_u.pop(r))
            hid = hid.astype(BF16)
            mine_row = RIM <= r < RIM + h
            if s == 1 or mine_row:
                p2o[s, :, at(r)] = slope
            if mine_row:
                h2o[s, :, at(r - RIM)] = hid
            third_u[r] = logits(hid, width)

        def advance(r):
            t3 = jnp.tanh(third_u.pop(r))
            if s == 1 or RIM <= r < RIM + h:
                t3o[s, :, at(r)] = t3
            center = fo[s, r]
            fo[s + 1, r] = center + 0.125 * wo[r] * change(
                t3, center, [fo[s, r + 1], fo[s, r - 1], fr[s, r], fl[s, r]]
            )

        pipeline(
            [
                (0, top - 2, bottom + 2, stack_x),
                (2, top - 1, bottom + 1, dot_first),
                (3, top - 1, bottom + 1, stack_h),
                (5, top, bottom, dot_second),
                (6, top, bottom, dot_third),
                (7, top, bottom, advance),
                (top + 1, 0, len(beside), lambda i: beside[i]()),
            ],
            top - 2, bottom + 2,
        )

    arrive(slice(0, 1))
    for t in range(tiles):
        fh[0, :, tile(t)] = side_tile(t, right, left, lambda r: fo[0, r])
    twist(fh, 0)
    for stage in halo_input(0):
        stage()
    arrive(slice(1, None))
    for t in range(tiles):
        rest = side_tile(
            t, right_rest, left_rest, lambda r: jnp.concatenate([widen(r), aim(r)], axis=0)
        )
        wh[t] = rest[:LEV]
        th[t] = rest[LEV:]
    for r in range(rows):
        wo[r] = widen(r)
    forward(0, 4, halo_step(0) + halo_input(1))
    fold = lambda v: sum(v[:, k * TILE : (k + 1) * TILE] for k in range(v.shape[1] // TILE))

    def errors(scaled, t3, center, others):
        e3 = jnp.concatenate([scaled * (other - center) for other in others], axis=0) * (1.0 - t3 * t3)
        return e3, e3.astype(BF16)

    sums = {
        3: jnp.zeros((K, TILE), F32), 2: jnp.zeros((C, TILE), F32), 1: jnp.zeros((C, TILE), F32)
    }
    own_rows = range(RIM, RIM + h)
    back, raw_one = {}, {}

    def dot_errors(s, r):
        wg = ao[r] if s else wo[r] * ad[r - RIM]
        e3, e3b = errors(
            wg * 0.0625, t3o[s, :, at(r)], fo[s, r], [fo[s, r + 1], fo[s, r - 1], fr[s, r], fl[s, r]]
        )
        back[r] = dot(w3t, e3b)
        if r in own_rows:
            e3o[s, :, at(r - RIM)] = e3b
            sums[3] = sums[3] + fold(e3)

    def stack_errors(s, r, halo):
        e2 = back.pop(r) * p2o[s, :, at(r)]
        e2b = e2.astype(BF16)
        eo[s, :, at(r)] = jnp.concatenate(
            [own_left(e2b, halo, r // tiles), e2b, own_right(e2b, halo, r // tiles)], axis=0
        )
        if r in own_rows:
            sums[2] = sums[2] + fold(e2)

    def dot_back(s, r):
        raw_one[r] = dot(w2t, stack_own(eo, s, r))

    def keep_one(s, r):
        e1 = raw_one.pop(r) * p1o[s, :, at(r)]
        e1o[s, :, at(r)] = e1.astype(BF16)
        if s == 0 or r in own_rows:
            sums[1] = sums[1] + fold(e1)

    def halo_errors(t):
        ah[t] = wh[t] * (fh[2, :, tile(t)] - th[t])
        lanes = slice(t * TILE, (t + 1) * TILE)
        _, e3b = errors(
            ah[t] * 0.0625, t3h[:, lanes], fh[1, :, tile(t)],
            [fh[1, :, tile(t + 1)], fh[1, :, tile(t - 1)], frh[1, t], flh[1, t]],
        )
        e2b = (dot(w3t, e3b) * p2h[:, lanes]).astype(BF16)
        eh[1, :, tile(t)] = jnp.concatenate(around(e2b), axis=0)

    def halo_one(i):
        t, n = pieces[i]
        e1 = dot(w2t, stack_halo(eh, 1, t, n)) * p1h[1, :, t * TILE : (t + n) * TILE]
        e1h[:, t * TILE : (t + n) * TILE] = e1.astype(BF16)

    halo_back = [functools.partial(halo_errors, t) for t in range(tiles)]
    halo_back += [lambda: twist(eh, 1)]
    halo_back += [functools.partial(halo_one, i) for i in range(count)]
    forward(1, 2, halo_step(1) + halo_back)
    for r in range(h):
        final_ref[:, r, :] = fo[2, RIM + r]

    for r in range(RIM - 2, RIM + h + 2):
        ao[r] = wo[r] * (fo[2, r] - to[r])
    top, bottom = RIM - 2, RIM + h + 2
    pipeline(
        [
            (0, top, bottom, lambda r: dot_errors(1, r)),
            (1, top, bottom, lambda r: stack_errors(1, r, eh[1, C : 2 * C, tile(r % tiles)])),
            (3, top + 1, bottom - 1, lambda r: dot_back(1, r)),
            (4, top + 1, bottom - 1, lambda r: keep_one(1, r)),
        ],
        top, bottom,
    )
    inner = slice(RIM * width, (RIM + h) * width)

    def shifted(ref, s):
        return jnp.concatenate(
            [ref[s, :, (RIM + a) * width : (RIM + a + h) * width] for a in (-1, 0, 1)], axis=0
        )

    def grad_two(s, a):
        return dot_nt(eo[s, C : 2 * C, inner], ho[s, :, (RIM + a) * width : (RIM + a + h) * width])

    def carry_field(r):
        t = r % tiles
        e1b = e1o[1, :, at(r)]
        halo = e1h[:, t * TILE : (t + 1) * TILE]
        vo[r] = dot(
            w1t,
            jnp.concatenate(
                [own_left(e1b, halo, r // tiles), e1b, own_right(e1b, halo, r // tiles)], axis=0
            ),
        )

    def carried(k, r):
        return 0.125 * ao[r] * (1.0 + t3o[1, k * LEV : (k + 1) * LEV, at(r)])

    def adjoint(r):
        t, q = r % tiles, r // tiles
        lanes = slice(t * TILE, (t + 1) * TILE)
        halo = lambda k: 0.125 * ah[t] * (1.0 + t3h[k * LEV : (k + 1) * LEV, lanes])
        parts_here = [carried(k, r) for k in range(4)]
        ad[r - RIM] = (
            ao[r]
            - (parts_here[0] + parts_here[1] + parts_here[2] + parts_here[3])
            + carried(0, r - 1)
            + carried(1, r + 1)
            + own_left(parts_here[2], halo(2), q)
            + own_right(parts_here[3], halo(3), q)
            + vo[r + 1, :LEV]
            + vo[r, LEV : 2 * LEV]
            + vo[r - 1, 2 * LEV :]
        )

    def early(i):
        if i < 3:
            acc2[i] = grad_two(1, i - 1)
        elif i == 3:
            acc1[...] = dot_nt(e1o[1, :, inner], shifted(xo, 1))
        else:
            acc3[...] = dot_nt(e3o[1], h2o[1])

    nothing = jnp.zeros((C, TILE), BF16)
    low, high = RIM, RIM + h
    pipeline(
        [
            (0, low - 1, high + 1, carry_field),
            (2, low, high, adjoint),
            (3, low, high, lambda r: dot_errors(0, r)),
            (4, low, high, lambda r: stack_errors(0, r, nothing)),
            (low, 0, 5, early),
        ],
        low - 1, high + 1,
    )

    g2 = [acc2[a] + grad_two(0, a - 1) for a in range(3)]
    g3 = acc3[...] + dot_nt(e3o[0], h2o[0])
    chunk = grads_ref.shape[1]
    cuts = [(0, 4 * C), (4 * C, 4 * C), (8 * C, TILE), (10 * C, TILE)]

    def spread_rows(i, v):
        lo, n = cuts[i]
        for y in range(n_gy):
            at_row = y * chunk
            inside_rows = at_row + chunk <= C
            grads_ref[y, :, lo : lo + n] = (
                v[at_row : at_row + chunk] if inside_rows else jnp.zeros((chunk, n), F32)
            )

    def to_peers(i, src, dst, send, recv, peers, key):
        span = pl.ds(*cuts[i])
        group = [
            pltpu.make_async_remote_copy(
                src_ref=src(k, p, span), dst_ref=dst(k, p, span),
                send_sem=send.at[i * len(peers) + k], recv_sem=recv.at[i * len(peers) + k],
                device_id=key(p), device_id_type=MESH,
            )
            for k, p in enumerate(peers)
        ]
        for copy in group:
            copy.start()
        return group

    def scatter(i):
        return to_peers(
            i, lambda k, y, n: grads_ref.at[y, :, n], lambda k, y, n: got.at[k, :, n],
            send_one, recv_one, ys, lambda y: (gx, y),
        )

    def cross(i):
        return to_peers(
            i, lambda k, x, n: part.at[:, n], lambda k, x, n: parts.at[gx, :, n],
            send_two, recv_two, xs, lambda x: (x, gy),
        )

    def gather(i):
        return to_peers(
            i, lambda k, y, n: mine.at[:, n], lambda k, y, n: out_ref.at[gy, :, n],
            send_three, recv_three, ys, lambda y: (gx, y),
        )

    spread_rows(0, jnp.concatenate([g2[0], g2[1][:, :C]], axis=1))
    one = [scatter(0)]
    spread_rows(1, jnp.concatenate([g2[1][:, C:], g2[2][:, : 2 * C]], axis=1))
    one.append(scatter(1))
    spread_rows(
        2,
        jnp.concatenate(
            [g2[2][:, 2 * C :], jnp.concatenate([g3, jnp.zeros((C - K, C), F32)], axis=0)], axis=1
        ),
    )
    one.append(scatter(2))

    for t in range(tiles):
        owns = [
            eo[0, C : 2 * C, at(t + tiles * q)] if RIM <= t + tiles * q < RIM + h else None
            for q in range(SLOTS)
        ]
        eh[0, :, tile(t)] = jnp.concatenate([edge_left(owns), nothing, edge_right(owns)], axis=0)
    twist(eh, 0)
    for r in (RIM - 2, RIM - 1, RIM + h, RIM + h + 1):
        eo[0, :, at(r)] = jnp.zeros((3 * C, width), BF16)
    g1 = acc1[...]
    for t, n in pieces:
        e1 = dot(w2t, stack_halo(eh, 0, t, n)) * p1h[0, :, t * TILE : (t + n) * TILE]
        sums[1] = sums[1] + fold(e1)
        g1 = g1 + dot_nt(e1.astype(BF16), stack_halo(xh, 0, t, n))
    pipeline(
        [
            (0, low - 1, high + 1, lambda r: dot_back(0, r)),
            (1, low - 1, high + 1, lambda r: keep_one(0, r)),
        ],
        low - 1, high + 1,
    )
    ring = h + 2
    g1 = g1 + dot_nt(
        e1o[0, :, (RIM - 1) * width : (RIM + h + 1) * width],
        jnp.concatenate(
            [xo[0, :, (RIM - 1 + a) * width : (RIM - 1 + a + ring) * width] for a in (-1, 0, 1)], axis=0
        ),
    )
    total = lambda v: jnp.sum(v, axis=1, keepdims=True)
    tall = lambda v: jnp.concatenate([v, jnp.zeros((C - v.shape[0], 1), F32)], axis=0)
    extra = pad16(
        jnp.concatenate([g1, total(sums[1]), total(sums[2]), tall(total(sums[3]))], axis=1), TILE
    )
    spread_rows(3, extra)
    one.append(scatter(3))
    two, three = [], []
    for i, (lo, n) in enumerate(cuts):
        span = slice(lo, lo + n)
        acc = grads_ref[gy, :, span]
        for k, copy in enumerate(one[i]):
            copy.wait_recv()
            acc = acc + got[k, :, span]
        part[:, span] = acc
        two.append(cross(i))
        parts[gx, :, span] = acc
    for i, (lo, n) in enumerate(cuts):
        span = slice(lo, lo + n)
        for copy in two[i]:
            copy.wait_recv()
        acc = parts[0, :, span]
        for x in range(1, n_gx):
            acc = acc + parts[x, :, span]
        acc = acc.astype(BF16)
        mine[:, span] = acc
        three.append(gather(i))
        out_ref[gy, :, span] = acc
    for group in three:
        for copy in group:
            copy.wait_recv()
    for dx, dy, group in copies:
        @pl.when(exists(dx, dy))
        def _():
            for copy in group:
                copy.wait_send()
    for group in one + two + three:
        for copy in group:
            copy.wait_send()


def finish_kernel(grads, final, d1, d2, d3, ids, final_out, u1, u2, u3):
    final_out[...] = final[...]
    n_parts = C // grads.shape[1]
    big = jnp.concatenate([grads[y].astype(F32) for y in range(n_parts)], axis=0)
    side = big[:, 10 * C :]
    one = jnp.concatenate(
        [side[:, 4 * LEV * a : 4 * LEV * a + 3 * LEV] for a in range(3)]
        + [side[:, 12 * LEV : 12 * LEV + 1]],
        axis=1,
    )
    two = jnp.concatenate([big[:, : 9 * C], side[:, 12 * LEV + 1 : 12 * LEV + 2]], axis=1)
    three = jnp.concatenate(
        [big[:K, 9 * C : 10 * C], side[:K, 12 * LEV + 2 : 12 * LEV + 3]], axis=1
    )
    members = [one, two, three]
    heads = [d1[...], d2[...], d3[...]]
    row_sq = lambda v: jnp.sum(v * v, axis=1, keepdims=True)
    grad_rows = jnp.concatenate([row_sq(m) for m in members], axis=0)
    dir_rows = jnp.concatenate([row_sq(m) for m in heads], axis=0)
    total = jnp.sum(grad_rows, axis=0, keepdims=True)
    factor = 1.0 / jnp.maximum(jnp.sqrt(total), 1.0)
    clip_rows = grad_rows * (factor * factor)
    count = grad_rows.shape[0]
    i0 = lax.broadcasted_iota(jnp.int32, (count, count), 0)
    i1 = lax.broadcasted_iota(jnp.int32, (count, count), 1)
    spread = jnp.broadcast_to(ids[...].astype(F32), (count, count))
    column = jnp.sum(jnp.where(i0 == i1, spread, 0.0), axis=1, keepdims=True)
    row_ratio = jnp.zeros((count, 1), F32)
    for k in range(GROUPS):
        hit = column == float(k)
        pick = lambda v: jnp.sum(jnp.where(hit, v, 0.0), axis=0, keepdims=True)
        ratio = jnp.sqrt(pick(clip_rows)) / jnp.sqrt(pick(dir_rows) + 1e-06)
        row_ratio = row_ratio + jnp.where(hit, ratio, 0.0)
    scaling = math.sqrt(PARAMS)
    start = 0
    for ref, member, head in zip((u1, u2, u3), members, heads):
        n = member.shape[0]
        ref[...] = scaling * (member * factor + row_ratio[start : start + n] * head)
        start += n


def per_device(sizes, field, target, mask, conv_one, conv_two, head, d1, d2, d3, ids):
    n_gx, n_gy = sizes
    _, h, width = field.shape
    rows = h + 2 * RIM
    tiles = rows // SLOTS
    flat = rows * width
    edge = (tiles + 2) * TILE
    shape = jax.ShapeDtypeStruct
    chunk = 8 * -(-C // (8 * n_gy))
    wide = 10 * C + TILE
    dma = pltpu.SemaphoreType.DMA
    vmem = pltpu.VMEM
    over_y = [dma((4 * (n_gy - 1),))] * 2
    over_x = [dma((4 * (n_gx - 1),))] * 2

    def sums(columns):
        return [
            vmem((n_gy, chunk, columns), F32),
            vmem((n_gy - 1, chunk, columns), F32),
            vmem((chunk, columns), F32),
            vmem((n_gx, chunk, columns), F32),
            vmem((chunk, columns), BF16),
        ]

    final, summed = pl.pallas_call(
        functools.partial(fused_kernel, sizes),
        name="fused",
        out_shape=[
            shape(field.shape, F32),
            shape((n_gy, chunk, wide), BF16),
        ],
        in_specs=[ANY] * 6,
        out_specs=[VM] * 2,
        scratch_shapes=[
            vmem((3, rows, LEV, width), F32),
            vmem((3, LEV, edge), F32),
            vmem((2, rows, LEV, width), F32),
            vmem((2, rows, LEV, width), F32),
            vmem((2, tiles, LEV, TILE), F32),
            vmem((2, tiles, LEV, TILE), F32),
            vmem((rows, LEV, width), F32),
            vmem((tiles, LEV, TILE), F32),
            vmem((rows, LEV, width), F32),
            vmem((tiles, LEV, TILE), F32),
            vmem((rows, LEV, width), F32),
            vmem((tiles, LEV, TILE), F32),
            vmem((h, LEV, width), F32),
            vmem((2, 4 * LEV, flat), BF16),
            vmem((2, 4 * LEV, edge), BF16),
            vmem((2, 3 * C, flat), BF16),
            vmem((2, 3 * C, edge), BF16),
            vmem((2, C, flat), F32),
            vmem((2, C, tiles * TILE), F32),
            vmem((2, C, flat), F32),
            vmem((C, tiles * TILE), F32),
            vmem((2, K, flat), F32),
            vmem((K, tiles * TILE), F32),
            vmem((2, C, h * width), BF16),
            vmem((2, 3 * C, flat), BF16),
            vmem((2, 3 * C, edge), BF16),
            vmem((2, K, h * width), BF16),
            vmem((2, C, flat), BF16),
            vmem((C, tiles * TILE), BF16),
            vmem((rows, 3 * LEV, width), F32),
            vmem((3, C, 3 * C), F32),
            vmem((C, 12 * LEV), F32),
            vmem((K, C), F32),
            vmem(field.shape, F32),
            vmem(target.shape, F32),
            vmem(mask.shape, jnp.int32),
            vmem(conv_one.shape, F32),
            vmem(conv_two.shape, F32),
            vmem(head.shape, F32),
            vmem((3, h, width), F32),
            vmem((3, LEV, TILE), F32),
            vmem((3, LEV, TILE), F32),
            vmem((3, 2 * LEV, TILE), F32),
            vmem((3, 2 * LEV, TILE), F32),
            vmem((2, LEV, TILE), F32),
            vmem((2, 2 * LEV, TILE), F32),
        ]
        + sums(wide)
        + [dma((6,)), dma((18,)), dma((18,))]
        + over_y + over_x + over_y,
        compiler_params=pltpu.CompilerParams(
            collective_id=0, has_side_effects=True, vmem_limit_bytes=LIMIT
        ),
    )(field, target, mask, conv_one, conv_two, head)
    final, u1, u2, u3 = pl.pallas_call(
        finish_kernel,
        name="update",
        out_shape=[
            shape(field.shape, F32),
            shape(conv_one.shape, F32), shape(conv_two.shape, F32), shape(head.shape, F32),
        ],
        in_specs=[VM] * 6,
        out_specs=[VM] * 4,
    )(summed, final, d1, d2, d3, ids.reshape(1, -1))
    return final, u1, u2, u3


def solution(mesh):
    grid = P(None, "gx", "gy")
    placed = (grid, grid, P("gx", "gy")) + (P(),) * 7
    return jax.shard_map(
        functools.partial(per_device, (mesh.shape["gx"], mesh.shape["gy"])),
        mesh=mesh,
        in_specs=placed,
        out_specs=(grid, P(), P(), P()),
        check_vma=False,
    )
```

```python
import functools
import math

import jax
import jax.numpy as jnp
from jax import lax
from jax.experimental import pallas as pl
from jax.experimental.pallas import tpu as pltpu
from jax.sharding import PartitionSpec as P

GROUPS = 6
PARAMS = 43680
RIM = 6
NEAR = 2
LEV = 8
C = 64
K = 32
TILE = 128
SLOTS = 4
SLOT = TILE // SLOTS
MESH = pl.DeviceIdType.MESH
F32 = jnp.float32
BF16 = jnp.bfloat16
VM = pl.BlockSpec(memory_space=pltpu.VMEM)
ANY = pl.BlockSpec(memory_space=pl.ANY)
LIMIT = 56 * 1024 * 1024
NT = (((1,), (1,)), ((), ()))


def dot(a, b):
    return jnp.dot(a, b, preferred_element_type=F32)


def dot_nt(a, b):
    return lax.dot_general(a, b, NT, preferred_element_type=F32)


def sigmoid(v):
    return 0.5 * jnp.tanh(0.5 * v) + 0.5


def roll(v, shift):
    return pltpu.roll(v, shift % v.shape[1], 1)


def fused_kernel(
    sizes, field_in, target_in, mask_in, w1_in, w2_in, w3_in,
    final_ref, out_ref,
    fo, fh, fl, fr, flh, frh, wo, wh, to, th, ao, ah, ad,
    xo, xh, ho, hh, p1o, p1h, p2o, p2h, t3o, t3h, h2o, eo, eh, e3o, e1o, e1h, vo, acc2, acc1, acc3,
    field, target, mask, w1_ref, w2_ref, w3_ref, wet, left, right, left_rest, right_rest, packed, packed_rest,
    grads_ref, got, part, parts, mine,
    load_sem, send_sem, recv_sem, send_one, recv_one, send_two, recv_two, send_three, recv_three,
):
    n_gx, n_gy = sizes
    gx = lax.axis_index("gx")
    gy = lax.axis_index("gy")
    h, width = mask.shape
    rows = h + 2 * RIM
    tiles = rows // SLOTS
    ys = [lax.rem(gy + k, n_gy) for k in range(1, n_gy)]
    xs = [lax.rem(gx + k, n_gx) for k in range(1, n_gx)]
    moves = [(dx, dy) for dx in (-1, 0, 1) for dy in (-1, 0, 1) if (dx, dy) != (0, 0)]

    def exists(dx, dy):
        x = gx + dx
        y = gy + dy
        return (x >= 0) & (x < n_gx) & (y >= 0) & (y < n_gy)

    barrier = pltpu.get_barrier_semaphore()
    count = jnp.int32(n_gy + n_gx - 2)
    for dx, dy in moves:
        if dx and dy:
            @pl.when(exists(dx, dy))
            def _():
                pl.semaphore_signal(barrier, inc=1, device_id=(gx + dx, gy + dy), device_id_type=MESH)
            count = count + jnp.where(exists(dx, dy), 1, 0)
    for x in xs:
        pl.semaphore_signal(barrier, inc=1, device_id=(x, gy), device_id_type=MESH)
    for y in ys:
        pl.semaphore_signal(barrier, inc=1, device_id=(gx, y), device_id_type=MESH)

    loads = [
        pltpu.make_async_copy(src, dst, load_sem.at[i])
        for i, (src, dst) in enumerate(
            [(field_in, field), (target_in, target), (mask_in, mask),
             (w1_in, w1_ref), (w2_in, w2_ref), (w3_in, w3_ref)]
        )
    ]
    for copy in loads:
        copy.start()

    def pairs(dx, dy):
        if dy:
            k = 0 if dy > 0 else 1
            side = left if dy > 0 else right
            rest = left_rest if dy > 0 else right_rest
            return [
                (packed.at[k], side.at[1 - dx]),
                (packed_rest.at[k], rest.at[1 - dx]),
            ]
        if dx > 0:
            return [
                (fo.at[0, pl.ds(h, RIM)], fo.at[0, pl.ds(0, RIM)]),
                (wet.at[1], wet.at[0]),
                (to.at[pl.ds(RIM + h - NEAR, NEAR)], to.at[pl.ds(RIM - NEAR, NEAR)]),
            ]
        return [
            (fo.at[0, pl.ds(RIM, RIM)], fo.at[0, pl.ds(RIM + h, RIM)]),
            (wet.at[1], wet.at[2]),
            (to.at[pl.ds(RIM, NEAR)], to.at[pl.ds(RIM + h, NEAR)]),
        ]

    for dx, dy in moves:
        @pl.when(jnp.logical_not(exists(-dx, -dy)))
        def _():
            for _, dst in pairs(dx, dy):
                dst[...] = jnp.zeros(dst.shape, F32)

    for copy in loads[:3]:
        copy.wait()
    lane = lax.broadcasted_iota(jnp.int32, (3 * LEV, TILE), 1)
    strips = [jnp.zeros((3 * LEV, TILE), F32) for _ in range(2)]
    for r in range(h):
        wide_wet = jnp.broadcast_to(mask[r : r + 1, :].astype(F32), (LEV, width))
        values = wide_wet * field[:, r, :]
        goal = target[:, r, :]
        fo[0, RIM + r] = values
        to[RIM + r] = goal
        mixed = jnp.concatenate([values, wide_wet, goal], axis=0)
        here = (lane >= LEV * r) & (lane < LEV * r + LEV)
        low = mixed[:, :TILE]
        high = mixed[:, width - TILE :]
        strips[0] = jnp.where(here, roll(high, LEV * r + LEV), strips[0])
        strips[1] = jnp.where(here, roll(low, LEV * r), strips[1])
    wet[1] = mask[...].astype(F32)
    for k in range(2):
        packed[k] = strips[k][:LEV]
        packed_rest[k] = strips[k][LEV:]

    pl.semaphore_wait(barrier, count)

    copies = []
    index = 0
    for dx, dy in moves:
        group = []
        for src, dst in pairs(dx, dy):
            group.append(
                pltpu.make_async_remote_copy(
                    src_ref=src,
                    dst_ref=dst,
                    send_sem=send_sem.at[index],
                    recv_sem=recv_sem.at[index],
                    device_id=(gx + dx, gy + dy),
                    device_id_type=MESH,
                )
            )
            index += 1
        copies.append((dx, dy, group))
    for part_of in (slice(0, 1), slice(1, None)):
        for dx, dy, group in copies:
            @pl.when(exists(dx, dy))
            def _():
                for copy in group[part_of]:
                    copy.start()

    for copy in loads[3:]:
        copy.wait()
    def pipeline(stages, start, stop):
        last = max(lag for lag, _, _, _ in stages)
        for i in range(start, stop + last):
            for lag, low, high, stage in stages:
                if low <= i - lag < high:
                    stage(i - lag)

    slot_lane = lax.broadcasted_iota(jnp.int32, (1, TILE), 1) % SLOT
    slot_row = lax.broadcasted_iota(jnp.int32, (1, TILE), 1) // SLOT * tiles
    lane1 = lax.broadcasted_iota(jnp.int32, (1, TILE), 1)

    def pad16(v, n):
        return jnp.concatenate([v, jnp.zeros((v.shape[0], n - v.shape[1]), F32)], axis=1)

    def thirds(b):
        high = b.astype(BF16).astype(F32)
        low = b - high
        middle = low.astype(BF16).astype(F32)
        return jnp.concatenate([high, middle, low - middle], axis=1)

    wa = 0.5 * w1_ref[...]
    wb = 0.5 * w2_ref[...]
    wc = 0.5 * w3_ref[...]
    none = jnp.zeros((C, LEV), F32)
    w1 = jnp.concatenate(
        [
            wa[:, : 3 * LEV], none,
            wa[:, 3 * LEV : 6 * LEV], pad16(thirds(wa[:, 9 * LEV :]), LEV),
            wa[:, 6 * LEV : 9 * LEV], none,
        ],
        axis=1,
    ).astype(BF16)
    w2 = jnp.concatenate([wb[:, : 9 * C], pad16(thirds(wb[:, 9 * C :]), 16)], axis=1).astype(BF16)
    w3 = jnp.concatenate([wc[:, :C], pad16(thirds(wc[:, C:]), 16)], axis=1).astype(BF16)
    w3t = wc[:, :C].T.astype(BF16)
    flip = wb[:, : 9 * C].T
    w2t = jnp.concatenate([flip[k * C : (k + 1) * C] for k in range(8, -1, -1)], axis=1).astype(BF16)
    turn = (2.0 * wa[:, : 9 * LEV]).T
    w1t = jnp.concatenate(
        [
            jnp.concatenate(
                [turn[(3 * a + b) * LEV : (3 * a + b + 1) * LEV] for b in (2, 1, 0)], axis=1
            )
            for a in range(3)
        ],
        axis=0,
    ).astype(BF16)
    ones = jnp.ones((16, width), BF16)
    unit = jnp.ones((LEV, width), F32)

    first_lane = lane1 == 0
    last_lane = lane1 == TILE - 1

    def own_left(own, halo, q):
        r0 = roll(own[:, :TILE], 1)
        r1 = roll(own[:, TILE:], 1)
        rh = roll(halo, 1 + LEV - SLOT * (q + 1))
        return jnp.concatenate([jnp.where(first_lane, rh, r0), jnp.where(first_lane, r0, r1)], axis=1)

    def own_right(own, halo, q):
        r0 = roll(own[:, :TILE], -1)
        r1 = roll(own[:, TILE:], -1)
        rh = roll(halo, TILE - 1 - LEV - SLOT * q)
        return jnp.concatenate([jnp.where(last_lane, r1, r0), jnp.where(last_lane, rh, r1)], axis=1)

    def edge_left(owns):
        out = jnp.zeros((C, TILE), BF16)
        for q, own in enumerate(owns):
            if own is not None:
                lane = SLOT * q + LEV
                out = jnp.where(lane1 == lane, roll(own[:, TILE:], lane + 1), out)
        return out

    def edge_right(owns):
        out = jnp.zeros((C, TILE), BF16)
        for q, own in enumerate(owns):
            if own is not None:
                lane = SLOT * (q + 1) - LEV - 1
                out = jnp.where(lane1 == lane, roll(own[:, :TILE], lane), out)
        return out

    def around(v):
        return roll(v, 1), v, roll(v, -1)

    def at(r):
        return slice(r * width, (r + 1) * width)

    def tile(t, n=1):
        return slice((t + 1) * TILE, (t + 1 + n) * TILE)

    def twist(ref, s):
        ref[s, :, tile(-1)] = roll(ref[s, :, tile(tiles - 1)], SLOT)
        ref[s, :, tile(tiles)] = roll(ref[s, :, tile(0)], -SLOT)

    def stack_own(ref, s, r, *more):
        return jnp.concatenate([ref[s, :, at(r + a)] for a in (-1, 0, 1)] + list(more), axis=0)

    def stack_halo(ref, s, t, n, *more):
        return jnp.concatenate([ref[s, :, tile(t + a, n)] for a in (-1, 0, 1)] + list(more), axis=0)

    pieces = [(t, min(2, tiles - t)) for t in range(0, tiles, 2)]
    up_ok = jnp.where(gx > 0, 1.0, 0.0).astype(F32)
    down_ok = jnp.where(gx < n_gx - 1, 1.0, 0.0).astype(F32)
    left_ok = jnp.where(gy > 0, 1.0, 0.0).astype(F32)
    right_ok = jnp.where(gy < n_gy - 1, 1.0, 0.0).astype(F32)

    def inside_halo(t):
        r = slot_row + t
        side = jnp.where(slot_lane < SLOT // 2, right_ok, left_ok)
        side = jnp.where((slot_lane < LEV) | (slot_lane >= SLOT - LEV), 1.0, side)
        return side * jnp.where(r < RIM, up_ok, jnp.where(r >= RIM + h, down_ok, 1.0))

    def inside_own(v, r):
        return v * up_ok if r < RIM else v * down_ok if r >= RIM + h else v

    in_halo = [inside_halo(t) for t in range(tiles)]

    def halo_mask(t, n):
        return jnp.concatenate(in_halo[t : t + n], axis=1)

    def arrive(part_of):
        for dx, dy, group in copies:
            @pl.when(exists(-dx, -dy))
            def _():
                for copy in group[part_of]:
                    copy.wait_recv()

    def place(r):
        return (0 if r < RIM else 1 if r < RIM + h else 2), (r + h - RIM) % h

    def side_tile(t, from_right, from_left, own):
        out = None
        for q in range(SLOTS):
            where, k = place(t + tiles * q)
            row = own(t + tiles * q)
            base = SLOT * q
            for lane, piece, shift in (
                (base, row[:, TILE:], base + LEV),
                (base + LEV, from_right[where], base + LEV - LEV * k),
                (base + 2 * LEV, from_left[where], base + 2 * LEV - LEV * k),
                (base + 3 * LEV, row[:, :TILE], base + 3 * LEV),
            ):
                moved = roll(piece, shift)
                out = moved if out is None else jnp.where(lane1 >= lane, moved, out)
        return out

    def widen(r):
        where, k = place(r)
        return jnp.broadcast_to(wet[where, k : k + 1, :], (LEV, width))

    def aim(r):
        inner_row = RIM - NEAR <= r < RIM + h + NEAR
        return to[r] if inner_row else jnp.zeros((LEV, width), F32)

    def activate(u):
        t = jnp.tanh(u)
        ut = u * t
        return u + ut, (1.0 + t) * (1.0 + u - ut)

    def logits(hid, n):
        return dot(w3, jnp.concatenate([hid, ones[:, :n]], axis=0))

    def change(t3, center, others):
        total = 0.0
        for k, other in enumerate(others):
            total = total + (1.0 + t3[k * LEV : (k + 1) * LEV]) * (other - center)
        return total

    count = len(pieces)

    def halo_input(s):
        def stack_x(t):
            before, halo, after = around(fh[s, :, tile(t)])
            flh[s, t] = before
            frh[s, t] = after
            xh[s, :, tile(t)] = jnp.concatenate(
                [before, halo, after, unit[:, :TILE]], axis=0
            ).astype(BF16)

        def all_x():
            for t in range(tiles):
                stack_x(t)
            twist(xh, s)

        def first(i):
            t, n = pieces[i]
            hid, slope = activate(dot(w1, stack_halo(xh, s, t, n)))
            ok = halo_mask(t, n)
            p1h[s, :, t * TILE : (t + n) * TILE] = slope * ok
            hid = (hid * ok).astype(BF16)
            for j in range(n):
                hh[s, :, tile(t + j)] = jnp.concatenate(
                    around(hid[:, j * TILE : (j + 1) * TILE]), axis=0
                )

        return (
            [all_x]
            + [functools.partial(first, i) for i in range(count)]
            + [lambda: twist(hh, s)]
        )

    def halo_step(s):
        second_u, third_u = {}, {}

        def second(i):
            t, n = pieces[i]
            second_u[i] = dot(w2, stack_halo(hh, s, t, n, ones[:, : n * TILE]))

        def third(i):
            t, n = pieces[i]
            hid, slope = activate(second_u.pop(i))
            if s == 1:
                p2h[:, t * TILE : (t + n) * TILE] = slope
            third_u[i] = logits(hid.astype(BF16), n * TILE)

        def advance(i):
            t, n = pieces[i]
            t3 = jnp.tanh(third_u.pop(i))
            if s == 1:
                t3h[:, t * TILE : (t + n) * TILE] = t3
            for j in range(n):
                center = fh[s, :, tile(t + j)]
                fh[s + 1, :, tile(t + j)] = center + 0.125 * wh[t + j] * change(
                    t3[:, j * TILE : (j + 1) * TILE], center,
                    [fh[s, :, tile(t + j + 1)], fh[s, :, tile(t + j - 1)], frh[s, t + j], flh[s, t + j]],
                )

        order = []
        for i in range(count + 2):
            order += [
                functools.partial(stage, i - lag)
                for lag, stage in ((0, second), (1, third), (2, advance))
                if 0 <= i - lag < count
            ]
        return order + [lambda: twist(fh, s + 1)]

    def own_input(s, r):
        own = fo[s, r]
        halo = fh[s, :, tile(r % tiles)]
        before = own_left(own, halo, r // tiles)
        after = own_right(own, halo, r // tiles)
        fl[s, r] = before
        fr[s, r] = after
        xo[s, :, at(r)] = jnp.concatenate([before, own, after, unit], axis=0).astype(BF16)

    def forward(s, rad, beside):
        first_u, second_u, third_u = {}, {}, {}
        top, bottom = RIM - rad, RIM + h + rad

        def dot_first(r):
            first_u[r] = dot(w1, stack_own(xo, s, r))

        def stack_h(r):
            hid, slope = activate(first_u.pop(r))
            if RIM - 1 <= r < RIM + h + 1:
                p1o[s, :, at(r)] = inside_own(slope, r)
            hid = inside_own(hid, r).astype(BF16)
            halo = hh[s, C : 2 * C, tile(r % tiles)]
            ho[s, :, at(r)] = jnp.concatenate(
                [own_left(hid, halo, r // tiles), hid, own_right(hid, halo, r // tiles)], axis=0
            )

        def dot_second(r):
            second_u[r] = dot(w2, stack_own(ho, s, r, ones))

        def dot_third(r):
            hid, slope = activate(second_u.pop(r))
            hid = hid.astype(BF16)
            mine_row = RIM <= r < RIM + h
            if s == 1 or mine_row:
                p2o[s, :, at(r)] = slope
            if mine_row:
                h2o[s, :, at(r - RIM)] = hid
            third_u[r] = logits(hid, width)

        def advance(r):
            t3 = jnp.tanh(third_u.pop(r))
            if s == 1 or RIM <= r < RIM + h:
                t3o[s, :, at(r)] = t3
            center = fo[s, r]
            fo[s + 1, r] = center + 0.125 * wo[r] * change(
                t3, center, [fo[s, r + 1], fo[s, r - 1], fr[s, r], fl[s, r]]
            )

        pipeline(
            [
                (0, top - 2, bottom + 2 if s else 0, lambda r: own_input(s, r)),
                (2, top - 1, bottom + 1, dot_first),
                (3, top - 1, bottom + 1, stack_h),
                (5, top, bottom, dot_second),
                (6, top, bottom, dot_third),
                (7, top, bottom, advance),
                (top + 1, 0, len(beside), lambda i: beside[i]()),
            ],
            top - 2, bottom + 2,
        )

    arrive(slice(0, 1))
    for t in range(tiles):
        fh[0, :, tile(t)] = side_tile(t, right, left, lambda r: fo[0, r])
    twist(fh, 0)
    opening = halo_input(0)
    pipeline(
        [
            (0, 0, len(opening), lambda i: opening[i]()),
            (0, 0, rows, lambda r: own_input(0, r)),
        ],
        0, rows,
    )
    arrive(slice(1, None))
    for t in range(tiles):
        rest = side_tile(
            t, right_rest, left_rest, lambda r: jnp.concatenate([widen(r), aim(r)], axis=0)
        )
        wh[t] = rest[:LEV]
        th[t] = rest[LEV:]
    for r in range(rows):
        wo[r] = widen(r)
    forward(0, 4, halo_step(0) + halo_input(1))
    fold = lambda v: sum(v[:, k * TILE : (k + 1) * TILE] for k in range(v.shape[1] // TILE))

    def errors(scaled, t3, center, others):
        e3 = jnp.concatenate([scaled * (other - center) for other in others], axis=0) * (1.0 - t3 * t3)
        return e3, e3.astype(BF16)

    sums = {
        3: jnp.zeros((K, TILE), F32), 2: jnp.zeros((C, TILE), F32), 1: jnp.zeros((C, TILE), F32)
    }
    own_rows = range(RIM, RIM + h)
    back, raw_one = {}, {}

    def dot_errors(s, r):
        wg = ao[r] if s else wo[r] * ad[r - RIM]
        e3, e3b = errors(
            wg * 0.0625, t3o[s, :, at(r)], fo[s, r], [fo[s, r + 1], fo[s, r - 1], fr[s, r], fl[s, r]]
        )
        back[r] = dot(w3t, e3b)
        if r in own_rows:
            e3o[s, :, at(r - RIM)] = e3b
            sums[3] = sums[3] + fold(e3)

    def stack_errors(s, r, halo):
        e2 = back.pop(r) * p2o[s, :, at(r)]
        e2b = e2.astype(BF16)
        eo[s, :, at(r)] = jnp.concatenate(
            [own_left(e2b, halo, r // tiles), e2b, own_right(e2b, halo, r // tiles)], axis=0
        )
        if r in own_rows:
            sums[2] = sums[2] + fold(e2)

    def dot_back(s, r):
        raw_one[r] = dot(w2t, stack_own(eo, s, r))

    def keep_one(s, r):
        e1 = raw_one.pop(r) * p1o[s, :, at(r)]
        e1o[s, :, at(r)] = e1.astype(BF16)
        if s == 0 or r in own_rows:
            sums[1] = sums[1] + fold(e1)

    def halo_errors(t):
        ah[t] = wh[t] * (fh[2, :, tile(t)] - th[t])
        lanes = slice(t * TILE, (t + 1) * TILE)
        _, e3b = errors(
            ah[t] * 0.0625, t3h[:, lanes], fh[1, :, tile(t)],
            [fh[1, :, tile(t + 1)], fh[1, :, tile(t - 1)], frh[1, t], flh[1, t]],
        )
        e2b = (dot(w3t, e3b) * p2h[:, lanes]).astype(BF16)
        eh[1, :, tile(t)] = jnp.concatenate(around(e2b), axis=0)

    def halo_one(i):
        t, n = pieces[i]
        e1 = dot(w2t, stack_halo(eh, 1, t, n)) * p1h[1, :, t * TILE : (t + n) * TILE]
        e1h[:, t * TILE : (t + n) * TILE] = e1.astype(BF16)

    halo_back = [functools.partial(halo_errors, t) for t in range(tiles)]
    halo_back += [lambda: twist(eh, 1)]
    halo_back += [functools.partial(halo_one, i) for i in range(count)]
    forward(1, 2, halo_step(1) + halo_back)
    for r in range(h):
        final_ref[:, r, :] = fo[2, RIM + r]

    for r in range(RIM - 2, RIM + h + 2):
        ao[r] = wo[r] * (fo[2, r] - to[r])
    top, bottom = RIM - 2, RIM + h + 2
    pipeline(
        [
            (0, top, bottom, lambda r: dot_errors(1, r)),
            (1, top, bottom, lambda r: stack_errors(1, r, eh[1, C : 2 * C, tile(r % tiles)])),
            (3, top + 1, bottom - 1, lambda r: dot_back(1, r)),
            (4, top + 1, bottom - 1, lambda r: keep_one(1, r)),
        ],
        top, bottom,
    )
    inner = slice(RIM * width, (RIM + h) * width)

    def shifted(ref, s):
        return jnp.concatenate(
            [ref[s, :, (RIM + a) * width : (RIM + a + h) * width] for a in (-1, 0, 1)], axis=0
        )

    def grad_two(s, a):
        return dot_nt(eo[s, C : 2 * C, inner], ho[s, :, (RIM + a) * width : (RIM + a + h) * width])

    def carry_field(r):
        t = r % tiles
        e1b = e1o[1, :, at(r)]
        halo = e1h[:, t * TILE : (t + 1) * TILE]
        vo[r] = dot(
            w1t,
            jnp.concatenate(
                [own_left(e1b, halo, r // tiles), e1b, own_right(e1b, halo, r // tiles)], axis=0
            ),
        )

    def carried(k, r):
        return 0.125 * ao[r] * (1.0 + t3o[1, k * LEV : (k + 1) * LEV, at(r)])

    def adjoint(r):
        t, q = r % tiles, r // tiles
        lanes = slice(t * TILE, (t + 1) * TILE)
        halo = lambda k: 0.125 * ah[t] * (1.0 + t3h[k * LEV : (k + 1) * LEV, lanes])
        parts_here = [carried(k, r) for k in range(4)]
        ad[r - RIM] = (
            ao[r]
            - (parts_here[0] + parts_here[1] + parts_here[2] + parts_here[3])
            + carried(0, r - 1)
            + carried(1, r + 1)
            + own_left(parts_here[2], halo(2), q)
            + own_right(parts_here[3], halo(3), q)
            + vo[r + 1, :LEV]
            + vo[r, LEV : 2 * LEV]
            + vo[r - 1, 2 * LEV :]
        )

    def early(i):
        if i < 3:
            acc2[i] = grad_two(1, i - 1)
        elif i == 3:
            acc1[...] = dot_nt(e1o[1, :, inner], shifted(xo, 1))
        else:
            acc3[...] = dot_nt(e3o[1], h2o[1])

    nothing = jnp.zeros((C, TILE), BF16)
    low, high = RIM, RIM + h
    pipeline(
        [
            (0, low - 1, high + 1, carry_field),
            (2, low, high, adjoint),
            (3, low, high, lambda r: dot_errors(0, r)),
            (4, low, high, lambda r: stack_errors(0, r, nothing)),
            (low, 0, 5, early),
        ],
        low - 1, high + 1,
    )

    g2 = [acc2[a] + grad_two(0, a - 1) for a in range(3)]
    g3 = acc3[...] + dot_nt(e3o[0], h2o[0])
    chunk = grads_ref.shape[1]
    cuts = [(0, 4 * C), (4 * C, 4 * C), (8 * C, TILE), (10 * C, TILE)]

    def spread_rows(i, v):
        lo, n = cuts[i]
        for y in range(n_gy):
            at_row = y * chunk
            inside_rows = at_row + chunk <= C
            grads_ref[y, :, lo : lo + n] = (
                v[at_row : at_row + chunk] if inside_rows else jnp.zeros((chunk, n), F32)
            )

    def to_peers(i, src, dst, send, recv, peers, key):
        span = pl.ds(*cuts[i])
        group = [
            pltpu.make_async_remote_copy(
                src_ref=src(k, p, span), dst_ref=dst(k, p, span),
                send_sem=send.at[i], recv_sem=recv.at[i],
                device_id=key(p), device_id_type=MESH,
            )
            for k, p in enumerate(peers)
        ]
        for copy in group:
            copy.start()

    def settle(i, ref, sem):
        span = pl.ds(*cuts[i])
        pltpu.make_async_copy(ref.at[:, :, span], ref.at[:, :, span], sem.at[i]).wait()

    def scatter(i):
        to_peers(
            i, lambda k, y, n: grads_ref.at[y, :, n], lambda k, y, n: got.at[k, :, n],
            send_one, recv_one, ys, lambda y: (gx, y),
        )

    def cross(i):
        to_peers(
            i, lambda k, x, n: part.at[:, n], lambda k, x, n: parts.at[gx, :, n],
            send_two, recv_two, xs, lambda x: (x, gy),
        )

    def gather(i):
        to_peers(
            i, lambda k, y, n: mine.at[:, n], lambda k, y, n: out_ref.at[gy, :, n],
            send_three, recv_three, ys, lambda y: (gx, y),
        )

    spread_rows(0, jnp.concatenate([g2[0], g2[1][:, :C]], axis=1))
    scatter(0)
    spread_rows(1, jnp.concatenate([g2[1][:, C:], g2[2][:, : 2 * C]], axis=1))
    scatter(1)
    spread_rows(
        2,
        jnp.concatenate(
            [g2[2][:, 2 * C :], jnp.concatenate([g3, jnp.zeros((C - K, C), F32)], axis=0)], axis=1
        ),
    )
    scatter(2)

    for r in (RIM - 2, RIM - 1, RIM + h, RIM + h + 1):
        eo[0, :, at(r)] = jnp.zeros((3 * C, width), BF16)
    g1 = {0: acc1[...]}

    def edges(t):
        owns = [
            eo[0, C : 2 * C, at(t + tiles * q)] if RIM <= t + tiles * q < RIM + h else None
            for q in range(SLOTS)
        ]
        eh[0, :, tile(t)] = jnp.concatenate([edge_left(owns), nothing, edge_right(owns)], axis=0)

    def edge_one(i):
        t, n = pieces[i]
        e1 = dot(w2t, stack_halo(eh, 0, t, n)) * p1h[0, :, t * TILE : (t + n) * TILE]
        sums[1] = sums[1] + fold(e1)
        g1[0] = g1[0] + dot_nt(e1.astype(BF16), stack_halo(xh, 0, t, n))

    closing = [functools.partial(edges, t) for t in range(tiles)]
    closing += [lambda: twist(eh, 0)] + [functools.partial(edge_one, i) for i in range(count)]
    pipeline(
        [
            (0, low - 1, high + 1, lambda r: dot_back(0, r)),
            (1, low - 1, high + 1, lambda r: keep_one(0, r)),
            (low - 1, 0, len(closing), lambda i: closing[i]()),
        ],
        low - 1, high + 1,
    )
    ring = h + 2
    g1 = g1[0] + dot_nt(
        e1o[0, :, (RIM - 1) * width : (RIM + h + 1) * width],
        jnp.concatenate(
            [xo[0, :, (RIM - 1 + a) * width : (RIM - 1 + a + ring) * width] for a in (-1, 0, 1)], axis=0
        ),
    )
    total = lambda v: jnp.sum(v, axis=1, keepdims=True)
    tall = lambda v: jnp.concatenate([v, jnp.zeros((C - v.shape[0], 1), F32)], axis=0)
    extra = pad16(
        jnp.concatenate([g1, total(sums[1]), total(sums[2]), tall(total(sums[3]))], axis=1), TILE
    )
    spread_rows(3, extra)
    scatter(3)
    others_x = parts.at[pl.ds(0, n_gx - 1)]
    others_y = out_ref.at[pl.ds(0, n_gy - 1)]
    for i, (lo, n) in enumerate(cuts):
        span = slice(lo, lo + n)
        settle(i, got, recv_one)
        acc = grads_ref[gy, :, span]
        for k in range(n_gy - 1):
            acc = acc + got[k, :, span]
        part[:, span] = acc
        cross(i)
        parts[gx, :, span] = acc
    for dx, dy, group in copies:
        @pl.when(exists(dx, dy))
        def _():
            for copy in group:
                copy.wait_send()
    for i in range(len(cuts)):
        settle(i, got, send_one)
    for i, (lo, n) in enumerate(cuts):
        span = slice(lo, lo + n)
        settle(i, others_x, recv_two)
        acc = parts[0, :, span]
        for x in range(1, n_gx):
            acc = acc + parts[x, :, span]
        acc = acc.astype(BF16)
        mine[:, span] = acc
        gather(i)
        out_ref[gy, :, span] = acc
    for i in range(len(cuts)):
        settle(i, others_x, send_two)
    for i in range(len(cuts)):
        settle(i, others_y, recv_three)
    for i in range(len(cuts)):
        settle(i, others_y, send_three)


def finish_kernel(grads, final, d1, d2, d3, ids, final_out, u1, u2, u3):
    final_out[...] = final[...]
    n_parts = C // grads.shape[1]
    big = jnp.concatenate([grads[y].astype(F32) for y in range(n_parts)], axis=0)
    side = big[:, 10 * C :]
    one = jnp.concatenate(
        [side[:, 4 * LEV * a : 4 * LEV * a + 3 * LEV] for a in range(3)]
        + [side[:, 12 * LEV : 12 * LEV + 1]],
        axis=1,
    )
    two = jnp.concatenate([big[:, : 9 * C], side[:, 12 * LEV + 1 : 12 * LEV + 2]], axis=1)
    three = jnp.concatenate(
        [big[:K, 9 * C : 10 * C], side[:K, 12 * LEV + 2 : 12 * LEV + 3]], axis=1
    )
    members = [one, two, three]
    heads = [d1[...], d2[...], d3[...]]
    row_sq = lambda v: jnp.sum(v * v, axis=1, keepdims=True)
    grad_rows = jnp.concatenate([row_sq(m) for m in members], axis=0)
    dir_rows = jnp.concatenate([row_sq(m) for m in heads], axis=0)
    total = jnp.sum(grad_rows, axis=0, keepdims=True)
    factor = 1.0 / jnp.maximum(jnp.sqrt(total), 1.0)
    clip_rows = grad_rows * (factor * factor)
    count = grad_rows.shape[0]
    i0 = lax.broadcasted_iota(jnp.int32, (count, count), 0)
    i1 = lax.broadcasted_iota(jnp.int32, (count, count), 1)
    spread = jnp.broadcast_to(ids[...].astype(F32), (count, count))
    column = jnp.sum(jnp.where(i0 == i1, spread, 0.0), axis=1, keepdims=True)
    row_ratio = jnp.zeros((count, 1), F32)
    for k in range(GROUPS):
        hit = column == float(k)
        pick = lambda v: jnp.sum(jnp.where(hit, v, 0.0), axis=0, keepdims=True)
        ratio = jnp.sqrt(pick(clip_rows)) / jnp.sqrt(pick(dir_rows) + 1e-06)
        row_ratio = row_ratio + jnp.where(hit, ratio, 0.0)
    scaling = math.sqrt(PARAMS)
    start = 0
    for ref, member, head in zip((u1, u2, u3), members, heads):
        n = member.shape[0]
        ref[...] = scaling * (member * factor + row_ratio[start : start + n] * head)
        start += n


def per_device(sizes, field, target, mask, conv_one, conv_two, head, d1, d2, d3, ids):
    n_gx, n_gy = sizes
    _, h, width = field.shape
    rows = h + 2 * RIM
    tiles = rows // SLOTS
    flat = rows * width
    edge = (tiles + 2) * TILE
    shape = jax.ShapeDtypeStruct
    chunk = 8 * -(-C // (8 * n_gy))
    wide = 10 * C + TILE
    dma = pltpu.SemaphoreType.DMA
    vmem = pltpu.VMEM
    over_y = [dma((4,))] * 2
    over_x = [dma((4,))] * 2

    def sums(columns):
        return [
            vmem((n_gy, chunk, columns), F32),
            vmem((n_gy - 1, chunk, columns), F32),
            vmem((chunk, columns), F32),
            vmem((n_gx, chunk, columns), F32),
            vmem((chunk, columns), BF16),
        ]

    final, summed = pl.pallas_call(
        functools.partial(fused_kernel, sizes),
        name="fused",
        out_shape=[
            shape(field.shape, F32),
            shape((n_gy, chunk, wide), BF16),
        ],
        in_specs=[ANY] * 6,
        out_specs=[VM] * 2,
        scratch_shapes=[
            vmem((3, rows, LEV, width), F32),
            vmem((3, LEV, edge), F32),
            vmem((2, rows, LEV, width), F32),
            vmem((2, rows, LEV, width), F32),
            vmem((2, tiles, LEV, TILE), F32),
            vmem((2, tiles, LEV, TILE), F32),
            vmem((rows, LEV, width), F32),
            vmem((tiles, LEV, TILE), F32),
            vmem((rows, LEV, width), F32),
            vmem((tiles, LEV, TILE), F32),
            vmem((rows, LEV, width), F32),
            vmem((tiles, LEV, TILE), F32),
            vmem((h, LEV, width), F32),
            vmem((2, 4 * LEV, flat), BF16),
            vmem((2, 4 * LEV, edge), BF16),
            vmem((2, 3 * C, flat), BF16),
            vmem((2, 3 * C, edge), BF16),
            vmem((2, C, flat), F32),
            vmem((2, C, tiles * TILE), F32),
            vmem((2, C, flat), F32),
            vmem((C, tiles * TILE), F32),
            vmem((2, K, flat), F32),
            vmem((K, tiles * TILE), F32),
            vmem((2, C, h * width), BF16),
            vmem((2, 3 * C, flat), BF16),
            vmem((2, 3 * C, edge), BF16),
            vmem((2, K, h * width), BF16),
            vmem((2, C, flat), BF16),
            vmem((C, tiles * TILE), BF16),
            vmem((rows, 3 * LEV, width), F32),
            vmem((3, C, 3 * C), F32),
            vmem((C, 12 * LEV), F32),
            vmem((K, C), F32),
            vmem(field.shape, F32),
            vmem(target.shape, F32),
            vmem(mask.shape, jnp.int32),
            vmem(conv_one.shape, F32),
            vmem(conv_two.shape, F32),
            vmem(head.shape, F32),
            vmem((3, h, width), F32),
            vmem((3, LEV, TILE), F32),
            vmem((3, LEV, TILE), F32),
            vmem((3, 2 * LEV, TILE), F32),
            vmem((3, 2 * LEV, TILE), F32),
            vmem((2, LEV, TILE), F32),
            vmem((2, 2 * LEV, TILE), F32),
        ]
        + sums(wide)
        + [dma((6,)), dma((18,)), dma((18,))]
        + over_y + over_x + over_y,
        compiler_params=pltpu.CompilerParams(
            collective_id=0, has_side_effects=True, vmem_limit_bytes=LIMIT
        ),
    )(field, target, mask, conv_one, conv_two, head)
    final, u1, u2, u3 = pl.pallas_call(
        finish_kernel,
        name="update",
        out_shape=[
            shape(field.shape, F32),
            shape(conv_one.shape, F32), shape(conv_two.shape, F32), shape(head.shape, F32),
        ],
        in_specs=[VM] * 6,
        out_specs=[VM] * 4,
    )(summed, final, d1, d2, d3, ids.reshape(1, -1))
    return final, u1, u2, u3


def solution(mesh):
    grid = P(None, "gx", "gy")
    placed = (grid, grid, P("gx", "gy")) + (P(),) * 7
    return jax.shard_map(
        functools.partial(per_device, (mesh.shape["gx"], mesh.shape["gy"])),
        mesh=mesh,
        in_specs=placed,
        out_specs=(grid, P(), P(), P()),
        check_vma=False,
    )
```

```python
import functools
import math

import jax
import jax.numpy as jnp
from jax import lax
from jax.experimental import pallas as pl
from jax.experimental.pallas import tpu as pltpu
from jax.sharding import PartitionSpec as P

GROUPS = 6
PARAMS = 43680
RIM = 6
NEAR = 2
LEV = 8
C = 64
K = 32
TILE = 128
SLOTS = 4
SLOT = TILE // SLOTS
MESH = pl.DeviceIdType.MESH
F32 = jnp.float32
BF16 = jnp.bfloat16
VM = pl.BlockSpec(memory_space=pltpu.VMEM)
ANY = pl.BlockSpec(memory_space=pl.ANY)
LIMIT = 28 * 1024 * 1024
SMALL = 8 * 1024 * 1024
NT = (((1,), (1,)), ((), ()))


def dot(a, b):
    return jnp.dot(a, b, preferred_element_type=F32)


def dot_nt(a, b):
    return lax.dot_general(a, b, NT, preferred_element_type=F32)


def sigmoid(v):
    return 0.5 * jnp.tanh(0.5 * v) + 0.5


def roll(v, shift):
    return pltpu.roll(v, shift % v.shape[1], 1)


def fused_kernel(
    sizes, field_in, target_in, mask_in, w1_in, w2_in, w3_in,
    final_ref, out_ref,
    fo, fh, fl, fr, flh, frh, wo, wh, to, th, ao, ah, ad,
    xo, xh, ho, hh, p1o, p1h, p2o, p2h, t3o, t3h, h2o, eo, eh, e3o, e1o, e1h, vo, acc2, acc1, acc3,
    field, target, mask, w1_ref, w2_ref, w3_ref, wet, left, right, left_rest, right_rest, packed, packed_rest,
    grads_ref, got, part, parts, mine,
    load_sem, send_sem, recv_sem, send_one, recv_one, send_two, recv_two, send_three, recv_three,
):
    n_gx, n_gy = sizes
    gx = lax.axis_index("gx")
    gy = lax.axis_index("gy")
    h, width = mask.shape
    rows = h + 2 * RIM
    tiles = rows // SLOTS
    ys = [lax.rem(gy + k, n_gy) for k in range(1, n_gy)]
    xs = [lax.rem(gx + k, n_gx) for k in range(1, n_gx)]
    moves = [(dx, dy) for dx in (-1, 0, 1) for dy in (-1, 0, 1) if (dx, dy) != (0, 0)]

    def exists(dx, dy):
        x = gx + dx
        y = gy + dy
        return (x >= 0) & (x < n_gx) & (y >= 0) & (y < n_gy)

    barrier = pltpu.get_barrier_semaphore()
    count = jnp.int32(n_gy + n_gx - 2)
    for dx, dy in moves:
        if dx and dy:
            @pl.when(exists(dx, dy))
            def _():
                pl.semaphore_signal(barrier, inc=1, device_id=(gx + dx, gy + dy), device_id_type=MESH)
            count = count + jnp.where(exists(dx, dy), 1, 0)
    for x in xs:
        pl.semaphore_signal(barrier, inc=1, device_id=(x, gy), device_id_type=MESH)
    for y in ys:
        pl.semaphore_signal(barrier, inc=1, device_id=(gx, y), device_id_type=MESH)

    loads = [
        pltpu.make_async_copy(src, dst, load_sem.at[i])
        for i, (src, dst) in enumerate(
            [(field_in, field), (target_in, target), (mask_in, mask),
             (w1_in, w1_ref), (w2_in, w2_ref), (w3_in, w3_ref)]
        )
    ]
    for copy in loads:
        copy.start()

    def pairs(dx, dy):
        if dy:
            k = 0 if dy > 0 else 1
            side = left if dy > 0 else right
            rest = left_rest if dy > 0 else right_rest
            return [
                (packed.at[k], side.at[1 - dx]),
                (packed_rest.at[k], rest.at[1 - dx]),
            ]
        if dx > 0:
            return [
                (fo.at[0, pl.ds(h, RIM)], fo.at[0, pl.ds(0, RIM)]),
                (wet.at[1], wet.at[0]),
                (to.at[pl.ds(RIM + h - NEAR, NEAR)], to.at[pl.ds(RIM - NEAR, NEAR)]),
            ]
        return [
            (fo.at[0, pl.ds(RIM, RIM)], fo.at[0, pl.ds(RIM + h, RIM)]),
            (wet.at[1], wet.at[2]),
            (to.at[pl.ds(RIM, NEAR)], to.at[pl.ds(RIM + h, NEAR)]),
        ]

    for dx, dy in moves:
        @pl.when(jnp.logical_not(exists(-dx, -dy)))
        def _():
            for _, dst in pairs(dx, dy):
                dst[...] = jnp.zeros(dst.shape, F32)

    for copy in loads[:3]:
        copy.wait()
    lane = lax.broadcasted_iota(jnp.int32, (3 * LEV, TILE), 1)
    strips = [jnp.zeros((3 * LEV, TILE), F32) for _ in range(2)]
    for r in range(h):
        wide_wet = jnp.broadcast_to(mask[r : r + 1, :].astype(F32), (LEV, width))
        values = wide_wet * field[:, r, :]
        goal = target[:, r, :]
        fo[0, RIM + r] = values
        to[RIM + r] = goal
        mixed = jnp.concatenate([values, wide_wet, goal], axis=0)
        here = (lane >= LEV * r) & (lane < LEV * r + LEV)
        low = mixed[:, :TILE]
        high = mixed[:, width - TILE :]
        strips[0] = jnp.where(here, roll(high, LEV * r + LEV), strips[0])
        strips[1] = jnp.where(here, roll(low, LEV * r), strips[1])
    wet[1] = mask[...].astype(F32)
    for k in range(2):
        packed[k] = strips[k][:LEV]
        packed_rest[k] = strips[k][LEV:]

    pl.semaphore_wait(barrier, count)

    copies = []
    index = 0
    for dx, dy in moves:
        group = []
        for src, dst in pairs(dx, dy):
            group.append(
                pltpu.make_async_remote_copy(
                    src_ref=src,
                    dst_ref=dst,
                    send_sem=send_sem.at[index],
                    recv_sem=recv_sem.at[index],
                    device_id=(gx + dx, gy + dy),
                    device_id_type=MESH,
                )
            )
            index += 1
        copies.append((dx, dy, group))
    for part_of in (slice(0, 1), slice(1, None)):
        for dx, dy, group in copies:
            @pl.when(exists(dx, dy))
            def _():
                for copy in group[part_of]:
                    copy.start()

    for copy in loads[3:]:
        copy.wait()
    def pipeline(stages, start, stop):
        last = max(lag for lag, _, _, _ in stages)
        for i in range(start, stop + last):
            for lag, low, high, stage in stages:
                if low <= i - lag < high:
                    stage(i - lag)

    slot_lane = lax.broadcasted_iota(jnp.int32, (1, TILE), 1) % SLOT
    slot_row = lax.broadcasted_iota(jnp.int32, (1, TILE), 1) // SLOT * tiles
    lane1 = lax.broadcasted_iota(jnp.int32, (1, TILE), 1)

    def pad16(v, n):
        return jnp.concatenate([v, jnp.zeros((v.shape[0], n - v.shape[1]), F32)], axis=1)

    def thirds(b):
        high = b.astype(BF16).astype(F32)
        low = b - high
        middle = low.astype(BF16).astype(F32)
        return jnp.concatenate([high, middle, low - middle], axis=1)

    wa = 0.5 * w1_ref[...]
    wb = 0.5 * w2_ref[...]
    wc = 0.5 * w3_ref[...]
    none = jnp.zeros((C, LEV), F32)
    w1 = jnp.concatenate(
        [
            wa[:, : 3 * LEV], none,
            wa[:, 3 * LEV : 6 * LEV], pad16(thirds(wa[:, 9 * LEV :]), LEV),
            wa[:, 6 * LEV : 9 * LEV], none,
        ],
        axis=1,
    ).astype(BF16)
    w2 = jnp.concatenate([wb[:, : 9 * C], pad16(thirds(wb[:, 9 * C :]), 16)], axis=1).astype(BF16)
    w3 = jnp.concatenate([wc[:, :C], pad16(thirds(wc[:, C:]), 16)], axis=1).astype(BF16)
    w3t = wc[:, :C].T.astype(BF16)
    flip = wb[:, : 9 * C].T
    w2t = jnp.concatenate([flip[k * C : (k + 1) * C] for k in range(8, -1, -1)], axis=1).astype(BF16)
    turn = (2.0 * wa[:, : 9 * LEV]).T
    w1t = jnp.concatenate(
        [
            jnp.concatenate(
                [turn[(3 * a + b) * LEV : (3 * a + b + 1) * LEV] for b in (2, 1, 0)], axis=1
            )
            for a in range(3)
        ],
        axis=0,
    ).astype(BF16)
    ones = jnp.ones((16, width), BF16)
    unit = jnp.ones((LEV, width), F32)

    first_lane = lane1 == 0
    last_lane = lane1 == TILE - 1

    def own_left(own, halo, q):
        r0 = roll(own[:, :TILE], 1)
        r1 = roll(own[:, TILE:], 1)
        rh = roll(halo, 1 + LEV - SLOT * (q + 1))
        return jnp.concatenate([jnp.where(first_lane, rh, r0), jnp.where(first_lane, r0, r1)], axis=1)

    def own_right(own, halo, q):
        r0 = roll(own[:, :TILE], -1)
        r1 = roll(own[:, TILE:], -1)
        rh = roll(halo, TILE - 1 - LEV - SLOT * q)
        return jnp.concatenate([jnp.where(last_lane, r1, r0), jnp.where(last_lane, rh, r1)], axis=1)

    def edge_left(owns):
        out = jnp.zeros((C, TILE), BF16)
        for q, own in enumerate(owns):
            if own is not None:
                lane = SLOT * q + LEV
                out = jnp.where(lane1 == lane, roll(own[:, TILE:], lane + 1), out)
        return out

    def edge_right(owns):
        out = jnp.zeros((C, TILE), BF16)
        for q, own in enumerate(owns):
            if own is not None:
                lane = SLOT * (q + 1) - LEV - 1
                out = jnp.where(lane1 == lane, roll(own[:, :TILE], lane), out)
        return out

    def around(v):
        return roll(v, 1), v, roll(v, -1)

    def at(r):
        return slice(r * width, (r + 1) * width)

    def tile(t, n=1):
        return slice((t + 1) * TILE, (t + 1 + n) * TILE)

    def twist(ref, s):
        ref[s, :, tile(-1)] = roll(ref[s, :, tile(tiles - 1)], SLOT)
        ref[s, :, tile(tiles)] = roll(ref[s, :, tile(0)], -SLOT)

    def stack_own(ref, s, r, *more):
        return jnp.concatenate([ref[s, :, at(r + a)] for a in (-1, 0, 1)] + list(more), axis=0)

    def stack_halo(ref, s, t, n, *more):
        return jnp.concatenate([ref[s, :, tile(t + a, n)] for a in (-1, 0, 1)] + list(more), axis=0)

    pieces = [(t, min(2, tiles - t)) for t in range(0, tiles, 2)]
    up_ok = jnp.where(gx > 0, 1.0, 0.0).astype(F32)
    down_ok = jnp.where(gx < n_gx - 1, 1.0, 0.0).astype(F32)
    left_ok = jnp.where(gy > 0, 1.0, 0.0).astype(F32)
    right_ok = jnp.where(gy < n_gy - 1, 1.0, 0.0).astype(F32)

    def inside_halo(t):
        r = slot_row + t
        side = jnp.where(slot_lane < SLOT // 2, right_ok, left_ok)
        side = jnp.where((slot_lane < LEV) | (slot_lane >= SLOT - LEV), 1.0, side)
        return side * jnp.where(r < RIM, up_ok, jnp.where(r >= RIM + h, down_ok, 1.0))

    def inside_own(v, r):
        return v * up_ok if r < RIM else v * down_ok if r >= RIM + h else v

    in_halo = [inside_halo(t) for t in range(tiles)]

    def halo_mask(t, n):
        return jnp.concatenate(in_halo[t : t + n], axis=1)

    def arrive(part_of):
        for dx, dy, group in copies:
            @pl.when(exists(-dx, -dy))
            def _():
                for copy in group[part_of]:
                    copy.wait_recv()

    def place(r):
        return (0 if r < RIM else 1 if r < RIM + h else 2), (r + h - RIM) % h

    def side_tile(t, from_right, from_left, own):
        out = None
        for q in range(SLOTS):
            where, k = place(t + tiles * q)
            row = own(t + tiles * q)
            base = SLOT * q
            for lane, piece, shift in (
                (base, row[:, TILE:], base + LEV),
                (base + LEV, from_right[where], base + LEV - LEV * k),
                (base + 2 * LEV, from_left[where], base + 2 * LEV - LEV * k),
                (base + 3 * LEV, row[:, :TILE], base + 3 * LEV),
            ):
                moved = roll(piece, shift)
                out = moved if out is None else jnp.where(lane1 >= lane, moved, out)
        return out

    def widen(r):
        where, k = place(r)
        return jnp.broadcast_to(wet[where, k : k + 1, :], (LEV, width))

    def aim(r):
        inner_row = RIM - NEAR <= r < RIM + h + NEAR
        return to[r] if inner_row else jnp.zeros((LEV, width), F32)

    def activate(u):
        t = jnp.tanh(u)
        ut = u * t
        return u + ut, (1.0 + t) * (1.0 + u - ut)

    def logits(hid, n):
        return dot(w3, jnp.concatenate([hid, ones[:, :n]], axis=0))

    def change(t3, center, others):
        total = 0.0
        for k, other in enumerate(others):
            total = total + (1.0 + t3[k * LEV : (k + 1) * LEV]) * (other - center)
        return total

    count = len(pieces)

    def halo_input(s):
        def stack_x(t):
            before, halo, after = around(fh[s, :, tile(t)])
            flh[s, t] = before
            frh[s, t] = after
            xh[s, :, tile(t)] = jnp.concatenate(
                [before, halo, after, unit[:, :TILE]], axis=0
            ).astype(BF16)

        def all_x():
            for t in range(tiles):
                stack_x(t)
            twist(xh, s)

        def first(i):
            t, n = pieces[i]
            hid, slope = activate(dot(w1, stack_halo(xh, s, t, n)))
            ok = halo_mask(t, n)
            p1h[s, :, t * TILE : (t + n) * TILE] = slope * ok
            hid = (hid * ok).astype(BF16)
            for j in range(n):
                hh[s, :, tile(t + j)] = jnp.concatenate(
                    around(hid[:, j * TILE : (j + 1) * TILE]), axis=0
                )

        return (
            [all_x]
            + [functools.partial(first, i) for i in range(count)]
            + [lambda: twist(hh, s)]
        )

    def halo_step(s):
        second_u, third_u = {}, {}

        def second(i):
            t, n = pieces[i]
            second_u[i] = dot(w2, stack_halo(hh, s, t, n, ones[:, : n * TILE]))

        def third(i):
            t, n = pieces[i]
            hid, slope = activate(second_u.pop(i))
            if s == 1:
                p2h[:, t * TILE : (t + n) * TILE] = slope
            third_u[i] = logits(hid.astype(BF16), n * TILE)

        def advance(i):
            t, n = pieces[i]
            t3 = jnp.tanh(third_u.pop(i))
            if s == 1:
                t3h[:, t * TILE : (t + n) * TILE] = t3
            for j in range(n):
                center = fh[s, :, tile(t + j)]
                fh[s + 1, :, tile(t + j)] = center + 0.125 * wh[t + j] * change(
                    t3[:, j * TILE : (j + 1) * TILE], center,
                    [fh[s, :, tile(t + j + 1)], fh[s, :, tile(t + j - 1)], frh[s, t + j], flh[s, t + j]],
                )

        order = []
        for i in range(count + 2):
            order += [
                functools.partial(stage, i - lag)
                for lag, stage in ((0, second), (1, third), (2, advance))
                if 0 <= i - lag < count
            ]
        return order + [lambda: twist(fh, s + 1)]

    def own_input(s, r):
        own = fo[s, r]
        halo = fh[s, :, tile(r % tiles)]
        before = own_left(own, halo, r // tiles)
        after = own_right(own, halo, r // tiles)
        fl[s, r] = before
        fr[s, r] = after
        xo[s, :, at(r)] = jnp.concatenate([before, own, after, unit], axis=0).astype(BF16)

    def forward(s, rad, beside):
        first_u, second_u, third_u = {}, {}, {}
        top, bottom = RIM - rad, RIM + h + rad

        def dot_first(r):
            first_u[r] = dot(w1, stack_own(xo, s, r))

        def stack_h(r):
            hid, slope = activate(first_u.pop(r))
            if RIM - 1 <= r < RIM + h + 1:
                p1o[s, :, at(r)] = inside_own(slope, r)
            hid = inside_own(hid, r).astype(BF16)
            halo = hh[s, C : 2 * C, tile(r % tiles)]
            ho[s, :, at(r)] = jnp.concatenate(
                [own_left(hid, halo, r // tiles), hid, own_right(hid, halo, r // tiles)], axis=0
            )

        def dot_second(r):
            second_u[r] = dot(w2, stack_own(ho, s, r, ones))

        def dot_third(r):
            hid, slope = activate(second_u.pop(r))
            hid = hid.astype(BF16)
            mine_row = RIM <= r < RIM + h
            if s == 1 or mine_row:
                p2o[s, :, at(r)] = slope
            if mine_row:
                h2o[s, :, at(r - RIM)] = hid
            third_u[r] = logits(hid, width)

        def advance(r):
            t3 = jnp.tanh(third_u.pop(r))
            if s == 1 or RIM <= r < RIM + h:
                t3o[s, :, at(r)] = t3
            center = fo[s, r]
            fo[s + 1, r] = center + 0.125 * wo[r] * change(
                t3, center, [fo[s, r + 1], fo[s, r - 1], fr[s, r], fl[s, r]]
            )

        pipeline(
            [
                (0, top - 2, bottom + 2 if s else 0, lambda r: own_input(s, r)),
                (2, top - 1, bottom + 1, dot_first),
                (3, top - 1, bottom + 1, stack_h),
                (5, top, bottom, dot_second),
                (6, top, bottom, dot_third),
                (7, top, bottom, advance),
                (top + 1, 0, len(beside), lambda i: beside[i]()),
            ],
            top - 2, bottom + 2,
        )

    arrive(slice(0, 1))
    for t in range(tiles):
        fh[0, :, tile(t)] = side_tile(t, right, left, lambda r: fo[0, r])
    twist(fh, 0)
    opening = halo_input(0)
    pipeline(
        [
            (0, 0, len(opening), lambda i: opening[i]()),
            (0, 0, rows, lambda r: own_input(0, r)),
        ],
        0, rows,
    )
    arrive(slice(1, None))
    for t in range(tiles):
        rest = side_tile(
            t, right_rest, left_rest, lambda r: jnp.concatenate([widen(r), aim(r)], axis=0)
        )
        wh[t] = rest[:LEV]
        th[t] = rest[LEV:]
    for r in range(rows):
        wo[r] = widen(r)
    forward(0, 4, halo_step(0) + halo_input(1))
    fold = lambda v: sum(v[:, k * TILE : (k + 1) * TILE] for k in range(v.shape[1] // TILE))

    def errors(scaled, t3, center, others):
        e3 = jnp.concatenate([scaled * (other - center) for other in others], axis=0) * (1.0 - t3 * t3)
        return e3, e3.astype(BF16)

    sums = {
        3: jnp.zeros((K, TILE), F32), 2: jnp.zeros((C, TILE), F32), 1: jnp.zeros((C, TILE), F32)
    }
    own_rows = range(RIM, RIM + h)
    back, raw_one = {}, {}

    def dot_errors(s, r):
        wg = ao[r] if s else wo[r] * ad[r - RIM]
        e3, e3b = errors(
            wg * 0.0625, t3o[s, :, at(r)], fo[s, r], [fo[s, r + 1], fo[s, r - 1], fr[s, r], fl[s, r]]
        )
        back[r] = dot(w3t, e3b)
        if r in own_rows:
            e3o[s, :, at(r - RIM)] = e3b
            sums[3] = sums[3] + fold(e3)

    def stack_errors(s, r, halo):
        e2 = back.pop(r) * p2o[s, :, at(r)]
        e2b = e2.astype(BF16)
        eo[s, :, at(r)] = jnp.concatenate(
            [own_left(e2b, halo, r // tiles), e2b, own_right(e2b, halo, r // tiles)], axis=0
        )
        if r in own_rows:
            sums[2] = sums[2] + fold(e2)

    def dot_back(s, r):
        raw_one[r] = dot(w2t, stack_own(eo, s, r))

    def keep_one(s, r):
        e1 = raw_one.pop(r) * p1o[s, :, at(r)]
        e1o[s, :, at(r)] = e1.astype(BF16)
        if s == 0 or r in own_rows:
            sums[1] = sums[1] + fold(e1)

    def halo_errors(t):
        ah[t] = wh[t] * (fh[2, :, tile(t)] - th[t])
        lanes = slice(t * TILE, (t + 1) * TILE)
        _, e3b = errors(
            ah[t] * 0.0625, t3h[:, lanes], fh[1, :, tile(t)],
            [fh[1, :, tile(t + 1)], fh[1, :, tile(t - 1)], frh[1, t], flh[1, t]],
        )
        e2b = (dot(w3t, e3b) * p2h[:, lanes]).astype(BF16)
        eh[1, :, tile(t)] = jnp.concatenate(around(e2b), axis=0)

    def halo_one(i):
        t, n = pieces[i]
        e1 = dot(w2t, stack_halo(eh, 1, t, n)) * p1h[1, :, t * TILE : (t + n) * TILE]
        e1h[:, t * TILE : (t + n) * TILE] = e1.astype(BF16)

    halo_back = [functools.partial(halo_errors, t) for t in range(tiles)]
    halo_back += [lambda: twist(eh, 1)]
    halo_back += [functools.partial(halo_one, i) for i in range(count)]
    forward(1, 2, halo_step(1) + halo_back)
    for r in range(h):
        final_ref[:, r, :] = fo[2, RIM + r]

    for r in range(RIM - 2, RIM + h + 2):
        ao[r] = wo[r] * (fo[2, r] - to[r])
    top, bottom = RIM - 2, RIM + h + 2
    pipeline(
        [
            (0, top, bottom, lambda r: dot_errors(1, r)),
            (1, top, bottom, lambda r: stack_errors(1, r, eh[1, C : 2 * C, tile(r % tiles)])),
            (3, top + 1, bottom - 1, lambda r: dot_back(1, r)),
            (4, top + 1, bottom - 1, lambda r: keep_one(1, r)),
        ],
        top, bottom,
    )
    inner = slice(RIM * width, (RIM + h) * width)

    def shifted(ref, s):
        return jnp.concatenate(
            [ref[s, :, (RIM + a) * width : (RIM + a + h) * width] for a in (-1, 0, 1)], axis=0
        )

    def grad_two(s, a):
        return dot_nt(eo[s, C : 2 * C, inner], ho[s, :, (RIM + a) * width : (RIM + a + h) * width])

    def carry_field(r):
        t = r % tiles
        e1b = e1o[1, :, at(r)]
        halo = e1h[:, t * TILE : (t + 1) * TILE]
        vo[r] = dot(
            w1t,
            jnp.concatenate(
                [own_left(e1b, halo, r // tiles), e1b, own_right(e1b, halo, r // tiles)], axis=0
            ),
        )

    def carried(k, r):
        return 0.125 * ao[r] * (1.0 + t3o[1, k * LEV : (k + 1) * LEV, at(r)])

    def adjoint(r):
        t, q = r % tiles, r // tiles
        lanes = slice(t * TILE, (t + 1) * TILE)
        halo = lambda k: 0.125 * ah[t] * (1.0 + t3h[k * LEV : (k + 1) * LEV, lanes])
        parts_here = [carried(k, r) for k in range(4)]
        ad[r - RIM] = (
            ao[r]
            - (parts_here[0] + parts_here[1] + parts_here[2] + parts_here[3])
            + carried(0, r - 1)
            + carried(1, r + 1)
            + own_left(parts_here[2], halo(2), q)
            + own_right(parts_here[3], halo(3), q)
            + vo[r + 1, :LEV]
            + vo[r, LEV : 2 * LEV]
            + vo[r - 1, 2 * LEV :]
        )

    def early(i):
        if i < 3:
            acc2[i] = grad_two(1, i - 1)
        elif i == 3:
            acc1[...] = dot_nt(e1o[1, :, inner], shifted(xo, 1))
        else:
            acc3[...] = dot_nt(e3o[1], h2o[1])

    nothing = jnp.zeros((C, TILE), BF16)
    low, high = RIM, RIM + h
    pipeline(
        [
            (0, low - 1, high + 1, carry_field),
            (2, low, high, adjoint),
            (3, low, high, lambda r: dot_errors(0, r)),
            (4, low, high, lambda r: stack_errors(0, r, nothing)),
            (low, 0, 5, early),
        ],
        low - 1, high + 1,
    )

    g2 = [acc2[a] + grad_two(0, a - 1) for a in range(3)]
    g3 = acc3[...] + dot_nt(e3o[0], h2o[0])
    chunk = grads_ref.shape[1]
    cuts = [(0, 4 * C), (4 * C, 4 * C), (8 * C, TILE), (10 * C, TILE)]

    def spread_rows(i, v):
        lo, n = cuts[i]
        for y in range(n_gy):
            at_row = y * chunk
            inside_rows = at_row + chunk <= C
            grads_ref[y, :, lo : lo + n] = (
                v[at_row : at_row + chunk] if inside_rows else jnp.zeros((chunk, n), F32)
            )

    def to_peers(i, src, dst, send, recv, peers, key):
        span = pl.ds(*cuts[i])
        group = [
            pltpu.make_async_remote_copy(
                src_ref=src(k, p, span), dst_ref=dst(k, p, span),
                send_sem=send.at[i], recv_sem=recv.at[i],
                device_id=key(p), device_id_type=MESH,
            )
            for k, p in enumerate(peers)
        ]
        for copy in group:
            copy.start()

    def settle(i, ref, sem):
        span = pl.ds(*cuts[i])
        pltpu.make_async_copy(ref.at[:, :, span], ref.at[:, :, span], sem.at[i]).wait()

    def scatter(i):
        to_peers(
            i, lambda k, y, n: grads_ref.at[y, :, n], lambda k, y, n: got.at[k, :, n],
            send_one, recv_one, ys, lambda y: (gx, y),
        )

    def cross(i):
        to_peers(
            i, lambda k, x, n: part.at[:, n], lambda k, x, n: parts.at[gx, :, n],
            send_two, recv_two, xs, lambda x: (x, gy),
        )

    def gather(i):
        to_peers(
            i, lambda k, y, n: mine.at[:, n], lambda k, y, n: out_ref.at[gy, :, n],
            send_three, recv_three, ys, lambda y: (gx, y),
        )

    spread_rows(0, jnp.concatenate([g2[0], g2[1][:, :C]], axis=1))
    scatter(0)
    spread_rows(1, jnp.concatenate([g2[1][:, C:], g2[2][:, : 2 * C]], axis=1))
    scatter(1)
    spread_rows(
        2,
        jnp.concatenate(
            [g2[2][:, 2 * C :], jnp.concatenate([g3, jnp.zeros((C - K, C), F32)], axis=0)], axis=1
        ),
    )
    scatter(2)

    for r in (RIM - 2, RIM - 1, RIM + h, RIM + h + 1):
        eo[0, :, at(r)] = jnp.zeros((3 * C, width), BF16)
    g1 = {0: acc1[...]}

    def edges(t):
        owns = [
            eo[0, C : 2 * C, at(t + tiles * q)] if RIM <= t + tiles * q < RIM + h else None
            for q in range(SLOTS)
        ]
        eh[0, :, tile(t)] = jnp.concatenate([edge_left(owns), nothing, edge_right(owns)], axis=0)

    def edge_one(i):
        t, n = pieces[i]
        e1 = dot(w2t, stack_halo(eh, 0, t, n)) * p1h[0, :, t * TILE : (t + n) * TILE]
        sums[1] = sums[1] + fold(e1)
        g1[0] = g1[0] + dot_nt(e1.astype(BF16), stack_halo(xh, 0, t, n))

    closing = [functools.partial(edges, t) for t in range(tiles)]
    closing += [lambda: twist(eh, 0)] + [functools.partial(edge_one, i) for i in range(count)]
    pipeline(
        [
            (0, low - 1, high + 1, lambda r: dot_back(0, r)),
            (1, low - 1, high + 1, lambda r: keep_one(0, r)),
            (low - 1, 0, len(closing), lambda i: closing[i]()),
        ],
        low - 1, high + 1,
    )
    ring = h + 2
    g1 = g1[0] + dot_nt(
        e1o[0, :, (RIM - 1) * width : (RIM + h + 1) * width],
        jnp.concatenate(
            [xo[0, :, (RIM - 1 + a) * width : (RIM - 1 + a + ring) * width] for a in (-1, 0, 1)], axis=0
        ),
    )
    total = lambda v: jnp.sum(v, axis=1, keepdims=True)
    tall = lambda v: jnp.concatenate([v, jnp.zeros((C - v.shape[0], 1), F32)], axis=0)
    extra = pad16(
        jnp.concatenate([g1, total(sums[1]), total(sums[2]), tall(total(sums[3]))], axis=1), TILE
    )
    spread_rows(3, extra)
    scatter(3)
    others_x = parts.at[pl.ds(0, n_gx - 1)]
    others_y = out_ref.at[pl.ds(0, n_gy - 1)]
    for i, (lo, n) in enumerate(cuts):
        span = slice(lo, lo + n)
        settle(i, got, recv_one)
        acc = grads_ref[gy, :, span]
        for k in range(n_gy - 1):
            acc = acc + got[k, :, span]
        part[:, span] = acc
        cross(i)
        parts[gx, :, span] = acc
    for dx, dy, group in copies:
        @pl.when(exists(dx, dy))
        def _():
            for copy in group:
                copy.wait_send()
    for i in range(len(cuts)):
        settle(i, got, send_one)
    for i, (lo, n) in enumerate(cuts):
        span = slice(lo, lo + n)
        settle(i, others_x, recv_two)
        acc = parts[0, :, span]
        for x in range(1, n_gx):
            acc = acc + parts[x, :, span]
        acc = acc.astype(BF16)
        mine[:, span] = acc
        gather(i)
        out_ref[gy, :, span] = acc
    for i in range(len(cuts)):
        settle(i, others_x, send_two)
    for i in range(len(cuts)):
        settle(i, others_y, recv_three)
    for i in range(len(cuts)):
        settle(i, others_y, send_three)


def finish_kernel(grads, final, d1, d2, d3, ids, final_out, u1, u2, u3):
    final_out[...] = final[...]
    n_parts = C // grads.shape[1]
    big = jnp.concatenate([grads[y].astype(F32) for y in range(n_parts)], axis=0)
    side = big[:, 10 * C :]
    one = jnp.concatenate(
        [side[:, 4 * LEV * a : 4 * LEV * a + 3 * LEV] for a in range(3)]
        + [side[:, 12 * LEV : 12 * LEV + 1]],
        axis=1,
    )
    two = jnp.concatenate([big[:, : 9 * C], side[:, 12 * LEV + 1 : 12 * LEV + 2]], axis=1)
    three = jnp.concatenate(
        [big[:K, 9 * C : 10 * C], side[:K, 12 * LEV + 2 : 12 * LEV + 3]], axis=1
    )
    members = [one, two, three]
    heads = [d1[...], d2[...], d3[...]]
    row_sq = lambda v: jnp.sum(v * v, axis=1, keepdims=True)
    grad_rows = jnp.concatenate([row_sq(m) for m in members], axis=0)
    dir_rows = jnp.concatenate([row_sq(m) for m in heads], axis=0)
    total = jnp.sum(grad_rows, axis=0, keepdims=True)
    factor = 1.0 / jnp.maximum(jnp.sqrt(total), 1.0)
    clip_rows = grad_rows * (factor * factor)
    count = grad_rows.shape[0]
    i0 = lax.broadcasted_iota(jnp.int32, (count, count), 0)
    i1 = lax.broadcasted_iota(jnp.int32, (count, count), 1)
    spread = jnp.broadcast_to(ids[...].astype(F32), (count, count))
    column = jnp.sum(jnp.where(i0 == i1, spread, 0.0), axis=1, keepdims=True)
    row_ratio = jnp.zeros((count, 1), F32)
    for k in range(GROUPS):
        hit = column == float(k)
        pick = lambda v: jnp.sum(jnp.where(hit, v, 0.0), axis=0, keepdims=True)
        ratio = jnp.sqrt(pick(clip_rows)) / jnp.sqrt(pick(dir_rows) + 1e-06)
        row_ratio = row_ratio + jnp.where(hit, ratio, 0.0)
    scaling = math.sqrt(PARAMS)
    start = 0
    for ref, member, head in zip((u1, u2, u3), members, heads):
        n = member.shape[0]
        ref[...] = scaling * (member * factor + row_ratio[start : start + n] * head)
        start += n


def per_device(sizes, field, target, mask, conv_one, conv_two, head, d1, d2, d3, ids):
    n_gx, n_gy = sizes
    _, h, width = field.shape
    rows = h + 2 * RIM
    tiles = rows // SLOTS
    flat = rows * width
    edge = (tiles + 2) * TILE
    shape = jax.ShapeDtypeStruct
    chunk = 8 * -(-C // (8 * n_gy))
    wide = 10 * C + TILE
    dma = pltpu.SemaphoreType.DMA
    vmem = pltpu.VMEM
    over_y = [dma((4,))] * 2
    over_x = [dma((4,))] * 2

    def sums(columns):
        return [
            vmem((n_gy, chunk, columns), F32),
            vmem((n_gy - 1, chunk, columns), F32),
            vmem((chunk, columns), F32),
            vmem((n_gx, chunk, columns), F32),
            vmem((chunk, columns), BF16),
        ]

    final, summed = pl.pallas_call(
        functools.partial(fused_kernel, sizes),
        name="fused",
        out_shape=[
            shape(field.shape, F32),
            shape((n_gy, chunk, wide), BF16),
        ],
        in_specs=[ANY] * 6,
        out_specs=[VM] * 2,
        scratch_shapes=[
            vmem((3, rows, LEV, width), F32),
            vmem((3, LEV, edge), F32),
            vmem((2, rows, LEV, width), F32),
            vmem((2, rows, LEV, width), F32),
            vmem((2, tiles, LEV, TILE), F32),
            vmem((2, tiles, LEV, TILE), F32),
            vmem((rows, LEV, width), F32),
            vmem((tiles, LEV, TILE), F32),
            vmem((rows, LEV, width), F32),
            vmem((tiles, LEV, TILE), F32),
            vmem((rows, LEV, width), F32),
            vmem((tiles, LEV, TILE), F32),
            vmem((h, LEV, width), F32),
            vmem((2, 4 * LEV, flat), BF16),
            vmem((2, 4 * LEV, edge), BF16),
            vmem((2, 3 * C, flat), BF16),
            vmem((2, 3 * C, edge), BF16),
            vmem((2, C, flat), F32),
            vmem((2, C, tiles * TILE), F32),
            vmem((2, C, flat), F32),
            vmem((C, tiles * TILE), F32),
            vmem((2, K, flat), F32),
            vmem((K, tiles * TILE), F32),
            vmem((2, C, h * width), BF16),
            vmem((2, 3 * C, flat), BF16),
            vmem((2, 3 * C, edge), BF16),
            vmem((2, K, h * width), BF16),
            vmem((2, C, flat), BF16),
            vmem((C, tiles * TILE), BF16),
            vmem((rows, 3 * LEV, width), F32),
            vmem((3, C, 3 * C), F32),
            vmem((C, 12 * LEV), F32),
            vmem((K, C), F32),
            vmem(field.shape, F32),
            vmem(target.shape, F32),
            vmem(mask.shape, jnp.int32),
            vmem(conv_one.shape, F32),
            vmem(conv_two.shape, F32),
            vmem(head.shape, F32),
            vmem((3, h, width), F32),
            vmem((3, LEV, TILE), F32),
            vmem((3, LEV, TILE), F32),
            vmem((3, 2 * LEV, TILE), F32),
            vmem((3, 2 * LEV, TILE), F32),
            vmem((2, LEV, TILE), F32),
            vmem((2, 2 * LEV, TILE), F32),
        ]
        + sums(wide)
        + [dma((6,)), dma((18,)), dma((18,))]
        + over_y + over_x + over_y,
        compiler_params=pltpu.CompilerParams(
            collective_id=0, has_side_effects=True, vmem_limit_bytes=LIMIT
        ),
    )(field, target, mask, conv_one, conv_two, head)
    final, u1, u2, u3 = pl.pallas_call(
        finish_kernel,
        name="update",
        out_shape=[
            shape(field.shape, F32),
            shape(conv_one.shape, F32), shape(conv_two.shape, F32), shape(head.shape, F32),
        ],
        in_specs=[VM] * 6,
        out_specs=[VM] * 4,
        compiler_params=pltpu.CompilerParams(vmem_limit_bytes=SMALL),
    )(summed, final, d1, d2, d3, ids.reshape(1, -1))
    return final, u1, u2, u3


def solution(mesh):
    grid = P(None, "gx", "gy")
    placed = (grid, grid, P("gx", "gy")) + (P(),) * 7
    return jax.shard_map(
        functools.partial(per_device, (mesh.shape["gx"], mesh.shape["gy"])),
        mesh=mesh,
        in_specs=placed,
        out_specs=(grid, P(), P(), P()),
        check_vma=False,
    )
```
